512 devices in a mesh: req: 64 (over z, x, core), tp: 8 (over y).
Axes of the slice: x: 4, y: 8, z: 8, core: 2. Of those that a mesh axis runs over, the one named last changes fastest.
Arguments:
- queries: bfloat16 [1024, 2560], P('req', 'tp'), may hold values from -64 to 64
- fresh_kv: bfloat16 [1024, 1280], P('req', 'tp'), may hold values from -9 to 9
- kv_cache: bfloat16 [8, 160, 655360], P('tp', None, 'req'), may hold values from -6 to 6
- out_weight: bfloat16 [2560, 2560], P('tp'), may hold values from -1.1953125 to 1.1953125
- offsets: int32 [1024], replicated, may hold values from 0 to 655358, as said below
- lengths: int32 [1024], replicated, may hold values from 2 to 8192, as said below
Outputs:
- mixed_out: bfloat16 [1024, 2560], P('req', 'tp')
The draws below stay inside these ranges and needn't reach their ends.
Inputs may be any that keep to these rules, and one draw needn't show every extreme that they name: Request r belongs to index floor(r / 16) of req and its cache to index floor(offsets[r] / 10240), where it lies whole: offsets[r] + lengths[r] <= (floor(offsets[r] / 10240) + 1) * 10240; caches never intersect. The first 8 requests of each index have their caches on that index; every index holds the caches of exactly 8 requests of other indices, and those of one index's other requests lie on distinct indices. `lengths`: on every index of req one held cache has exactly 8192 tokens.
All inputs are finite; a program needn't handle non-finite values.
Results may differ from the reference program's by a relative error of at most 0.019.
Values may be sent and summed in bfloat16 or wider, within the bound.
No kernel may reach another device: no remote copies, remote signals or barrier semaphores. Data moves between devices by JAX's collectives and lax.ppermute only.
A program may use at most 64 MiB of HBM per device.

```python
import jax
import jax.numpy as jnp
from jax import lax

D = 2560
HQ = 32
KVH = 8
HD = 80
W = 4096
LMAX = 8192
CACHE_DEV = 10240
R_DEV = 16
G = 4
REQ = 1024


def layout(key):
    devices = REQ // R_DEV
    half_rows = R_DEV // 2
    subkeys = jax.random.split(jax.random.fold_in(key, 7), 4)
    placing = jax.random.permutation(subkeys[0], devices).astype(jnp.int32)
    shifts = (jax.random.permutation(subkeys[1], devices - 1)[:half_rows] + 1).astype(jnp.int32)
    position = jnp.arange(devices, dtype=jnp.int32)
    far_owner = placing[(position[:, None] + shifts[None, :]) % devices]
    far_owner = jnp.zeros((devices, half_rows), jnp.int32).at[placing].set(far_owner)
    home_owner = jnp.broadcast_to(position[:, None], (devices, half_rows))
    owner_table = jnp.concatenate([home_owner, far_owner], 1)
    flat_far = far_owner.reshape(-1)
    onehot = (flat_far[:, None] == position[None, :]).astype(jnp.int32)
    rank_list = jnp.sum(jnp.cumsum(onehot, 0) * onehot, 1) - 1
    home_slots = jnp.broadcast_to(jnp.arange(half_rows, dtype=jnp.int32)[None, :], (devices, half_rows))
    slot_index = jnp.concatenate([home_slots, half_rows + rank_list.reshape(devices, half_rows)], 1)
    short_most = (CACHE_DEV - LMAX) // (R_DEV - 1)
    length_table = jax.random.randint(subkeys[2], (devices, R_DEV), 2, short_most + 1).astype(jnp.int32)
    long_slot = jax.random.randint(subkeys[3], (devices,), 0, R_DEV).astype(jnp.int32)
    length_table = jnp.where(jnp.arange(R_DEV, dtype=jnp.int32)[None, :] == long_slot[:, None], LMAX, length_table)
    start_table = jnp.cumsum(length_table, 1) - length_table + position[:, None] * CACHE_DEV
    owner_flat = owner_table.reshape(-1)
    slot_flat = slot_index.reshape(-1)
    return (start_table[owner_flat, slot_flat].astype(jnp.int32), length_table[owner_flat, slot_flat].astype(jnp.int32))


def draw_offsets(key, part):
    return layout(key)[0]


def draw_lengths(key, part):
    return layout(key)[1]


def draw_queries(key, part):
    ground_key = jax.random.fold_in(key, 11)
    drawn = jnp.clip(jax.random.normal(ground_key, (REQ, HQ * HD), jnp.float32), -6.0, 6.0)
    return drawn.astype(jnp.bfloat16)


def draw_kv_cache(key, part):
    ground_key = jax.random.fold_in(key, 17)
    full_shape = (KVH, 2 * HD, CACHE_DEV * (REQ // R_DEV))
    drawn = jnp.clip(jax.random.normal(ground_key, full_shape, jnp.float32), -6.0, 6.0)
    return drawn.astype(jnp.bfloat16)


def block_scale(rng, extent, cuts, smallest, largest):
    factor_of = 1.0
    for axis_at, shards_of in cuts:
        draws = jax.random.uniform(jax.random.fold_in(jax.random.fold_in(rng, 6), axis_at), (shards_of,), jnp.float32, smallest / len(cuts), largest / len(cuts))
        factor_of = factor_of * jnp.repeat(jnp.exp(draws), extent[axis_at] // shards_of).reshape((-1,) + (1,) * (len(extent) - 1 - axis_at))
    return factor_of


def bell_draw(stream_key, dims, scale, bound, cuts=(), held_as=jnp.bfloat16):
    values = jax.random.normal(stream_key, dims, jnp.float32) * scale
    if len(cuts) > 0:
        values = block_scale(stream_key, dims, cuts, -0.22, 0.18) * values
    return jnp.clip(values, min=-bound, max=bound).astype(held_as)


def setup_inputs(seed: int = 0) -> dict:
    key_of = jax.random.split(jax.random.key(seed), 7)
    return {
        "queries": draw_queries(jax.random.fold_in(key_of[6], 71), 0),
        "fresh_kv": bell_draw(key_of[1], (REQ, KVH * 2 * HD), 1.5, 9.0, ((0, 64), (1, 8))),
        "kv_cache": draw_kv_cache(jax.random.fold_in(key_of[6], 71), 0),
        "out_weight": bell_draw(key_of[3], (HQ * HD, D), 0.2, 1.1953125, ((0, 8),)),
        "offsets": draw_offsets(jax.random.fold_in(key_of[6], 71), 0),
        "lengths": draw_lengths(jax.random.fold_in(key_of[6], 71), 0),
    }


def one_request(kv_cache, query_row, fresh_row, request_offset, request_length):
    span = W - 1
    whole_tokens = kv_cache.shape[2]
    window_end = request_offset + request_length
    first_token = jnp.clip(window_end - span, 0, whole_tokens - span).astype(jnp.int32)
    window_block = lax.dynamic_slice_in_dim(kv_cache, first_token, span, 2).astype(jnp.float32)
    positions = first_token + jnp.arange(span, dtype=jnp.int32)
    inside = (positions >= request_offset) & (positions < window_end) & (positions >= window_end - span)
    grouped = query_row.astype(jnp.float32).reshape(KVH, G, HD)
    fresh_split = fresh_row.astype(jnp.float32).reshape(KVH, 2, HD)
    score_scale = HD ** -0.5
    scores = jnp.einsum("hgd,hdt->hgt", grouped, window_block[:, :HD, :]) * score_scale
    scores = jnp.where(inside[None, None, :], scores, -jnp.inf)
    own_score = jnp.einsum("hgd,hd->hg", grouped, fresh_split[:, 0, :]) * score_scale
    highest = jnp.maximum(jnp.max(scores, axis=2), own_score)
    weights = jnp.exp(scores - highest[:, :, None])
    own_weight = jnp.exp(own_score - highest)
    totals = jnp.sum(weights, axis=2) + own_weight
    rounded = lax.optimization_barrier(weights.astype(jnp.bfloat16)).astype(jnp.float32)
    own_rounded = lax.optimization_barrier(own_weight.astype(jnp.bfloat16)).astype(jnp.float32)
    summed = jnp.einsum("hgt,hdt->hgd", rounded, window_block[:, HD:, :])
    summed = summed + own_rounded[:, :, None] * fresh_split[:, None, 1, :]
    return (summed / totals[:, :, None]).astype(jnp.bfloat16).reshape(KVH * G * HD)


def reference(queries, fresh_kv, kv_cache, out_weight, offsets, lengths):
    def per_request(items):
        return one_request(kv_cache, items[0], items[1], items[2], items[3])

    attended = lax.map(per_request, (queries, fresh_kv, offsets, lengths))
    return jnp.dot(attended, out_weight, preferred_element_type=jnp.float32).astype(jnp.bfloat16)
```

```python
import jax
import jax.numpy as jnp
from jax import lax
from jax.sharding import PartitionSpec as P

HD = 80
W = 4096
MESSAGE = 512


def attend(queries, fresh_kv, cache_block, starts, lengths):
    row_count = queries.shape[0]
    kv_heads = cache_block.shape[0]
    tokens = cache_block.shape[2]
    score_scale = HD ** (-0.5)
    grouped = queries.reshape(row_count, kv_heads, -1, HD)
    fresh_split = fresh_kv.reshape(row_count, kv_heads, 2, HD)
    scores = (
        jnp.einsum(
            "nhgd,hdt->hngt", grouped, cache_block[:, :HD, :], preferred_element_type=jnp.float32
        )
        * score_scale
    )
    positions = jnp.arange(tokens, dtype=jnp.int32)[None, :]
    window_end = (starts + lengths)[:, None]
    inside = (
        (positions >= starts[:, None])
        & (positions < window_end)
        & (positions >= window_end - (W - 1))
    )
    scores = jnp.where(inside[None, :, None, :], scores, -jnp.inf)
    own_score = (
        jnp.einsum(
            "nhgd,nhd->hng", grouped, fresh_split[:, :, 0, :], preferred_element_type=jnp.float32
        )
        * score_scale
    )
    highest = jnp.maximum(jnp.max(scores, axis=3), own_score)
    weights = jnp.exp(scores - highest[..., None])
    own_weight = jnp.exp(own_score - highest)
    totals = jnp.sum(weights, axis=3) + own_weight
    summed = jnp.einsum(
        "hngt,hdt->nhgd",
        weights.astype(jnp.bfloat16),
        cache_block[:, HD:, :],
        preferred_element_type=jnp.float32,
    )
    summed = summed + jnp.einsum(
        "hng,nhd->nhgd",
        own_weight.astype(jnp.bfloat16),
        fresh_split[:, :, 1, :],
        preferred_element_type=jnp.float32,
    )
    normed = summed / jnp.transpose(totals, (1, 0, 2))[..., None]
    return normed.astype(jnp.bfloat16).reshape(row_count, -1)


def shards(queries, fresh_kv, kv_cache, out_weight, offsets, lengths):
    devices = lax.axis_size("req")
    columns = lax.axis_size("tp")
    device_index = lax.axis_index("req")
    row_count, width = queries.shape
    half_rows = row_count // 2
    shard_tokens = kv_cache.shape[2]
    home_first = device_index * row_count
    my_offsets = lax.dynamic_slice_in_dim(offsets, home_first, row_count)
    my_lengths = lax.dynamic_slice_in_dim(lengths, home_first, row_count)
    my_owners = my_offsets // shard_tokens
    my_starts = my_offsets - my_owners * shard_tokens
    slot = jnp.arange(devices, dtype=jnp.int32)
    placed = (slot[:, None] == my_owners[None, half_rows:]).astype(jnp.bfloat16)
    digits = jnp.stack(
        [
            jnp.ones_like(my_starts),
            my_starts >> 7,
            my_starts & 127,
            my_lengths >> 7,
            my_lengths & 127,
        ],
        axis=1,
    )
    digits = jnp.pad(digits, ((0, 0), (0, MESSAGE - 3 * width // 2 - 5)))
    message = jnp.concatenate([queries, fresh_kv, digits.astype(jnp.bfloat16)], axis=1)
    sent = jnp.dot(placed, message[half_rows:], preferred_element_type=jnp.float32)
    got = lax.all_to_all(sent.astype(jnp.bfloat16), "req", 0, 0, tiled=True)
    valid = got[:, 3 * width // 2] > 0.5
    rank = jnp.sum((slot[None, :] < slot[:, None]) & valid[None, :], axis=1)
    chosen = (
        (rank[:, None] == jnp.arange(half_rows)[None, :]) & valid[:, None]
    ).astype(jnp.bfloat16)
    held = lax.dot_general(
        chosen, got, (((0,), (0,)), ((), ())), preferred_element_type=jnp.float32
    )
    held_digits = held[:, 3 * width // 2 :].astype(jnp.int32)
    held_starts = held_digits[:, 1] * 128 + held_digits[:, 2]
    held_lengths = held_digits[:, 3] * 128 + held_digits[:, 4]
    held = held.astype(jnp.bfloat16)
    attended = attend(
        jnp.concatenate([queries[:half_rows], held[:, :width]], axis=0),
        jnp.concatenate([fresh_kv[:half_rows], held[:, width : 3 * width // 2]], axis=0),
        kv_cache,
        jnp.concatenate([my_starts[:half_rows], held_starts]),
        jnp.concatenate([my_lengths[:half_rows], held_lengths]),
    )
    partial_value = jnp.dot(attended, out_weight, preferred_element_type=jnp.float32)
    shares = partial_value.astype(jnp.bfloat16).reshape(row_count, columns, width)
    shares = lax.all_to_all(jnp.transpose(shares, (1, 0, 2)), "tp", 0, 0, tiled=True)
    mixed = jnp.sum(shares.astype(jnp.float32), axis=0).astype(jnp.bfloat16)
    spread = jnp.dot(chosen, mixed[half_rows:], preferred_element_type=jnp.float32)
    returned = lax.all_to_all(spread.astype(jnp.bfloat16), "req", 0, 0, tiled=True)
    far = lax.dot_general(
        placed, returned, (((0,), (0,)), ((), ())), preferred_element_type=jnp.float32
    )
    return jnp.concatenate([mixed[:half_rows], far.astype(jnp.bfloat16)], axis=0)


def solution(mesh):
    in_specs = (P("req", "tp"), P("req", "tp"), P("tp", None, "req"), P("tp", None), P(), P())
    out_specs = P("req", "tp")
    return jax.shard_map(shards, mesh=mesh, in_specs=in_specs, out_specs=out_specs, check_vma=False)
```

```python
import functools

import jax
import jax.numpy as jnp
from jax import lax
from jax.experimental import pallas as pl
from jax.experimental.pallas import tpu as pltpu
from jax.sharding import PartitionSpec as P

HD = 80
G = 4
W = 4096
LMAX = 8192
LANES = 128
BF = jnp.bfloat16
F32 = jnp.float32
I32 = jnp.int32
VMEM = pl.BlockSpec(memory_space=pltpu.VMEM)


def iota(shape, axis):
    return lax.broadcasted_iota(I32, shape, axis)


def dot(a, b):
    return jnp.dot(a, b, preferred_element_type=F32)


def dot_t(a, b):
    return lax.dot_general(a, b, (((1,), (1,)), ((), ())), preferred_element_type=F32)


def own_row(table_ref, index, shift):
    per_row = LANES // 16
    row = table_ref[pl.ds(index // per_row, 1), :]
    back = (index % per_row) * 16 + shift
    return pltpu.roll(row, (LANES - back) % LANES, 1)


def column(row, count):
    wide = jnp.broadcast_to(row, (count, LANES))
    same = iota((count, LANES), 0) == iota((count, LANES), 1)
    return jnp.sum(jnp.where(same, wide, 0), axis=1, keepdims=True)


def slot_matrix(offsets_ref, index, tokens, slots):
    owners = own_row(offsets_ref, index, 8) // tokens
    lane = iota((1, LANES), 1)
    spread = jnp.where(lane < 8, owners, 0)
    spread = spread + jnp.where((lane >= 8) & (lane < 16), pltpu.roll(owners, 8, 1), 0)
    spread = spread + jnp.where((lane >= 16) & (lane < 24), pltpu.roll(owners, 16, 1), 0)
    spread = spread + jnp.where((lane >= 24) & (lane < 32), pltpu.roll(owners, 24, 1), 0)
    row = iota((slots * 4, LANES), 0)
    col = iota((slots * 4, LANES), 1)
    hit = ((row >> 2) == jnp.broadcast_to(spread, (slots * 4, LANES))) & ((row & 3) == (col >> 3))
    return jnp.where(hit, 1.0, 0.0).astype(BF)


def send_kernel(tokens, offsets_ref, lengths_ref, queries_ref, fresh_ref, out_ref):
    index = lax.axis_index("req")
    slots = out_ref.shape[0] // 4
    placed = slot_matrix(offsets_ref, index, tokens, slots)
    starts = column(own_row(offsets_ref, index, 8) % tokens, 8)
    lengths = column(own_row(lengths_ref, index, 8), 8)
    queries = queries_ref[...].astype(F32)[8:]
    fresh = fresh_ref[...].astype(F32)[8:]
    lane = iota((8, LANES), 1)
    meta = jnp.where(lane == 96, 1, 0)
    meta = jnp.where(lane == 97, starts >> 7, meta)
    meta = jnp.where(lane == 98, starts & 127, meta)
    meta = jnp.where(lane == 99, lengths >> 7, meta)
    meta = jnp.where(lane == 100, lengths & 127, meta)
    third = jnp.concatenate(
        [queries[:, 256:], fresh[:, 128:], jnp.zeros((8, 32), F32)], axis=1
    ) + meta.astype(F32)
    stack = jnp.concatenate(
        [queries[:, :128], queries[:, 128:256], third, fresh[:, :128], jnp.zeros((96, LANES), F32)],
        axis=0,
    )
    out_ref[...] = dot(placed, stack.astype(BF)).astype(BF)


def attend_kernel(
    tokens, offsets_ref, lengths_ref, queries_ref, fresh_ref, got_ref, cache_ref, weight_ref, out_ref, chosen_ref
):
    index = lax.axis_index("req")
    rows = got_ref.shape[0]
    scale = HD ** (-0.5)
    got = got_ref[...]
    flag = jnp.where(
        (iota((rows, LANES), 1) == 96) & ((iota((rows, LANES), 0) & 3) == 2), got.astype(F32), 0.0
    )
    flag = jnp.sum(flag, axis=1, keepdims=True)
    flags = jnp.broadcast_to(flag, (rows, LANES)).astype(BF)
    slot_a = iota((rows, rows), 0) >> 2
    slot_b = iota((rows, rows), 1) >> 2
    valid = dot(jnp.where(slot_a == slot_b, 1.0, 0.0).astype(BF), flags)
    rank = dot(jnp.where(slot_b < slot_a, 1.0, 0.0).astype(BF), flags)
    row = iota((rows, LANES), 0)
    col = iota((rows, LANES), 1)
    hit = (valid > 0.5) & (rank.astype(I32) == (col & 7)) & ((row & 3) == (col >> 3))
    chosen = jnp.where(hit, 1.0, 0.0)
    chosen_ref[...] = chosen.astype(BF)
    held = dot(jnp.transpose(chosen).astype(BF), got)
    meta = held[16:24]
    held_starts = (meta[:, 97:98] * 128.0 + meta[:, 98:99]).astype(I32)
    held_lengths = (meta[:, 99:100] * 128.0 + meta[:, 100:101]).astype(I32)
    held_queries = jnp.concatenate([held[0:8], held[8:16], held[16:24, :64]], axis=1)
    held_fresh = jnp.concatenate([held[24:32], held[16:24, 64:96]], axis=1)
    starts = column(own_row(offsets_ref, index, 0), 8) - index * tokens
    lengths = column(own_row(lengths_ref, index, 0), 8)
    starts = jnp.concatenate([starts, held_starts], axis=0)
    lengths = jnp.concatenate([lengths, held_lengths], axis=0)
    queries = jnp.concatenate([queries_ref[...].astype(F32)[:8], held_queries], axis=0)
    fresh = jnp.concatenate([fresh_ref[...].astype(F32)[:8], held_fresh], axis=0)
    fresh_key, fresh_value = fresh[:, :HD], fresh[:, HD : 2 * HD]
    heads = [queries[:, g * HD : (g + 1) * HD] for g in range(G)]
    own = [jnp.sum(h * fresh_key, axis=1, keepdims=True) * scale for h in heads]
    stacked = jnp.concatenate(heads, axis=0).astype(BF)
    own_all = jnp.concatenate(own, axis=0)
    is_long = lengths == LMAX
    long_start = jnp.sum(jnp.where(is_long, starts, 0))
    sub = iota((8, HD), 0)
    long_query = jnp.zeros((8, HD), F32)
    long_own = jnp.zeros((8, 1), F32)
    for g in range(G):
        picked = jnp.sum(jnp.where(is_long, heads[g], 0.0), axis=0, keepdims=True)
        long_query = jnp.where(sub == g, picked, long_query)
        picked_own = jnp.sum(jnp.where(is_long, own[g], 0.0), axis=0, keepdims=True)
        long_own = jnp.where(iota((8, 1), 0) == g, picked_own, long_own)
    long_value = jnp.sum(jnp.where(is_long, fresh_value, 0.0), axis=0, keepdims=True)
    span = W + LANES
    first = long_start + (LMAX - W + 1)
    base = jnp.minimum(first // LANES * LANES, tokens - span)
    window = pl.ds(pl.multiple_of(base, LANES), span)
    scores = dot(long_query.astype(BF), cache_ref[:HD, window]) * scale
    position = base + iota((8, span), 1)
    scores = jnp.where((position >= first) & (position < first + (W - 1)), scores, -jnp.inf)
    highest = jnp.maximum(jnp.max(scores, axis=1, keepdims=True), long_own)
    weights = jnp.exp(scores - highest)
    own_weight = jnp.exp(long_own - highest)
    totals = jnp.sum(weights, axis=1, keepdims=True) + own_weight
    summed = dot_t(weights.astype(BF), cache_ref[HD : 2 * HD, window])
    summed = summed + own_weight.astype(BF).astype(F32) * long_value
    long_out = summed / totals
    blocks = (tokens - LMAX) // LANES + 1
    before = (long_start + LANES - 1) // LANES
    after = (long_start + LMAX) // LANES
    last = tokens // LANES - 1
    keys, values, places = [], [], []
    for i in range(blocks):
        block = jnp.where(i < before, i, after + i - before)
        spare = block > last
        begin = pl.multiple_of(jnp.minimum(block, last) * LANES, LANES)
        keys.append(cache_ref[:HD, pl.ds(begin, LANES)])
        values.append(cache_ref[HD : 2 * HD, pl.ds(begin, LANES)])
        places.append(jnp.where(spare, -LANES, begin) + iota((1, LANES), 1))
    keys = jnp.concatenate(keys, axis=1)
    values = jnp.concatenate(values, axis=1)
    position = jnp.concatenate(places, axis=1)
    ends = starts + lengths
    firsts = jnp.maximum(starts, ends - (W - 1))
    ends = jnp.concatenate([ends] * G, axis=0)
    firsts = jnp.concatenate([firsts] * G, axis=0)
    scores = dot(stacked, keys) * scale
    scores = jnp.where((position >= firsts) & (position < ends), scores, -jnp.inf)
    highest = jnp.maximum(jnp.max(scores, axis=1, keepdims=True), own_all)
    weights = jnp.exp(scores - highest)
    own_weight = jnp.exp(own_all - highest)
    totals = jnp.sum(weights, axis=1, keepdims=True) + own_weight
    summed = dot_t(weights.astype(BF), values)
    summed = summed + own_weight.astype(BF).astype(F32) * jnp.concatenate([fresh_value] * G, axis=0)
    outs = summed / totals
    count = starts.shape[0]
    attended = [
        jnp.where(is_long, long_out[g : g + 1], outs[g * count : (g + 1) * count]) for g in range(G)
    ]
    attended = jnp.concatenate(attended, axis=1).astype(BF)
    width = G * HD
    for j in range(out_ref.shape[0]):
        left = j * width // LANES * LANES
        out_ref[j] = dot(attended, weight_ref[:, left : left + out_ref.shape[2]]).astype(BF)


def spread_kernel(shares_ref, chosen_ref, home_ref, out_ref):
    odd = (lax.axis_index("tp") % 2) == 1
    total = jnp.sum(shares_ref[...].astype(F32), axis=0)
    moved = jnp.concatenate([total[:, 64:], total[:, :64]], axis=1)
    mixed = jnp.where(odd, moved, total).astype(BF).astype(F32)
    home_ref[...] = mixed[:8, : home_ref.shape[1]].astype(BF)
    far = mixed[8:]
    stack = jnp.concatenate(
        [far[:, :128], far[:, 128:256], far[:, 256:], jnp.zeros((104, LANES), F32)], axis=0
    )
    out_ref[...] = dot(chosen_ref[...], stack.astype(BF)).astype(BF)


def pick_kernel(tokens, offsets_ref, home_ref, returned_ref, out_ref):
    index = lax.axis_index("req")
    placed = slot_matrix(offsets_ref, index, tokens, returned_ref.shape[0] // 4)
    far = dot(jnp.transpose(placed.astype(F32)).astype(BF), returned_ref[...])
    far = jnp.concatenate([far[0:8], far[8:16], far[16:24, :64]], axis=1)
    out_ref[...] = jnp.concatenate([home_ref[...].astype(F32), far], axis=0).astype(BF)


def call(kernel, out_shape, *args):
    return pl.pallas_call(
        kernel,
        out_shape=out_shape,
        in_specs=[VMEM] * len(args),
        out_specs=jax.tree.map(lambda _: VMEM, out_shape),
    )(*args)


def shards(queries, fresh_kv, kv_cache, out_weight, offsets, lengths):
    devices = lax.axis_size("req")
    columns = lax.axis_size("tp")
    row_count, width = queries.shape
    tokens = kv_cache.shape[2]
    cache = kv_cache.reshape(kv_cache.shape[1:])
    offsets = offsets.reshape(-1, LANES)
    lengths = lengths.reshape(-1, LANES)
    shape = jax.ShapeDtypeStruct
    slots = shape((devices * 4, LANES), BF)
    message = call(
        functools.partial(send_kernel, tokens), slots, offsets, lengths, queries, fresh_kv
    )
    got = lax.all_to_all(message.reshape(devices, 4, LANES), "req", 0, 0, tiled=True)
    shares, chosen = call(
        functools.partial(attend_kernel, tokens),
        (shape((columns, row_count, 384), BF), slots),
        offsets, lengths, queries, fresh_kv, got.reshape(devices * 4, LANES), cache, out_weight,
    )
    shares = lax.all_to_all(shares, "tp", 0, 0, tiled=True)
    home, spread = call(
        spread_kernel, (shape((row_count // 2, width), BF), slots), shares, chosen
    )
    returned = lax.all_to_all(spread.reshape(devices, 4, LANES), "req", 0, 0, tiled=True)
    return call(
        functools.partial(pick_kernel, tokens),
        shape((row_count, width), BF),
        offsets, home, returned.reshape(devices * 4, LANES),
    )


def solution(mesh):
    in_specs = (P("req", "tp"), P("req", "tp"), P("tp", None, "req"), P("tp", None), P(), P())
    out_specs = P("req", "tp")
    return jax.shard_map(shards, mesh=mesh, in_specs=in_specs, out_specs=out_specs, check_vma=False)
```

```python
import functools

import jax
import jax.numpy as jnp
from jax import lax
from jax.experimental import pallas as pl
from jax.experimental.pallas import tpu as pltpu
from jax.sharding import PartitionSpec as P

HD = 80
G = 4
W = 4096
LMAX = 8192
LANES = 128
HALF = 8
BF = jnp.bfloat16
F32 = jnp.float32
I32 = jnp.int32
NEAR = pl.BlockSpec(memory_space=pltpu.VMEM)
ANYWHERE = pl.BlockSpec(memory_space=pltpu.HBM)


def iota(shape, axis):
    return lax.broadcasted_iota(I32, shape, axis)


def dot(a, b):
    return jnp.dot(a, b, preferred_element_type=F32)


def dot_t(a, b):
    return lax.dot_general(a, b, (((1,), (1,)), ((), ())), preferred_element_type=F32)


def own_row(table_ref, index, shift):
    per_row = LANES // 16
    row = table_ref[pl.ds(index // per_row, 1), :]
    back = (index % per_row) * 16 + shift
    return pltpu.roll(row, (LANES - back) % LANES, 1)


def column(row, count):
    wide = jnp.broadcast_to(row, (count, LANES))
    same = iota((count, LANES), 0) == iota((count, LANES), 1)
    return jnp.sum(jnp.where(same, wide, 0), axis=1, keepdims=True)


def pack(queries, fresh, starts, lengths):
    lane = iota((HALF, LANES), 1)
    meta = jnp.where(lane == 96, 1, 0)
    meta = jnp.where(lane == 97, starts >> 7, meta)
    meta = jnp.where(lane == 98, starts & 127, meta)
    meta = jnp.where(lane == 99, lengths >> 7, meta)
    meta = jnp.where(lane == 100, lengths & 127, meta)
    third = jnp.concatenate([queries[:, 256:], fresh[:, 128:], jnp.zeros((HALF, 32), F32)], axis=1)
    return jnp.concatenate(
        [queries[:, :128], queries[:, 128:256], third + meta.astype(F32), fresh[:, :128]], axis=0
    )


def unpack(stack):
    meta = stack[16:24]
    starts = (meta[:, 97:98] * 128.0 + meta[:, 98:99]).astype(I32)
    lengths = (meta[:, 99:100] * 128.0 + meta[:, 100:101]).astype(I32)
    queries = jnp.concatenate([stack[0:8], stack[8:16], stack[16:24, :64]], axis=1)
    fresh = jnp.concatenate([stack[24:32], stack[16:24, 64:96]], axis=1)
    return queries, fresh[:, :HD], fresh[:, HD:], starts, lengths


def fetch(sources, targets, sems):
    copies = [
        pltpu.make_async_copy(s, t, sems.at[i]) for i, (s, t) in enumerate(zip(sources, targets))
    ]
    for copy in copies:
        copy.start()
    return copies


def send_kernel(
    tokens, offsets_hbm, lengths_hbm, queries_hbm, fresh_hbm, out_ref, placed_ref, mine_ref,
    offsets_ref, lengths_ref, queries_ref, fresh_ref, sems,
):
    sources = (offsets_hbm, lengths_hbm, queries_hbm, fresh_hbm)
    for copy in fetch(sources, (offsets_ref, lengths_ref, queries_ref, fresh_ref), sems):
        copy.wait()
    index = lax.axis_index("req")
    rows = out_ref.shape[0]
    offsets = own_row(offsets_ref, index, 0)
    owners = offsets // tokens
    starts = column(offsets - owners * tokens, 16)
    lengths = column(own_row(lengths_ref, index, 0), 16)
    far = pltpu.roll(owners, LANES - HALF, 1)
    lane = iota((1, LANES), 1)
    spread = jnp.where(lane < 8, far, 0)
    for k in (1, 2, 3):
        here = (lane >= 8 * k) & (lane < 8 * k + 8)
        spread = spread + jnp.where(here, pltpu.roll(far, 8 * k, 1), 0)
    row = iota((rows, LANES), 0)
    col = iota((rows, LANES), 1)
    hit = ((row >> 2) == jnp.broadcast_to(spread, (rows, LANES))) & ((row & 3) == (col >> 3))
    placed = jnp.where(hit, 1.0, 0.0).astype(BF)
    placed_ref[...] = placed
    queries = queries_ref[...].astype(F32)
    fresh = fresh_ref[...].astype(F32)
    mine_ref[...] = pack(queries[:8], fresh[:8], starts[:8], lengths[:8])
    stack = pack(queries[8:], fresh[8:], starts[8:], lengths[8:])
    stack = jnp.concatenate([stack, jnp.zeros((96, LANES), F32)], axis=0)
    out_ref[...] = dot(placed, stack.astype(BF)).astype(BF)


def attend(stack, long_start, cache_ref, long_ref):
    tokens = cache_ref.shape[1]
    scale = HD ** (-0.5)
    queries, fresh_key, fresh_value, starts, lengths = unpack(stack)
    heads = [queries[:, g * HD : (g + 1) * HD] for g in range(G)]
    own = [jnp.sum(h * fresh_key, axis=1, keepdims=True) * scale for h in heads]
    is_long = lengths == LMAX

    @pl.when(jnp.max(lengths) == LMAX)
    def _():
        sub = iota((8, HD), 0)
        long_query = jnp.zeros((8, HD), F32)
        long_own = jnp.zeros((8, 1), F32)
        for g in range(G):
            picked = jnp.sum(jnp.where(is_long, heads[g], 0.0), axis=0, keepdims=True)
            long_query = jnp.where(sub == g, picked, long_query)
            picked_own = jnp.sum(jnp.where(is_long, own[g], 0.0), axis=0, keepdims=True)
            long_own = jnp.where(iota((8, 1), 0) == g, picked_own, long_own)
        long_value = jnp.sum(jnp.where(is_long, fresh_value, 0.0), axis=0, keepdims=True)
        span = W + LANES
        first = long_start + (LMAX - W + 1)
        base = jnp.minimum(first // LANES * LANES, tokens - span)
        window = pl.ds(pl.multiple_of(base, LANES), span)
        scores = dot(long_query.astype(BF), cache_ref[:HD, window]) * scale
        position = base + iota((8, span), 1)
        scores = jnp.where((position >= first) & (position < first + (W - 1)), scores, -jnp.inf)
        highest = jnp.maximum(jnp.max(scores, axis=1, keepdims=True), long_own)
        weights = jnp.exp(scores - highest)
        own_weight = jnp.exp(long_own - highest)
        totals = jnp.sum(weights, axis=1, keepdims=True) + own_weight
        summed = dot_t(weights.astype(BF), cache_ref[HD : 2 * HD, window])
        summed = summed + own_weight.astype(BF).astype(F32) * long_value
        long_ref[...] = summed / totals

    blocks = (tokens - LMAX) // LANES + 1
    before = (long_start + LANES - 1) // LANES
    after = (long_start + LMAX) // LANES
    last = tokens // LANES - 1
    keys, values, places = [], [], []
    for i in range(blocks):
        block = jnp.where(i < before, i, after + i - before)
        spare = block > last
        begin = pl.multiple_of(jnp.minimum(block, last) * LANES, LANES)
        keys.append(cache_ref[:HD, pl.ds(begin, LANES)])
        values.append(cache_ref[HD : 2 * HD, pl.ds(begin, LANES)])
        places.append(jnp.where(spare, -LANES, begin) + iota((1, LANES), 1))
    keys = jnp.concatenate(keys, axis=1)
    values = jnp.concatenate(values, axis=1)
    position = jnp.concatenate(places, axis=1)
    ends = starts + lengths
    firsts = jnp.maximum(starts, ends - (W - 1))
    ends = jnp.concatenate([ends] * G, axis=0)
    firsts = jnp.concatenate([firsts] * G, axis=0)
    own_all = jnp.concatenate(own, axis=0)
    scores = dot(jnp.concatenate(heads, axis=0).astype(BF), keys) * scale
    scores = jnp.where((position >= firsts) & (position < ends), scores, -jnp.inf)
    highest = jnp.maximum(jnp.max(scores, axis=1, keepdims=True), own_all)
    weights = jnp.exp(scores - highest)
    own_weight = jnp.exp(own_all - highest)
    totals = jnp.sum(weights, axis=1, keepdims=True) + own_weight
    summed = dot_t(weights.astype(BF), values)
    summed = summed + own_weight.astype(BF).astype(F32) * jnp.concatenate([fresh_value] * G, axis=0)
    outs = summed / totals
    long_out = long_ref[...]
    return jnp.concatenate(
        [jnp.where(is_long, long_out[g : g + 1], outs[g * 8 : g * 8 + 8]) for g in range(G)], axis=1
    )


def home_kernel(
    mine_ref, offsets_hbm, lengths_hbm, cache_hbm,
    cache_ref, home_ref, chosen_ref, long_start_ref, offsets_ref, lengths_ref, long_ref, sems,
):
    index = lax.axis_index("req")
    tokens = cache_ref.shape[1]
    sources = (offsets_hbm, lengths_hbm, cache_hbm)
    copies = fetch(sources, (offsets_ref, lengths_ref, cache_ref), sems)
    copies[0].wait()
    copies[1].wait()
    offsets = offsets_ref[...]
    held = (offsets // tokens) == index
    long_start = jnp.sum(jnp.where(held & (lengths_ref[...] == LMAX), offsets, 0)) - index * tokens
    long_start_ref[...] = jnp.full((8, LANES), long_start, I32)
    rows = chosen_ref.shape[0]
    lane = iota((8, LANES), 1)
    flags = jnp.where(held & ((lane & 15) >= HALF), 1.0, 0.0).astype(BF)
    line = iota((rows, 8), 0) >> 5
    here = dot(jnp.where(line == iota((rows, 8), 1), 1.0, 0.0).astype(BF), flags)
    earlier = dot(jnp.where(line > iota((rows, 8), 1), 1.0, 0.0).astype(BF), flags)
    row = iota((rows, LANES), 0)
    col = iota((rows, LANES), 1)
    slot = (row >> 2) & 7
    valid = jnp.sum(jnp.where((col >> 4) == slot, here, 0.0), axis=1, keepdims=True)
    rank = jnp.sum(earlier + jnp.where((col >> 4) < slot, here, 0.0), axis=1, keepdims=True)
    hit = (valid > 0.5) & (rank.astype(I32) == (col & 7)) & ((row & 3) == (col >> 3))
    chosen_ref[...] = jnp.where(hit, 1.0, 0.0).astype(BF)
    long_ref[...] = jnp.zeros_like(long_ref)
    copies[2].wait()
    home_ref[...] = attend(mine_ref[...], long_start, cache_ref, long_ref)


def far_kernel(
    got_ref, chosen_ref, long_start_ref, home_ref, cache_ref, weight_hbm, out_ref,
    weight_ref, long_ref, sems,
):
    (copy,) = fetch((weight_hbm,), (weight_ref,), sems)
    long_ref[...] = jnp.zeros_like(long_ref)
    held = dot(jnp.transpose(chosen_ref[...].astype(F32)).astype(BF), got_ref[...])
    far = attend(held[:32], jnp.max(long_start_ref[0:1, :]), cache_ref, long_ref)
    attended = jnp.concatenate([home_ref[...], far], axis=0).astype(BF)
    copy.wait()
    width = G * HD
    for j in range(out_ref.shape[0]):
        left = j * width // LANES * LANES
        out_ref[j] = dot(attended, weight_ref[:, left : left + out_ref.shape[2]]).astype(BF)


def spread_kernel(shares_ref, chosen_ref, home_ref, out_ref):
    odd = (lax.axis_index("tp") % 2) == 1
    total = jnp.sum(shares_ref[...].astype(F32), axis=0)
    moved = jnp.concatenate([total[:, 64:], total[:, :64]], axis=1)
    mixed = jnp.where(odd, moved, total).astype(BF).astype(F32)
    home_ref[...] = mixed[:8, : home_ref.shape[1]]
    far = mixed[8:]
    stack = jnp.concatenate(
        [far[:, :128], far[:, 128:256], far[:, 256:], jnp.zeros((104, LANES), F32)], axis=0
    )
    out_ref[...] = dot(chosen_ref[...], stack.astype(BF)).astype(BF)


def pick_kernel(placed_ref, home_ref, returned_ref, out_ref):
    far = dot(jnp.transpose(placed_ref[...].astype(F32)).astype(BF), returned_ref[...])
    far = jnp.concatenate([far[0:8], far[8:16], far[16:24, :64]], axis=1)
    out_ref[...] = jnp.concatenate([home_ref[...], far], axis=0).astype(BF)


def near(x):
    return pltpu.with_memory_space_constraint(x, pltpu.VMEM)


def held_back(x):
    return pltpu.with_memory_space_constraint(x, pltpu.HBM)


def call(kernel, out_shape, *args, far_args=(), scratch=(), in_hbm=False):
    outs = out_shape if in_hbm else [pltpu.VMEM(s.shape, s.dtype) for s in out_shape]
    return pl.pallas_call(
        kernel,
        out_shape=outs,
        in_specs=[NEAR] * len(args) + [ANYWHERE] * len(far_args),
        out_specs=[NEAR] * len(out_shape),
        scratch_shapes=scratch,
        compiler_params=pltpu.CompilerParams(vmem_limit_bytes=16 << 20),
    )(*(near(a) for a in args), *(held_back(a) for a in far_args))


def shards(queries, fresh_kv, kv_cache, out_weight, offsets, lengths):
    devices = lax.axis_size("req")
    columns = lax.axis_size("tp")
    row_count, width = queries.shape
    tokens = kv_cache.shape[2]
    cache = kv_cache.reshape(kv_cache.shape[1:])
    offsets = offsets.reshape(-1, LANES)
    lengths = lengths.reshape(-1, LANES)
    shape = jax.ShapeDtypeStruct
    slots = shape((devices * 4, LANES), BF)
    scratch = lambda x: pltpu.VMEM(x.shape, x.dtype)
    semaphores = pltpu.SemaphoreType.DMA
    long_scratch = pltpu.VMEM((8, HD), F32)
    inputs = (offsets, lengths, queries, fresh_kv)
    message, placed, mine = call(
        functools.partial(send_kernel, tokens),
        [slots, slots, shape((32, LANES), F32)],
        far_args=inputs,
        scratch=[*map(scratch, inputs), semaphores((4,))],
    )
    got = lax.all_to_all(message.reshape(devices, 4, LANES), "req", 0, 0, tiled=True)
    home_cache, home_out, chosen, long_start = call(
        home_kernel,
        [shape(cache.shape, BF), shape((HALF, width), F32), slots, shape((8, LANES), I32)],
        mine,
        far_args=(offsets, lengths, cache),
        scratch=[scratch(offsets), scratch(lengths), long_scratch, semaphores((3,))],
    )
    (shares,) = call(
        far_kernel,
        [shape((columns, row_count, 384), BF)],
        got.reshape(devices * 4, LANES), chosen, long_start, home_out, home_cache,
        far_args=(out_weight,),
        scratch=[scratch(out_weight), long_scratch, semaphores((1,))],
    )
    shares = lax.all_to_all(shares, "tp", 0, 0, tiled=True)
    home, spread = call(spread_kernel, [shape((HALF, width), F32), slots], shares, chosen)
    returned = lax.all_to_all(spread.reshape(devices, 4, LANES), "req", 0, 0, tiled=True)
    (mixed,) = call(
        pick_kernel,
        [shape((row_count, width), BF)],
        placed, home, returned.reshape(devices * 4, LANES),
        in_hbm=True,
    )
    return mixed


def solution(mesh):
    in_specs = (P("req", "tp"), P("req", "tp"), P("tp", None, "req"), P("tp", None), P(), P())
    out_specs = P("req", "tp")
    return jax.shard_map(shards, mesh=mesh, in_specs=in_specs, out_specs=out_specs, check_vma=False)
```

```python
import functools

import jax
import jax.numpy as jnp
from jax import lax
from jax.experimental import pallas as pl
from jax.experimental.pallas import tpu as pltpu
from jax.sharding import PartitionSpec as P

HD = 80
G = 4
W = 4096
LMAX = 8192
LANES = 128
HALF = 8
REQ_FIRST = 52
TP_FIRST = 4
BF = jnp.bfloat16
F32 = jnp.float32
I32 = jnp.int32
NEAR = pl.BlockSpec(memory_space=pltpu.VMEM)
ANYWHERE = pl.BlockSpec(memory_space=pltpu.HBM)


def iota(shape, axis):
    return lax.broadcasted_iota(I32, shape, axis)


def dot(a, b):
    return jnp.dot(a, b, preferred_element_type=F32)


def dot_t(a, b):
    return lax.dot_general(a, b, (((1,), (1,)), ((), ())), preferred_element_type=F32)


def own_row(table_ref, index, shift):
    per_row = LANES // 16
    row = table_ref[pl.ds(index // per_row, 1), :]
    back = (index % per_row) * 16 + shift
    return pltpu.roll(row, (LANES - back) % LANES, 1)


def column(row, count):
    wide = jnp.broadcast_to(row, (count, LANES))
    same = iota((count, LANES), 0) == iota((count, LANES), 1)
    return jnp.sum(jnp.where(same, wide, 0), axis=1, keepdims=True)


def pack(queries, fresh, starts, lengths):
    lane = iota((HALF, LANES), 1)
    meta = jnp.where(lane == 96, 1, 0)
    meta = jnp.where(lane == 97, starts >> 7, meta)
    meta = jnp.where(lane == 98, starts & 127, meta)
    meta = jnp.where(lane == 99, lengths >> 7, meta)
    meta = jnp.where(lane == 100, lengths & 127, meta)
    third = jnp.concatenate([queries[:, 256:], fresh[:, 128:], jnp.zeros((HALF, 32), F32)], axis=1)
    return jnp.concatenate(
        [queries[:, :128], queries[:, 128:256], third + meta.astype(F32), fresh[:, :128]], axis=0
    )


def unpack(stack):
    meta = stack[16:24]
    starts = (meta[:, 97:98] * 128.0 + meta[:, 98:99]).astype(I32)
    lengths = (meta[:, 99:100] * 128.0 + meta[:, 100:101]).astype(I32)
    queries = jnp.concatenate([stack[0:8], stack[8:16], stack[16:24, :64]], axis=1)
    fresh = jnp.concatenate([stack[24:32], stack[16:24, 64:96]], axis=1)
    return queries, fresh[:, :HD], fresh[:, HD:], starts, lengths


def fetch(sources, targets, sems):
    copies = [
        pltpu.make_async_copy(s, t, sems.at[i]) for i, (s, t) in enumerate(zip(sources, targets))
    ]
    for copy in copies:
        copy.start()
    return copies


def send_kernel(
    tokens, offsets_hbm, lengths_hbm, queries_hbm, fresh_hbm, out_ref, placed_ref, mine_ref,
    offsets_ref, lengths_ref, queries_ref, fresh_ref, sems,
):
    sources = (offsets_hbm, lengths_hbm, queries_hbm, fresh_hbm)
    for copy in fetch(sources, (offsets_ref, lengths_ref, queries_ref, fresh_ref), sems):
        copy.wait()
    index = lax.axis_index("req")
    rows = out_ref.shape[0]
    offsets = own_row(offsets_ref, index, 0)
    owners = offsets // tokens
    starts = column(offsets - owners * tokens, 16)
    lengths = column(own_row(lengths_ref, index, 0), 16)
    slot_of = jnp.where(owners < REQ_FIRST, owners + (rows // 4 - REQ_FIRST), owners - REQ_FIRST)
    far = pltpu.roll(slot_of, LANES - HALF, 1)
    lane = iota((1, LANES), 1)
    spread = jnp.where(lane < 8, far, 0)
    for k in (1, 2, 3):
        here = (lane >= 8 * k) & (lane < 8 * k + 8)
        spread = spread + jnp.where(here, pltpu.roll(far, 8 * k, 1), 0)
    row = iota((rows, LANES), 0)
    col = iota((rows, LANES), 1)
    hit = ((row >> 2) == jnp.broadcast_to(spread, (rows, LANES))) & ((row & 3) == (col >> 3))
    placed = jnp.where(hit, 1.0, 0.0).astype(BF)
    placed_ref[...] = placed
    queries = queries_ref[...].astype(F32)
    fresh = fresh_ref[...].astype(F32)
    mine_ref[...] = pack(queries[:8], fresh[:8], starts[:8], lengths[:8])
    stack = pack(queries[8:], fresh[8:], starts[8:], lengths[8:])
    stack = jnp.concatenate([stack, jnp.zeros((96, LANES), F32)], axis=0)
    out_ref[...] = dot(placed, stack.astype(BF)).astype(BF)


def attend(stack, long_start, cache_ref, long_ref):
    tokens = cache_ref.shape[1]
    scale = HD ** (-0.5)
    queries, fresh_key, fresh_value, starts, lengths = unpack(stack)
    heads = [queries[:, g * HD : (g + 1) * HD] for g in range(G)]
    own = [jnp.sum(h * fresh_key, axis=1, keepdims=True) * scale for h in heads]
    is_long = lengths == LMAX

    @pl.when(jnp.max(lengths) == LMAX)
    def _():
        sub = iota((8, HD), 0)
        long_query = jnp.zeros((8, HD), F32)
        long_own = jnp.zeros((8, 1), F32)
        for g in range(G):
            picked = jnp.sum(jnp.where(is_long, heads[g], 0.0), axis=0, keepdims=True)
            long_query = jnp.where(sub == g, picked, long_query)
            picked_own = jnp.sum(jnp.where(is_long, own[g], 0.0), axis=0, keepdims=True)
            long_own = jnp.where(iota((8, 1), 0) == g, picked_own, long_own)
        long_value = jnp.sum(jnp.where(is_long, fresh_value, 0.0), axis=0, keepdims=True)
        span = W + LANES
        first = long_start + (LMAX - W + 1)
        base = jnp.minimum(first // LANES * LANES, tokens - span)
        window = pl.ds(pl.multiple_of(base, LANES), span)
        scores = dot(long_query.astype(BF), cache_ref[:HD, window]) * scale
        position = base + iota((8, span), 1)
        scores = jnp.where((position >= first) & (position < first + (W - 1)), scores, -jnp.inf)
        highest = jnp.maximum(jnp.max(scores, axis=1, keepdims=True), long_own)
        weights = jnp.exp(scores - highest)
        own_weight = jnp.exp(long_own - highest)
        totals = jnp.sum(weights, axis=1, keepdims=True) + own_weight
        summed = dot_t(weights.astype(BF), cache_ref[HD : 2 * HD, window])
        summed = summed + own_weight.astype(BF).astype(F32) * long_value
        long_ref[...] = summed / totals

    blocks = (tokens - LMAX) // LANES + 1
    before = (long_start + LANES - 1) // LANES
    after = (long_start + LMAX) // LANES
    last = tokens // LANES - 1
    keys, values, places = [], [], []
    for i in range(blocks):
        block = jnp.where(i < before, i, after + i - before)
        spare = block > last
        begin = pl.multiple_of(jnp.minimum(block, last) * LANES, LANES)
        keys.append(cache_ref[:HD, pl.ds(begin, LANES)])
        values.append(cache_ref[HD : 2 * HD, pl.ds(begin, LANES)])
        places.append(jnp.where(spare, -LANES, begin) + iota((1, LANES), 1))
    keys = jnp.concatenate(keys, axis=1)
    values = jnp.concatenate(values, axis=1)
    position = jnp.concatenate(places, axis=1)
    ends = starts + lengths
    firsts = jnp.maximum(starts, ends - (W - 1))
    ends = jnp.concatenate([ends] * G, axis=0)
    firsts = jnp.concatenate([firsts] * G, axis=0)
    own_all = jnp.concatenate(own, axis=0)
    scores = dot(jnp.concatenate(heads, axis=0).astype(BF), keys) * scale
    scores = jnp.where((position >= firsts) & (position < ends), scores, -jnp.inf)
    highest = jnp.maximum(jnp.max(scores, axis=1, keepdims=True), own_all)
    weights = jnp.exp(scores - highest)
    own_weight = jnp.exp(own_all - highest)
    totals = jnp.sum(weights, axis=1, keepdims=True) + own_weight
    summed = dot_t(weights.astype(BF), values)
    summed = summed + own_weight.astype(BF).astype(F32) * jnp.concatenate([fresh_value] * G, axis=0)
    outs = summed / totals
    long_out = long_ref[...]
    return jnp.concatenate(
        [jnp.where(is_long, long_out[g : g + 1], outs[g * 8 : g * 8 + 8]) for g in range(G)], axis=1
    )


def home_kernel(
    mine_ref, offsets_hbm, lengths_hbm, cache_hbm,
    cache_ref, home_ref, chosen_ref, long_start_ref, offsets_ref, lengths_ref, long_ref, sems,
):
    index = lax.axis_index("req")
    tokens = cache_ref.shape[1]
    sources = (offsets_hbm, lengths_hbm, cache_hbm)
    copies = fetch(sources, (offsets_ref, lengths_ref, cache_ref), sems)
    copies[0].wait()
    copies[1].wait()
    offsets = offsets_ref[...]
    held = (offsets // tokens) == index
    long_start = jnp.sum(jnp.where(held & (lengths_ref[...] == LMAX), offsets, 0)) - index * tokens
    long_start_ref[...] = jnp.full((8, LANES), long_start, I32)
    rows = chosen_ref.shape[0]
    lane = iota((8, LANES), 1)
    flags = jnp.where(held & ((lane & 15) >= HALF), 1.0, 0.0).astype(BF)
    slots = rows // 4
    source = (iota((rows, 8), 0) >> 2) + REQ_FIRST
    line = jnp.where(source < slots, source, source - slots) >> 3
    here = dot(jnp.where(line == iota((rows, 8), 1), 1.0, 0.0).astype(BF), flags)
    earlier = dot(jnp.where(line > iota((rows, 8), 1), 1.0, 0.0).astype(BF), flags)
    row = iota((rows, LANES), 0)
    col = iota((rows, LANES), 1)
    source = (row >> 2) + REQ_FIRST
    slot = jnp.where(source < slots, source, source - slots) & 7
    valid = jnp.sum(jnp.where((col >> 4) == slot, here, 0.0), axis=1, keepdims=True)
    rank = jnp.sum(earlier + jnp.where((col >> 4) < slot, here, 0.0), axis=1, keepdims=True)
    hit = (valid > 0.5) & (rank.astype(I32) == (col & 7)) & ((row & 3) == (col >> 3))
    chosen_ref[...] = jnp.where(hit, 1.0, 0.0).astype(BF)
    long_ref[...] = jnp.zeros_like(long_ref)
    copies[2].wait()
    home_ref[...] = attend(mine_ref[...], long_start, cache_ref, long_ref)


def far_kernel(
    got_ref, chosen_ref, long_start_ref, home_ref, cache_ref, weight_hbm, out_ref,
    weight_ref, long_ref, sems,
):
    (copy,) = fetch((weight_hbm,), (weight_ref,), sems)
    long_ref[...] = jnp.zeros_like(long_ref)
    held = dot(jnp.transpose(chosen_ref[...].astype(F32)).astype(BF), got_ref[...])
    far = attend(held[:32], jnp.max(long_start_ref[0:1, :]), cache_ref, long_ref)
    attended = jnp.concatenate([home_ref[...], far], axis=0).astype(BF)
    copy.wait()
    width = G * HD
    for j in range(out_ref.shape[0]):
        left = j * width // LANES * LANES
        out_ref[(j - TP_FIRST) % out_ref.shape[0]] = dot(attended, weight_ref[:, left : left + out_ref.shape[2]]).astype(BF)


def spread_kernel(shares_ref, chosen_ref, home_ref, out_ref):
    odd = (lax.axis_index("tp") % 2) == 1
    total = jnp.sum(shares_ref[...].astype(F32), axis=0)
    moved = jnp.concatenate([total[:, 64:], total[:, :64]], axis=1)
    mixed = jnp.where(odd, moved, total).astype(BF).astype(F32)
    home_ref[...] = mixed[:8, : home_ref.shape[1]]
    far = mixed[8:]
    stack = jnp.concatenate(
        [far[:, :128], far[:, 128:256], far[:, 256:], jnp.zeros((104, LANES), F32)], axis=0
    )
    out_ref[...] = dot(chosen_ref[...], stack.astype(BF)).astype(BF)


def pick_kernel(placed_ref, home_ref, returned_ref, out_ref):
    far = dot(jnp.transpose(placed_ref[...].astype(F32)).astype(BF), returned_ref[...])
    far = jnp.concatenate([far[0:8], far[8:16], far[16:24, :64]], axis=1)
    out_ref[...] = jnp.concatenate([home_ref[...], far], axis=0).astype(BF)


def exchange(x, axis, first):
    size = lax.axis_size(axis)
    group = [(first + i) % size for i in range(size)]
    return lax.all_to_all(x, axis, 0, 0, axis_index_groups=[group], tiled=True)


def near(x):
    return pltpu.with_memory_space_constraint(x, pltpu.VMEM)


def held_back(x):
    return pltpu.with_memory_space_constraint(x, pltpu.HBM)


def call(kernel, out_shape, *args, far_args=(), scratch=(), in_hbm=False):
    outs = out_shape if in_hbm else [pltpu.VMEM(s.shape, s.dtype) for s in out_shape]
    return pl.pallas_call(
        kernel,
        out_shape=outs,
        in_specs=[NEAR] * len(args) + [ANYWHERE] * len(far_args),
        out_specs=[NEAR] * len(out_shape),
        scratch_shapes=scratch,
        compiler_params=pltpu.CompilerParams(vmem_limit_bytes=16 << 20),
    )(*(near(a) for a in args), *(held_back(a) for a in far_args))


def shards(queries, fresh_kv, kv_cache, out_weight, offsets, lengths):
    devices = lax.axis_size("req")
    columns = lax.axis_size("tp")
    row_count, width = queries.shape
    tokens = kv_cache.shape[2]
    cache = kv_cache.reshape(kv_cache.shape[1:])
    offsets = offsets.reshape(-1, LANES)
    lengths = lengths.reshape(-1, LANES)
    shape = jax.ShapeDtypeStruct
    slots = shape((devices * 4, LANES), BF)
    scratch = lambda x: pltpu.VMEM(x.shape, x.dtype)
    semaphores = pltpu.SemaphoreType.DMA
    long_scratch = pltpu.VMEM((8, HD), F32)
    inputs = (offsets, lengths, queries, fresh_kv)
    message, placed, mine = call(
        functools.partial(send_kernel, tokens),
        [slots, slots, shape((32, LANES), F32)],
        far_args=inputs,
        scratch=[*map(scratch, inputs), semaphores((4,))],
    )
    got = exchange(message.reshape(devices, 4, LANES), "req", REQ_FIRST)
    home_cache, home_out, chosen, long_start = call(
        home_kernel,
        [shape(cache.shape, BF), shape((HALF, width), F32), slots, shape((8, LANES), I32)],
        mine,
        far_args=(offsets, lengths, cache),
        scratch=[scratch(offsets), scratch(lengths), long_scratch, semaphores((3,))],
    )
    (shares,) = call(
        far_kernel,
        [shape((columns, row_count, 384), BF)],
        got.reshape(devices * 4, LANES), chosen, long_start, home_out, home_cache,
        far_args=(out_weight,),
        scratch=[scratch(out_weight), long_scratch, semaphores((1,))],
    )
    shares = exchange(shares, "tp", TP_FIRST)
    home, spread = call(spread_kernel, [shape((HALF, width), F32), slots], shares, chosen)
    returned = exchange(spread.reshape(devices, 4, LANES), "req", REQ_FIRST)
    (mixed,) = call(
        pick_kernel,
        [shape((row_count, width), BF)],
        placed, home, returned.reshape(devices * 4, LANES),
        in_hbm=True,
    )
    return mixed


def solution(mesh):
    in_specs = (P("req", "tp"), P("req", "tp"), P("tp", None, "req"), P("tp", None), P(), P())
    out_specs = P("req", "tp")
    return jax.shard_map(shards, mesh=mesh, in_specs=in_specs, out_specs=out_specs, check_vma=False)
```

```python
import functools

import jax
import jax.numpy as jnp
from jax import lax
from jax.experimental import pallas as pl
from jax.experimental.pallas import tpu as pltpu
from jax.sharding import PartitionSpec as P

HD = 80
G = 4
W = 4096
LMAX = 8192
LANES = 128
HALF = 8
REQ_FIRST = 52
TP_FIRST = 4
BF = jnp.bfloat16
F32 = jnp.float32
I32 = jnp.int32
NEAR = pl.BlockSpec(memory_space=pltpu.VMEM)
ANYWHERE = pl.BlockSpec(memory_space=pltpu.HBM)


def iota(shape, axis):
    return lax.broadcasted_iota(I32, shape, axis)


def dot(a, b):
    return jnp.dot(a, b, preferred_element_type=F32)


def dot_t(a, b):
    return lax.dot_general(a, b, (((1,), (1,)), ((), ())), preferred_element_type=F32)


def owner_of(offsets, tokens):
    return ((offsets.astype(F32) + 0.5) * (1.0 / tokens)).astype(I32)


def own_row(table_ref, index, shift):
    per_row = LANES // 16
    row = table_ref[pl.ds(index // per_row, 1), :]
    back = (index % per_row) * 16 + shift
    return pltpu.roll(row, (LANES - back) % LANES, 1)


def column(row, count):
    wide = jnp.broadcast_to(row, (count, LANES))
    same = iota((count, LANES), 0) == iota((count, LANES), 1)
    return jnp.sum(jnp.where(same, wide, 0), axis=1, keepdims=True)


def pack(queries, fresh, starts, lengths):
    lane = iota((HALF, LANES), 1)
    meta = jnp.where(lane == 96, 1, 0)
    meta = jnp.where(lane == 97, starts >> 7, meta)
    meta = jnp.where(lane == 98, starts & 127, meta)
    meta = jnp.where(lane == 99, lengths >> 7, meta)
    meta = jnp.where(lane == 100, lengths & 127, meta)
    third = jnp.concatenate([queries[:, 256:], fresh[:, 128:], jnp.zeros((HALF, 32), F32)], axis=1)
    return jnp.concatenate(
        [queries[:, :128], queries[:, 128:256], third + meta.astype(F32), fresh[:, :128]], axis=0
    )


def unpack(stack):
    meta = stack[16:24]
    starts = (meta[:, 97:98] * 128.0 + meta[:, 98:99]).astype(I32)
    lengths = (meta[:, 99:100] * 128.0 + meta[:, 100:101]).astype(I32)
    queries = jnp.concatenate([stack[0:8], stack[8:16], stack[16:24, :64]], axis=1)
    fresh = jnp.concatenate([stack[24:32], stack[16:24, 64:96]], axis=1)
    return queries, fresh[:, :HD], fresh[:, HD:], starts, lengths


def fetch(sources, targets, sems):
    copies = [
        pltpu.make_async_copy(s, t, sems.at[i]) for i, (s, t) in enumerate(zip(sources, targets))
    ]
    for copy in copies:
        copy.start()
    return copies


def slot_of(owners, slots):
    return jnp.where(owners < REQ_FIRST, owners + (slots - REQ_FIRST), owners - REQ_FIRST)


def send_kernel(
    tokens, offsets_hbm, lengths_hbm, queries_hbm, fresh_hbm, out_ref,
    offsets_ref, lengths_ref, queries_ref, fresh_ref, sems,
):
    sources = (offsets_hbm, lengths_hbm, queries_hbm, fresh_hbm)
    for copy in fetch(sources, (offsets_ref, lengths_ref, queries_ref, fresh_ref), sems):
        copy.wait()
    index = lax.axis_index("req")
    rows = out_ref.shape[0]
    offsets = own_row(offsets_ref, index, HALF)
    owners = owner_of(offsets, tokens)
    starts = column(offsets - owners * tokens, HALF)
    lengths = column(own_row(lengths_ref, index, HALF), HALF)
    far = slot_of(owners, rows // 4)
    lane = iota((1, LANES), 1)
    spread = jnp.where(lane < 8, far, 0)
    for k in (1, 2, 3):
        here = (lane >= 8 * k) & (lane < 8 * k + 8)
        spread = spread + jnp.where(here, pltpu.roll(far, 8 * k, 1), 0)
    row = iota((rows, LANES), 0)
    col = iota((rows, LANES), 1)
    hit = ((row >> 2) == jnp.broadcast_to(spread, (rows, LANES))) & ((row & 3) == (col >> 3))
    placed = jnp.where(hit, 1.0, 0.0).astype(BF)
    queries = queries_ref[...].astype(F32)
    fresh = fresh_ref[...].astype(F32)
    stack = pack(queries[8:], fresh[8:], starts, lengths)
    stack = jnp.concatenate([stack, jnp.zeros((96, LANES), F32)], axis=0)
    out_ref[...] = dot(placed, stack.astype(BF)).astype(BF)


def weigh(queries, keys, values, inside, own, own_value):
    scores = jnp.where(inside, dot(queries.astype(BF), keys) * HD ** (-0.5), -jnp.inf)
    highest = jnp.maximum(jnp.max(scores, axis=1, keepdims=True), own)
    weights = jnp.exp(scores - highest)
    own_weight = jnp.exp(own - highest)
    totals = jnp.sum(weights, axis=1, keepdims=True) + own_weight
    summed = dot_t(weights.astype(BF), values) + own_weight.astype(BF).astype(F32) * own_value
    return summed / totals


def attend(queries, fresh_key, fresh_value, starts, lengths, long_start, cache_ref):
    tokens = cache_ref.shape[1]
    heads = [queries[:, g * HD : (g + 1) * HD] for g in range(G)]
    own = [jnp.sum(h * fresh_key, axis=1, keepdims=True) * HD ** (-0.5) for h in heads]
    is_long = lengths == LMAX
    long_query = jnp.zeros((8, HD), F32)
    long_own = jnp.zeros((8, 1), F32)
    for g in range(G):
        picked = jnp.sum(jnp.where(is_long, heads[g], 0.0), axis=0, keepdims=True)
        long_query = jnp.where(iota((8, HD), 0) == g, picked, long_query)
        picked_own = jnp.sum(jnp.where(is_long, own[g], 0.0), axis=0, keepdims=True)
        long_own = jnp.where(iota((8, 1), 0) == g, picked_own, long_own)
    long_value = jnp.sum(jnp.where(is_long, fresh_value, 0.0), axis=0, keepdims=True)
    span = W + LANES
    first = long_start + (LMAX - W + 1)
    base = jnp.minimum(first // LANES * LANES, tokens - span)
    window = pl.ds(pl.multiple_of(base, LANES), span)
    position = base + iota((8, span), 1)
    long_out = weigh(
        long_query,
        cache_ref[:HD, window],
        cache_ref[HD : 2 * HD, window],
        (position >= first) & (position < first + (W - 1)),
        long_own,
        long_value,
    )
    blocks = (tokens - LMAX) // LANES + 1
    before = (long_start + LANES - 1) // LANES
    after = (long_start + LMAX) // LANES
    last = tokens // LANES - 1
    keys, values, places = [], [], []
    for i in range(blocks):
        block = jnp.where(i < before, i, after + i - before)
        spare = block > last
        begin = pl.multiple_of(jnp.minimum(block, last) * LANES, LANES)
        keys.append(cache_ref[:HD, pl.ds(begin, LANES)])
        values.append(cache_ref[HD : 2 * HD, pl.ds(begin, LANES)])
        places.append(jnp.where(spare, -LANES, begin) + iota((1, LANES), 1))
    position = jnp.concatenate(places, axis=1)
    ends = starts + lengths
    firsts = jnp.maximum(starts, ends - (W - 1))
    ends = jnp.concatenate([ends] * G, axis=0)
    firsts = jnp.concatenate([firsts] * G, axis=0)
    outs = weigh(
        jnp.concatenate(heads, axis=0),
        jnp.concatenate(keys, axis=1),
        jnp.concatenate(values, axis=1),
        (position >= firsts) & (position < ends),
        jnp.concatenate(own, axis=0),
        jnp.concatenate([fresh_value] * G, axis=0),
    )
    return jnp.concatenate(
        [jnp.where(is_long, long_out[g : g + 1], outs[g * 8 : g * 8 + 8]) for g in range(G)], axis=1
    )


def home_kernel(
    offsets_hbm, lengths_hbm, queries_hbm, fresh_hbm, cache_hbm,
    cache_ref, home_ref, chosen_ref, chosen_t_ref, placed_t_ref, long_start_ref,
    offsets_ref, lengths_ref, queries_ref, fresh_ref, sems,
):
    sources = (offsets_hbm, lengths_hbm, queries_hbm, fresh_hbm, cache_hbm)
    copies = fetch(sources, (offsets_ref, lengths_ref, queries_ref, fresh_ref, cache_ref), sems)
    for copy in copies[:4]:
        copy.wait()
    index = lax.axis_index("req")
    tokens = cache_ref.shape[1]
    rows = chosen_ref.shape[0]
    slots = rows // 4
    offsets = offsets_ref[...]
    held = owner_of(offsets, tokens) == index
    long_start = jnp.sum(jnp.where(held & (lengths_ref[...] == LMAX), offsets, 0)) - index * tokens
    long_start_ref[...] = jnp.full((8, LANES), long_start, I32)
    flags = jnp.where(held & ((iota((8, LANES), 1) & 15) >= HALF), 1.0, 0.0).astype(BF)
    source = (iota((rows, 8), 0) >> 2) + REQ_FIRST
    line = jnp.where(source < slots, source, source - slots) >> 3
    here = dot(jnp.where(line == iota((rows, 8), 1), 1.0, 0.0).astype(BF), flags)
    earlier = dot(jnp.where(line > iota((rows, 8), 1), 1.0, 0.0).astype(BF), flags)
    row = iota((rows, LANES), 0)
    col = iota((rows, LANES), 1)
    source = (row >> 2) + REQ_FIRST
    slot = jnp.where(source < slots, source, source - slots) & 7
    valid = jnp.sum(jnp.where((col >> 4) == slot, here, 0.0), axis=1, keepdims=True)
    rank = jnp.sum(earlier + jnp.where((col >> 4) < slot, here, 0.0), axis=1, keepdims=True)
    hit = (valid > 0.5) & (rank.astype(I32) == (col & 7)) & ((row & 3) == (col >> 3))
    chosen = jnp.where(hit, 1.0, 0.0)
    chosen_ref[...] = chosen.astype(BF)
    chosen_t_ref[...] = jnp.transpose(chosen)[:32].astype(BF)
    offsets = own_row(offsets_ref, index, 0)
    starts = column(offsets, 16)
    lengths = column(own_row(lengths_ref, index, 0), 16)
    far = slot_of(owner_of(starts[8:], tokens), slots)
    far = jnp.concatenate([far] * 4, axis=0)
    row = iota((32, rows), 0)
    col = iota((32, rows), 1)
    placed_t_ref[...] = jnp.where(((col >> 2) == far) & ((col & 3) == (row >> 3)), 1.0, 0.0).astype(BF)
    queries = queries_ref[...].astype(F32)[:8]
    fresh = fresh_ref[...].astype(F32)[:8]
    copies[4].wait()
    home_ref[...] = attend(
        queries, fresh[:, :HD], fresh[:, HD:], starts[:8] - index * tokens, lengths[:8],
        long_start, cache_ref,
    )


def far_kernel(
    got_ref, chosen_t_ref, long_start_ref, home_ref, cache_ref, weight_hbm, out_ref,
    weight_ref, sems,
):
    (copy,) = fetch((weight_hbm,), (weight_ref,), sems)
    held = dot(chosen_t_ref[...], got_ref[...])
    far = attend(*unpack(held), jnp.max(long_start_ref[0:1, :]), cache_ref)
    attended = jnp.concatenate([home_ref[...], far], axis=0).astype(BF)
    copy.wait()
    mixed = dot(attended, weight_ref[...])
    columns = out_ref.shape[0]
    low = iota((HALF, LANES), 1) < 64
    for j in range(columns):
        left = j * G * HD // LANES * LANES
        tiles = [mixed[:, left + k * LANES : left + (k + 1) * LANES] for k in range(3)]
        if j % 2 == 0:
            half = jnp.where(low, tiles[2][:8], pltpu.roll(tiles[2][8:], 64, 1))
            full = tiles[:2]
        else:
            half = jnp.where(low, pltpu.roll(tiles[0][:8], 64, 1), tiles[0][8:])
            full = tiles[1:]
        out_ref[(j - TP_FIRST) % columns] = jnp.concatenate([*full, half], axis=0).astype(BF)


def spread_kernel(shares_ref, chosen_ref, home_ref, out_ref):
    mixed = jnp.sum(shares_ref[...].astype(F32), axis=0).astype(BF).astype(F32)
    home_ref[...] = mixed
    stack = jnp.concatenate(
        [mixed[8:16], mixed[24:32], mixed[32:40], jnp.zeros((104, LANES), F32)], axis=0
    )
    out_ref[...] = dot(chosen_ref[...], stack.astype(BF)).astype(BF)


def pick_kernel(placed_t_ref, home_ref, returned_ref, out_ref):
    far = dot(placed_t_ref[...], returned_ref[...])
    home = home_ref[...]
    first = jnp.concatenate([home[0:8], far[0:8]], axis=0)
    second = jnp.concatenate([home[16:24], far[8:16]], axis=0)
    half = jnp.concatenate([home[32:40], pltpu.roll(far[16:24], 64, 1)], axis=0)[:, :64]
    odd = (lax.axis_index("tp") % 2) == 1
    even = jnp.concatenate([first, second, half], axis=1)
    out_ref[...] = jnp.where(odd, jnp.concatenate([half, first, second], axis=1), even).astype(BF)


def exchange(x, axis, first):
    size = lax.axis_size(axis)
    group = [(first + i) % size for i in range(size)]
    return lax.all_to_all(x, axis, 0, 0, axis_index_groups=[group], tiled=True)


def near(x):
    return pltpu.with_memory_space_constraint(x, pltpu.VMEM)


def held_back(x):
    return pltpu.with_memory_space_constraint(x, pltpu.HBM)


def call(kernel, out_shape, *args, far_args=(), scratch=(), in_hbm=False):
    outs = out_shape if in_hbm else [pltpu.VMEM(s.shape, s.dtype) for s in out_shape]
    return pl.pallas_call(
        kernel,
        out_shape=outs,
        in_specs=[NEAR] * len(args) + [ANYWHERE] * len(far_args),
        out_specs=[NEAR] * len(out_shape),
        scratch_shapes=scratch,
        compiler_params=pltpu.CompilerParams(vmem_limit_bytes=16 << 20),
    )(*(near(a) for a in args), *(held_back(a) for a in far_args))


def shards(queries, fresh_kv, kv_cache, out_weight, offsets, lengths):
    devices = lax.axis_size("req")
    columns = lax.axis_size("tp")
    row_count, width = queries.shape
    tokens = kv_cache.shape[2]
    cache = kv_cache.reshape(kv_cache.shape[1:])
    offsets = offsets.reshape(-1, LANES)
    lengths = lengths.reshape(-1, LANES)
    shape = jax.ShapeDtypeStruct
    slots = shape((devices * 4, LANES), BF)
    scratch = lambda x: pltpu.VMEM(x.shape, x.dtype)
    semaphores = pltpu.SemaphoreType.DMA
    inputs = (offsets, lengths, queries, fresh_kv)
    (message,) = call(
        functools.partial(send_kernel, tokens),
        [slots],
        far_args=inputs,
        scratch=[*map(scratch, inputs), semaphores((4,))],
    )
    got = exchange(message.reshape(devices, 4, LANES), "req", REQ_FIRST)
    home_cache, home_out, chosen, chosen_t, placed_t, long_start = call(
        home_kernel,
        [
            shape(cache.shape, BF),
            shape((HALF, width), F32),
            slots,
            shape((32, devices * 4), BF),
            shape((32, devices * 4), BF),
            shape((8, LANES), I32),
        ],
        far_args=(*inputs, cache),
        scratch=[*map(scratch, inputs), semaphores((5,))],
    )
    (shares,) = call(
        far_kernel,
        [shape((columns, 40, LANES), BF)],
        got.reshape(devices * 4, LANES), chosen_t, long_start, home_out, home_cache,
        far_args=(out_weight,),
        scratch=[scratch(out_weight), semaphores((1,))],
    )
    shares = exchange(shares, "tp", TP_FIRST)
    home, spread = call(spread_kernel, [shape((40, LANES), F32), slots], shares, chosen)
    returned = exchange(spread.reshape(devices, 4, LANES), "req", REQ_FIRST)
    (mixed,) = call(
        pick_kernel,
        [shape((row_count, width), BF)],
        placed_t, home, returned.reshape(devices * 4, LANES),
        in_hbm=True,
    )
    return mixed


def solution(mesh):
    in_specs = (P("req", "tp"), P("req", "tp"), P("tp", None, "req"), P("tp", None), P(), P())
    out_specs = P("req", "tp")
    return jax.shard_map(shards, mesh=mesh, in_specs=in_specs, out_specs=out_specs, check_vma=False)
```

```python
import functools

import jax
import jax.numpy as jnp
from jax import lax
from jax.experimental import pallas as pl
from jax.experimental.pallas import tpu as pltpu
from jax.sharding import PartitionSpec as P

HD = 80
G = 4
W = 4096
LMAX = 8192
LANES = 128
HALF = 8
REQ_FIRST = 52
TP_FIRST = 4
BF = jnp.bfloat16
F32 = jnp.float32
I32 = jnp.int32
NEAR = pl.BlockSpec(memory_space=pltpu.VMEM)
ANYWHERE = pl.BlockSpec(memory_space=pltpu.HBM)


def iota(shape, axis):
    return lax.broadcasted_iota(I32, shape, axis)


def dot(a, b):
    return jnp.dot(a, b, preferred_element_type=F32)


def dot_t(a, b):
    return lax.dot_general(a, b, (((1,), (1,)), ((), ())), preferred_element_type=F32)


def owner_of(offsets, tokens):
    return ((offsets.astype(F32) + 0.5) * (1.0 / tokens)).astype(I32)


def own_row(table_ref, index, shift):
    per_row = LANES // 16
    row = table_ref[pl.ds(index // per_row, 1), :]
    back = (index % per_row) * 16 + shift
    return pltpu.roll(row, (LANES - back) % LANES, 1)


def column(row, count):
    wide = jnp.broadcast_to(row, (count, LANES))
    same = iota((count, LANES), 0) == iota((count, LANES), 1)
    return jnp.sum(jnp.where(same, wide, 0), axis=1, keepdims=True)


def pack(queries, fresh, starts, lengths):
    lane = iota((HALF, LANES), 1)
    meta = jnp.where(lane == 96, 1, 0)
    meta = jnp.where(lane == 97, starts >> 7, meta)
    meta = jnp.where(lane == 98, starts & 127, meta)
    meta = jnp.where(lane == 99, lengths >> 7, meta)
    meta = jnp.where(lane == 100, lengths & 127, meta)
    third = jnp.concatenate([queries[:, 256:], fresh[:, 128:], jnp.zeros((HALF, 32), F32)], axis=1)
    return jnp.concatenate(
        [queries[:, :128], queries[:, 128:256], third + meta.astype(F32), fresh[:, :128]], axis=0
    )


def unpack(stack):
    meta = stack[16:24]
    starts = (meta[:, 97:98] * 128.0 + meta[:, 98:99]).astype(I32)
    lengths = (meta[:, 99:100] * 128.0 + meta[:, 100:101]).astype(I32)
    queries = jnp.concatenate([stack[0:8], stack[8:16], stack[16:24, :64]], axis=1)
    fresh = jnp.concatenate([stack[24:32], stack[16:24, 64:96]], axis=1)
    return queries, fresh[:, :HD], fresh[:, HD:], starts, lengths


def fetch(sources, targets, sems):
    copies = [
        pltpu.make_async_copy(s, t, sems.at[i]) for i, (s, t) in enumerate(zip(sources, targets))
    ]
    for copy in copies:
        copy.start()
    return copies


def slot_of(owners, slots):
    return jnp.where(owners < REQ_FIRST, owners + (slots - REQ_FIRST), owners - REQ_FIRST)


def send_kernel(
    tokens, offsets_hbm, lengths_hbm, queries_hbm, fresh_hbm, out_ref,
    offsets_ref, lengths_ref, queries_ref, fresh_ref, sems,
):
    sources = (offsets_hbm, lengths_hbm, queries_hbm, fresh_hbm)
    for copy in fetch(sources, (offsets_ref, lengths_ref, queries_ref, fresh_ref), sems):
        copy.wait()
    index = lax.axis_index("req")
    rows = out_ref.shape[0]
    offsets = own_row(offsets_ref, index, HALF)
    owners = owner_of(offsets, tokens)
    starts = column(offsets - owners * tokens, HALF)
    lengths = column(own_row(lengths_ref, index, HALF), HALF)
    far = slot_of(owners, rows // 4)
    lane = iota((1, LANES), 1)
    spread = jnp.where(lane < 8, far, 0)
    for k in (1, 2, 3):
        here = (lane >= 8 * k) & (lane < 8 * k + 8)
        spread = spread + jnp.where(here, pltpu.roll(far, 8 * k, 1), 0)
    row = iota((rows, LANES), 0)
    col = iota((rows, LANES), 1)
    hit = ((row >> 2) == jnp.broadcast_to(spread, (rows, LANES))) & ((row & 3) == (col >> 3))
    placed = jnp.where(hit, 1.0, 0.0).astype(BF)
    queries = queries_ref[...].astype(F32)
    fresh = fresh_ref[...].astype(F32)
    stack = pack(queries[8:], fresh[8:], starts, lengths)
    stack = jnp.concatenate([stack, jnp.zeros((96, LANES), F32)], axis=0)
    out_ref[...] = dot(placed, stack.astype(BF)).astype(BF)


def weigh(queries, keys, values, inside, own, own_value):
    scores = jnp.where(inside, dot(queries.astype(BF), keys) * HD ** (-0.5), -jnp.inf)
    highest = jnp.maximum(jnp.max(scores, axis=1, keepdims=True), own)
    weights = jnp.exp(scores - highest)
    own_weight = jnp.exp(own - highest)
    totals = jnp.sum(weights, axis=1, keepdims=True) + own_weight
    summed = dot_t(weights.astype(BF), values) + own_weight.astype(BF).astype(F32) * own_value
    return summed / totals


def places(long_start, tokens):
    before = (long_start + LANES - 1) // LANES
    after = (long_start + LMAX) // LANES
    last = tokens // LANES - 1
    blocks = []
    for i in range((tokens - LMAX) // LANES + 1):
        block = jnp.where(i < before, i, after + i - before)
        blocks.append((pl.multiple_of(jnp.minimum(block, last) * LANES, LANES), block > last))
    first = long_start + (LMAX - W + 1)
    base = jnp.minimum(first // LANES * LANES, tokens - (W + LANES))
    return blocks, first, pl.multiple_of(base, LANES)


def attend(queries, fresh_key, fresh_value, starts, lengths, long_start, tokens, near_ref):
    blocks, first, base = places(long_start, tokens)
    others, span = len(blocks) * LANES, W + LANES
    heads = [queries[:, g * HD : (g + 1) * HD] for g in range(G)]
    own = [jnp.sum(h * fresh_key, axis=1, keepdims=True) * HD ** (-0.5) for h in heads]
    is_long = lengths == LMAX
    long_query = jnp.zeros((8, HD), F32)
    long_own = jnp.zeros((8, 1), F32)
    for g in range(G):
        picked = jnp.sum(jnp.where(is_long, heads[g], 0.0), axis=0, keepdims=True)
        long_query = jnp.where(iota((8, HD), 0) == g, picked, long_query)
        picked_own = jnp.sum(jnp.where(is_long, own[g], 0.0), axis=0, keepdims=True)
        long_own = jnp.where(iota((8, 1), 0) == g, picked_own, long_own)
    long_value = jnp.sum(jnp.where(is_long, fresh_value, 0.0), axis=0, keepdims=True)
    position = base + iota((8, span), 1)
    long_out = weigh(
        long_query,
        near_ref[:HD, others:],
        near_ref[HD : 2 * HD, others:],
        (position >= first) & (position < first + (W - 1)),
        long_own,
        long_value,
    )
    position = jnp.concatenate(
        [jnp.where(spare, -LANES, begin) + iota((1, LANES), 1) for begin, spare in blocks], axis=1
    )
    ends = starts + lengths
    firsts = jnp.maximum(starts, ends - (W - 1))
    ends = jnp.concatenate([ends] * G, axis=0)
    firsts = jnp.concatenate([firsts] * G, axis=0)
    outs = weigh(
        jnp.concatenate(heads, axis=0),
        near_ref[:HD, :others],
        near_ref[HD : 2 * HD, :others],
        (position >= firsts) & (position < ends),
        jnp.concatenate(own, axis=0),
        jnp.concatenate([fresh_value] * G, axis=0),
    )
    return jnp.concatenate(
        [jnp.where(is_long, long_out[g : g + 1], outs[g * 8 : g * 8 + 8]) for g in range(G)], axis=1
    )


def home_kernel(
    offsets_hbm, lengths_hbm, queries_hbm, fresh_hbm, cache_hbm, weight_hbm,
    near_ref, weight_ref, home_ref, chosen_ref, chosen_t_ref, placed_t_ref, long_start_ref,
    offsets_ref, lengths_ref, queries_ref, fresh_ref, sems, weight_sems, near_sems,
):
    sources = (offsets_hbm, lengths_hbm, queries_hbm, fresh_hbm)
    copies = fetch(sources, (offsets_ref, lengths_ref, queries_ref, fresh_ref), sems)
    weight_rows = pl.ds(0, weight_ref.shape[0])
    (weight_copy,) = fetch((weight_hbm.at[weight_rows],), (weight_ref,), weight_sems)
    for copy in copies[:2]:
        copy.wait()
    index = lax.axis_index("req")
    tokens = cache_hbm.shape[1]
    rows = chosen_ref.shape[0]
    slots = rows // 4
    offsets = offsets_ref[...]
    held = owner_of(offsets, tokens) == index
    long_start = jnp.sum(jnp.where(held & (lengths_ref[...] == LMAX), offsets, 0)) - index * tokens
    blocks, _, base = places(long_start, tokens)
    sources = [cache_hbm.at[:, pl.ds(begin, LANES)] for begin, _ in blocks]
    targets = [near_ref.at[:, pl.ds(i * LANES, LANES)] for i in range(len(blocks))]
    sources.append(cache_hbm.at[:, pl.ds(base, W + LANES)])
    targets.append(near_ref.at[:, pl.ds(len(blocks) * LANES, W + LANES)])
    near_copies = fetch(sources, targets, near_sems)
    long_start_ref[...] = jnp.full((8, LANES), long_start, I32)
    flags = jnp.where(held & ((iota((8, LANES), 1) & 15) >= HALF), 1.0, 0.0).astype(BF)
    source = (iota((rows, 8), 0) >> 2) + REQ_FIRST
    line = jnp.where(source < slots, source, source - slots) >> 3
    here = dot(jnp.where(line == iota((rows, 8), 1), 1.0, 0.0).astype(BF), flags)
    earlier = dot(jnp.where(line > iota((rows, 8), 1), 1.0, 0.0).astype(BF), flags)
    row = iota((rows, LANES), 0)
    col = iota((rows, LANES), 1)
    source = (row >> 2) + REQ_FIRST
    slot = jnp.where(source < slots, source, source - slots) & 7
    valid = jnp.sum(jnp.where((col >> 4) == slot, here, 0.0), axis=1, keepdims=True)
    rank = jnp.sum(earlier + jnp.where((col >> 4) < slot, here, 0.0), axis=1, keepdims=True)
    hit = (valid > 0.5) & (rank.astype(I32) == (col & 7)) & ((row & 3) == (col >> 3))
    chosen = jnp.where(hit, 1.0, 0.0)
    chosen_ref[...] = chosen.astype(BF)
    chosen_t_ref[...] = jnp.transpose(chosen)[:32].astype(BF)
    offsets = own_row(offsets_ref, index, 0)
    starts = column(offsets, 16)
    lengths = column(own_row(lengths_ref, index, 0), 16)
    far = slot_of(owner_of(starts[8:], tokens), slots)
    far = jnp.concatenate([far] * 4, axis=0)
    row = iota((32, rows), 0)
    col = iota((32, rows), 1)
    placed_t_ref[...] = jnp.where(((col >> 2) == far) & ((col & 3) == (row >> 3)), 1.0, 0.0).astype(BF)
    for copy in copies[2:]:
        copy.wait()
    queries = queries_ref[...].astype(F32)[:8]
    fresh = fresh_ref[...].astype(F32)[:8]
    for copy in near_copies:
        copy.wait()
    home_ref[...] = attend(
        queries, fresh[:, :HD], fresh[:, HD:], starts[:8] - index * tokens, lengths[:8],
        long_start, tokens, near_ref,
    )
    weight_copy.wait()


def far_kernel(
    tokens, got_ref, chosen_t_ref, long_start_ref, home_ref, near_ref, weight_ref, weight_hbm, out_ref,
    rest_ref, sems,
):
    upper, rest = weight_ref.shape[0], rest_ref.shape[0]
    (copy,) = fetch((weight_hbm.at[pl.ds(upper, rest)],), (rest_ref,), sems)
    held = dot(chosen_t_ref[...], got_ref[...])
    far = attend(*unpack(held), jnp.max(long_start_ref[0:1, :]), tokens, near_ref)
    attended = jnp.concatenate([home_ref[...], far], axis=0).astype(BF)
    copy.wait()
    mixed = dot(attended[:, :upper], weight_ref[...]) + dot(attended[:, upper:], rest_ref[...])
    columns = out_ref.shape[0]
    low = iota((HALF, LANES), 1) < 64
    for j in range(columns):
        left = j * G * HD // LANES * LANES
        tiles = [mixed[:, left + k * LANES : left + (k + 1) * LANES] for k in range(3)]
        if j % 2 == 0:
            half = jnp.where(low, tiles[2][:8], pltpu.roll(tiles[2][8:], 64, 1))
            full = tiles[:2]
        else:
            half = jnp.where(low, pltpu.roll(tiles[0][:8], 64, 1), tiles[0][8:])
            full = tiles[1:]
        out_ref[(j - TP_FIRST) % columns] = jnp.concatenate([*full, half], axis=0).astype(BF)


def spread_kernel(shares_ref, chosen_ref, home_ref, out_ref):
    mixed = jnp.sum(shares_ref[...].astype(F32), axis=0).astype(BF).astype(F32)
    home_ref[...] = mixed
    stack = jnp.concatenate(
        [mixed[8:16], mixed[24:32], mixed[32:40], jnp.zeros((104, LANES), F32)], axis=0
    )
    out_ref[...] = dot(chosen_ref[...], stack.astype(BF)).astype(BF)


def pick_kernel(placed_t_ref, home_ref, returned_ref, out_ref):
    far = dot(placed_t_ref[...], returned_ref[...])
    home = home_ref[...]
    first = jnp.concatenate([home[0:8], far[0:8]], axis=0)
    second = jnp.concatenate([home[16:24], far[8:16]], axis=0)
    half = jnp.concatenate([home[32:40], pltpu.roll(far[16:24], 64, 1)], axis=0)[:, :64]
    odd = (lax.axis_index("tp") % 2) == 1
    even = jnp.concatenate([first, second, half], axis=1)
    out_ref[...] = jnp.where(odd, jnp.concatenate([half, first, second], axis=1), even).astype(BF)


def exchange(x, axis, first):
    size = lax.axis_size(axis)
    group = [(first + i) % size for i in range(size)]
    return lax.all_to_all(x, axis, 0, 0, axis_index_groups=[group], tiled=True)


def near(x):
    return pltpu.with_memory_space_constraint(x, pltpu.VMEM)


def held_back(x):
    return pltpu.with_memory_space_constraint(x, pltpu.HBM)


def call(kernel, out_shape, *args, far_args=(), scratch=(), in_hbm=False):
    outs = out_shape if in_hbm else [pltpu.VMEM(s.shape, s.dtype) for s in out_shape]
    return pl.pallas_call(
        kernel,
        out_shape=outs,
        in_specs=[NEAR] * len(args) + [ANYWHERE] * len(far_args),
        out_specs=[NEAR] * len(out_shape),
        scratch_shapes=scratch,
        compiler_params=pltpu.CompilerParams(vmem_limit_bytes=16 << 20),
    )(*(near(a) for a in args), *(held_back(a) for a in far_args))


def shards(queries, fresh_kv, kv_cache, out_weight, offsets, lengths):
    devices = lax.axis_size("req")
    columns = lax.axis_size("tp")
    row_count, width = queries.shape
    tokens = kv_cache.shape[2]
    cache = kv_cache.reshape(kv_cache.shape[1:])
    offsets = offsets.reshape(-1, LANES)
    lengths = lengths.reshape(-1, LANES)
    shape = jax.ShapeDtypeStruct
    slots = shape((devices * 4, LANES), BF)
    scratch = lambda x: pltpu.VMEM(x.shape, x.dtype)
    semaphores = pltpu.SemaphoreType.DMA
    inputs = (offsets, lengths, queries, fresh_kv)
    (message,) = call(
        functools.partial(send_kernel, tokens),
        [slots],
        far_args=inputs,
        scratch=[*map(scratch, inputs), semaphores((4,))],
    )
    got = exchange(message.reshape(devices, 4, LANES), "req", REQ_FIRST)
    near_blocks = (tokens - LMAX) // LANES + 1
    upper = out_weight.shape[0] * 4 // 5
    home_near, home_weight, home_out, chosen, chosen_t, placed_t, long_start = call(
        home_kernel,
        [
            shape((2 * HD, near_blocks * LANES + W + LANES), BF),
            shape((upper, out_weight.shape[1]), BF),
            shape((HALF, width), F32),
            slots,
            shape((32, devices * 4), BF),
            shape((32, devices * 4), BF),
            shape((8, LANES), I32),
        ],
        far_args=(*inputs, cache, out_weight),
        scratch=[
            *map(scratch, inputs), semaphores((4,)), semaphores((1,)), semaphores((near_blocks + 1,))
        ],
    )
    (shares,) = call(
        functools.partial(far_kernel, tokens),
        [shape((columns, 40, LANES), BF)],
        got.reshape(devices * 4, LANES), chosen_t, long_start, home_out, home_near, home_weight,
        far_args=(out_weight,),
        scratch=[
            pltpu.VMEM((out_weight.shape[0] - upper, out_weight.shape[1]), BF), semaphores((1,))
        ],
    )
    shares = exchange(shares, "tp", TP_FIRST)
    home, spread = call(spread_kernel, [shape((40, LANES), F32), slots], shares, chosen)
    returned = exchange(spread.reshape(devices, 4, LANES), "req", REQ_FIRST)
    (mixed,) = call(
        pick_kernel,
        [shape((row_count, width), BF)],
        placed_t, home, returned.reshape(devices * 4, LANES),
        in_hbm=True,
    )
    return mixed


def solution(mesh):
    in_specs = (P("req", "tp"), P("req", "tp"), P("tp", None, "req"), P("tp", None), P(), P())
    out_specs = P("req", "tp")
    return jax.shard_map(shards, mesh=mesh, in_specs=in_specs, out_specs=out_specs, check_vma=False)
```

```python
import functools

import jax
import jax.numpy as jnp
from jax import lax
from jax.experimental import pallas as pl
from jax.experimental.pallas import tpu as pltpu
from jax.sharding import PartitionSpec as P

HD = 80
G = 4
W = 4096
LMAX = 8192
LANES = 128
HALF = 8
REQ_FIRST = 52
TP_FIRST = 4
BF = jnp.bfloat16
F32 = jnp.float32
I32 = jnp.int32
NEAR = pl.BlockSpec(memory_space=pltpu.VMEM)
ANYWHERE = pl.BlockSpec(memory_space=pltpu.HBM)


def iota(shape, axis):
    return lax.broadcasted_iota(I32, shape, axis)


def dot(a, b):
    return jnp.dot(a, b, preferred_element_type=F32)


def dot_t(a, b):
    return lax.dot_general(a, b, (((1,), (1,)), ((), ())), preferred_element_type=F32)


def owner_of(offsets, tokens):
    return ((offsets.astype(F32) + 0.5) * (1.0 / tokens)).astype(I32)


def own_row(table_ref, index, shift):
    per_row = LANES // 16
    row = table_ref[pl.ds(index // per_row, 1), :]
    back = (index % per_row) * 16 + shift
    return pltpu.roll(row, (LANES - back) % LANES, 1)


def column(row, count):
    wide = jnp.broadcast_to(row, (count, LANES))
    same = iota((count, LANES), 0) == iota((count, LANES), 1)
    return jnp.sum(jnp.where(same, wide, 0), axis=1, keepdims=True)


def pack(queries, fresh, starts, lengths):
    lane = iota((HALF, LANES), 1)
    meta = jnp.where(lane == 96, 1, 0)
    meta = jnp.where(lane == 97, starts >> 7, meta)
    meta = jnp.where(lane == 98, starts & 127, meta)
    meta = jnp.where(lane == 99, lengths >> 7, meta)
    meta = jnp.where(lane == 100, lengths & 127, meta)
    third = jnp.concatenate([queries[:, 256:], fresh[:, 128:], jnp.zeros((HALF, 32), F32)], axis=1)
    return jnp.concatenate(
        [queries[:, :128], queries[:, 128:256], third + meta.astype(F32), fresh[:, :128]], axis=0
    )


def unpack(stack):
    meta = stack[16:24]
    starts = (meta[:, 97:98] * 128.0 + meta[:, 98:99]).astype(I32)
    lengths = (meta[:, 99:100] * 128.0 + meta[:, 100:101]).astype(I32)
    queries = jnp.concatenate([stack[0:8], stack[8:16], stack[16:24, :64]], axis=1)
    fresh = jnp.concatenate([stack[24:32], stack[16:24, 64:96]], axis=1)
    return queries, fresh[:, :HD], fresh[:, HD:], starts, lengths


def fetch(sources, targets, sems):
    copies = [
        pltpu.make_async_copy(s, t, sems.at[i]) for i, (s, t) in enumerate(zip(sources, targets))
    ]
    for copy in copies:
        copy.start()
    return copies


def slot_of(owners, slots):
    return jnp.where(owners < REQ_FIRST, owners + (slots - REQ_FIRST), owners - REQ_FIRST)


def send_kernel(
    tokens, offsets_hbm, lengths_hbm, queries_hbm, fresh_hbm, out_ref,
    offsets_ref, lengths_ref, queries_ref, fresh_ref, sems,
):
    sources = (offsets_hbm, lengths_hbm, queries_hbm, fresh_hbm)
    for copy in fetch(sources, (offsets_ref, lengths_ref, queries_ref, fresh_ref), sems):
        copy.wait()
    index = lax.axis_index("req")
    rows = out_ref.shape[0]
    offsets = own_row(offsets_ref, index, HALF)
    owners = owner_of(offsets, tokens)
    starts = column(offsets - owners * tokens, HALF)
    lengths = column(own_row(lengths_ref, index, HALF), HALF)
    far = slot_of(owners, rows // 4)
    lane = iota((1, LANES), 1)
    spread = jnp.where(lane < 8, far, 0)
    for k in (1, 2, 3):
        here = (lane >= 8 * k) & (lane < 8 * k + 8)
        spread = spread + jnp.where(here, pltpu.roll(far, 8 * k, 1), 0)
    row = iota((rows, LANES), 0)
    col = iota((rows, LANES), 1)
    hit = ((row >> 2) == jnp.broadcast_to(spread, (rows, LANES))) & ((row & 3) == (col >> 3))
    placed = jnp.where(hit, 1.0, 0.0).astype(BF)
    queries = queries_ref[...].astype(F32)
    fresh = fresh_ref[...].astype(F32)
    stack = pack(queries[8:], fresh[8:], starts, lengths)
    stack = jnp.concatenate([stack, jnp.zeros((96, LANES), F32)], axis=0)
    out_ref[...] = dot(placed, stack.astype(BF)).astype(BF)


def weigh(queries, keys, values, inside, own, own_value):
    scores = jnp.where(inside, dot(queries.astype(BF), keys) * HD ** (-0.5), -jnp.inf)
    highest = jnp.maximum(jnp.max(scores, axis=1, keepdims=True), own)
    weights = jnp.exp(scores - highest)
    own_weight = jnp.exp(own - highest)
    totals = jnp.sum(weights, axis=1, keepdims=True) + own_weight
    summed = dot_t(weights.astype(BF), values) + own_weight.astype(BF).astype(F32) * own_value
    return summed / totals


def places(long_start, tokens):
    before = (long_start + LANES - 1) // LANES
    after = (long_start + LMAX) // LANES
    last = tokens // LANES - 1
    blocks = []
    for i in range((tokens - LMAX) // LANES + 1):
        block = jnp.where(i < before, i, after + i - before)
        blocks.append((pl.multiple_of(jnp.minimum(block, last) * LANES, LANES), block > last))
    first = long_start + (LMAX - W + 1)
    base = jnp.minimum(first // LANES * LANES, tokens - (W + LANES))
    return blocks, first, pl.multiple_of(base, LANES)


def attend(queries, fresh_key, fresh_value, starts, lengths, long_start, tokens, near_ref):
    blocks, first, base = places(long_start, tokens)
    others, span = len(blocks) * LANES, W + LANES
    heads = [queries[:, g * HD : (g + 1) * HD] for g in range(G)]
    own = [jnp.sum(h * fresh_key, axis=1, keepdims=True) * HD ** (-0.5) for h in heads]
    is_long = lengths == LMAX
    long_query = jnp.zeros((8, HD), F32)
    long_own = jnp.zeros((8, 1), F32)
    for g in range(G):
        picked = jnp.sum(jnp.where(is_long, heads[g], 0.0), axis=0, keepdims=True)
        long_query = jnp.where(iota((8, HD), 0) == g, picked, long_query)
        picked_own = jnp.sum(jnp.where(is_long, own[g], 0.0), axis=0, keepdims=True)
        long_own = jnp.where(iota((8, 1), 0) == g, picked_own, long_own)
    long_value = jnp.sum(jnp.where(is_long, fresh_value, 0.0), axis=0, keepdims=True)
    position = base + iota((8, span), 1)
    long_out = weigh(
        long_query,
        near_ref[:HD, others:],
        near_ref[HD : 2 * HD, others:],
        (position >= first) & (position < first + (W - 1)),
        long_own,
        long_value,
    )
    position = jnp.concatenate(
        [jnp.where(spare, -LANES, begin) + iota((1, LANES), 1) for begin, spare in blocks], axis=1
    )
    ends = starts + lengths
    firsts = jnp.maximum(starts, ends - (W - 1))
    ends = jnp.concatenate([ends] * G, axis=0)
    firsts = jnp.concatenate([firsts] * G, axis=0)
    outs = weigh(
        jnp.concatenate(heads, axis=0),
        near_ref[:HD, :others],
        near_ref[HD : 2 * HD, :others],
        (position >= firsts) & (position < ends),
        jnp.concatenate(own, axis=0),
        jnp.concatenate([fresh_value] * G, axis=0),
    )
    count = starts.shape[0]
    return jnp.concatenate(
        [jnp.where(is_long, long_out[g : g + 1], outs[g * count : (g + 1) * count]) for g in range(G)],
        axis=1,
    )


def load_kernel(
    offsets_hbm, lengths_hbm, queries_hbm, fresh_hbm, cache_hbm, weight_hbm,
    near_ref, weight_ref, home_queries_ref, home_fresh_ref, numbers_ref, chosen_ref, chosen_t_ref, placed_t_ref,
    offsets_ref, lengths_ref, queries_ref, fresh_ref, sems, weight_sems, near_sems,
):
    sources = (offsets_hbm, lengths_hbm, queries_hbm, fresh_hbm)
    copies = fetch(sources, (offsets_ref, lengths_ref, queries_ref, fresh_ref), sems)
    weight_rows = pl.ds(0, weight_ref.shape[0])
    (weight_copy,) = fetch((weight_hbm.at[weight_rows],), (weight_ref,), weight_sems)
    for copy in copies[:2]:
        copy.wait()
    index = lax.axis_index("req")
    tokens = cache_hbm.shape[1]
    rows = chosen_ref.shape[0]
    slots = rows // 4
    offsets = offsets_ref[...]
    held = owner_of(offsets, tokens) == index
    long_start = jnp.sum(jnp.where(held & (lengths_ref[...] == LMAX), offsets, 0)) - index * tokens
    blocks, _, base = places(long_start, tokens)
    sources = [cache_hbm.at[:, pl.ds(begin, LANES)] for begin, _ in blocks]
    targets = [near_ref.at[:, pl.ds(i * LANES, LANES)] for i in range(len(blocks))]
    sources.append(cache_hbm.at[:, pl.ds(base, W + LANES)])
    targets.append(near_ref.at[:, pl.ds(len(blocks) * LANES, W + LANES)])
    near_copies = fetch(sources, targets, near_sems)
    flags = jnp.where(held & ((iota((8, LANES), 1) & 15) >= HALF), 1.0, 0.0).astype(BF)
    source = (iota((rows, 8), 0) >> 2) + REQ_FIRST
    line = jnp.where(source < slots, source, source - slots) >> 3
    here = dot(jnp.where(line == iota((rows, 8), 1), 1.0, 0.0).astype(BF), flags)
    earlier = dot(jnp.where(line > iota((rows, 8), 1), 1.0, 0.0).astype(BF), flags)
    row = iota((rows, LANES), 0)
    col = iota((rows, LANES), 1)
    source = (row >> 2) + REQ_FIRST
    slot = jnp.where(source < slots, source, source - slots) & 7
    valid = jnp.sum(jnp.where((col >> 4) == slot, here, 0.0), axis=1, keepdims=True)
    rank = jnp.sum(earlier + jnp.where((col >> 4) < slot, here, 0.0), axis=1, keepdims=True)
    hit = (valid > 0.5) & (rank.astype(I32) == (col & 7)) & ((row & 3) == (col >> 3))
    chosen = jnp.where(hit, 1.0, 0.0)
    chosen_ref[...] = chosen.astype(BF)
    chosen_t_ref[...] = jnp.transpose(chosen)[:32].astype(BF)
    offsets = own_row(offsets_ref, index, 0)
    starts = column(offsets, 16)
    lengths = column(own_row(lengths_ref, index, 0), 16)
    far = slot_of(owner_of(starts[8:], tokens), slots)
    far = jnp.concatenate([far] * 4, axis=0)
    row = iota((32, rows), 0)
    col = iota((32, rows), 1)
    placed_t_ref[...] = jnp.where(((col >> 2) == far) & ((col & 3) == (row >> 3)), 1.0, 0.0).astype(BF)
    numbers_ref[0:8] = jnp.broadcast_to(starts[:8] - index * tokens, (8, LANES))
    numbers_ref[8:16] = jnp.broadcast_to(lengths[:8], (8, LANES))
    numbers_ref[16:24] = jnp.full((8, LANES), long_start, I32)
    for copy in copies[2:]:
        copy.wait()
    home_queries_ref[...] = queries_ref[...].astype(F32)[:8]
    home_fresh_ref[...] = fresh_ref[...].astype(F32)[:8]
    for copy in near_copies:
        copy.wait()
    weight_copy.wait()


def attend_kernel(
    tokens, got_ref, chosen_t_ref, home_queries_ref, home_fresh_ref, numbers_ref, near_ref, weight_ref,
    weight_hbm, out_ref, rest_ref, sems,
):
    upper, rest = weight_ref.shape[0], rest_ref.shape[0]
    (copy,) = fetch((weight_hbm.at[pl.ds(upper, rest)],), (rest_ref,), sems)
    numbers = numbers_ref[...]
    long_start = jnp.max(numbers[16:17])
    far = unpack(dot(chosen_t_ref[...], got_ref[...]))
    home_fresh = home_fresh_ref[...]
    home = (
        home_queries_ref[...], home_fresh[:, :HD], home_fresh[:, HD:], numbers[:8, :1], numbers[8:16, :1]
    )
    both = [jnp.concatenate(pair, axis=0) for pair in zip(home, far)]
    attended = attend(*both, long_start, tokens, near_ref).astype(BF)
    mixed = dot(attended[:, :upper], weight_ref[...])
    copy.wait()
    mixed = mixed + dot(attended[:, upper:], rest_ref[...])
    columns = out_ref.shape[0]
    low = iota((HALF, LANES), 1) < 64
    for j in range(columns):
        left = j * G * HD // LANES * LANES
        tiles = [mixed[:, left + k * LANES : left + (k + 1) * LANES] for k in range(3)]
        if j % 2 == 0:
            half = jnp.where(low, tiles[2][:8], pltpu.roll(tiles[2][8:], 64, 1))
            full = tiles[:2]
        else:
            half = jnp.where(low, pltpu.roll(tiles[0][:8], 64, 1), tiles[0][8:])
            full = tiles[1:]
        out_ref[(j - TP_FIRST) % columns] = jnp.concatenate([*full, half], axis=0).astype(BF)


def spread_kernel(shares_ref, chosen_ref, home_ref, out_ref):
    mixed = jnp.sum(shares_ref[...].astype(F32), axis=0).astype(BF).astype(F32)
    home_ref[...] = mixed
    stack = jnp.concatenate(
        [mixed[8:16], mixed[24:32], mixed[32:40], jnp.zeros((104, LANES), F32)], axis=0
    )
    out_ref[...] = dot(chosen_ref[...], stack.astype(BF)).astype(BF)


def pick_kernel(placed_t_ref, home_ref, returned_ref, out_ref):
    far = dot(placed_t_ref[...], returned_ref[...])
    home = home_ref[...]
    first = jnp.concatenate([home[0:8], far[0:8]], axis=0)
    second = jnp.concatenate([home[16:24], far[8:16]], axis=0)
    half = jnp.concatenate([home[32:40], pltpu.roll(far[16:24], 64, 1)], axis=0)[:, :64]
    odd = (lax.axis_index("tp") % 2) == 1
    even = jnp.concatenate([first, second, half], axis=1)
    out_ref[...] = jnp.where(odd, jnp.concatenate([half, first, second], axis=1), even).astype(BF)


def exchange(x, axis, first):
    size = lax.axis_size(axis)
    group = [(first + i) % size for i in range(size)]
    return lax.all_to_all(x, axis, 0, 0, axis_index_groups=[group], tiled=True)


def in_vmem(x):
    return pltpu.with_memory_space_constraint(x, pltpu.VMEM)


def in_hbm(x):
    return pltpu.with_memory_space_constraint(x, pltpu.HBM)


def call(kernel, out_shape, *args, far_args=(), scratch=(), result_in_hbm=False):
    outs = out_shape if result_in_hbm else [pltpu.VMEM(s.shape, s.dtype) for s in out_shape]
    return pl.pallas_call(
        kernel,
        out_shape=outs,
        in_specs=[NEAR] * len(args) + [ANYWHERE] * len(far_args),
        out_specs=[NEAR] * len(out_shape),
        scratch_shapes=scratch,
        compiler_params=pltpu.CompilerParams(vmem_limit_bytes=16 << 20),
    )(*(in_vmem(a) for a in args), *(in_hbm(a) for a in far_args))


def shards(queries, fresh_kv, kv_cache, out_weight, offsets, lengths):
    devices = lax.axis_size("req")
    columns = lax.axis_size("tp")
    row_count, width = queries.shape
    tokens = kv_cache.shape[2]
    cache = kv_cache.reshape(kv_cache.shape[1:])
    offsets = offsets.reshape(-1, LANES)
    lengths = lengths.reshape(-1, LANES)
    shape = jax.ShapeDtypeStruct
    slots = shape((devices * 4, LANES), BF)
    scratch = lambda x: pltpu.VMEM(x.shape, x.dtype)
    semaphores = pltpu.SemaphoreType.DMA
    inputs = (offsets, lengths, queries, fresh_kv)
    (message,) = call(
        functools.partial(send_kernel, tokens),
        [slots],
        far_args=inputs,
        scratch=[*map(scratch, inputs), semaphores((4,))],
    )
    got = exchange(message.reshape(devices, 4, LANES), "req", REQ_FIRST)
    near_blocks = (tokens - LMAX) // LANES + 1
    upper = out_weight.shape[0] * 4 // 5
    near, weight, home_queries, home_fresh, numbers, chosen, chosen_t, placed_t = call(
        load_kernel,
        [
            shape((2 * HD, near_blocks * LANES + W + LANES), BF),
            shape((upper, out_weight.shape[1]), BF),
            shape((HALF, width), F32),
            shape((HALF, fresh_kv.shape[1]), F32),
            shape((3 * HALF, LANES), I32),
            slots,
            shape((32, devices * 4), BF),
            shape((32, devices * 4), BF),
        ],
        far_args=(*inputs, cache, out_weight),
        scratch=[
            *map(scratch, inputs), semaphores((4,)), semaphores((1,)), semaphores((near_blocks + 1,))
        ],
    )
    (shares,) = call(
        functools.partial(attend_kernel, tokens),
        [shape((columns, 40, LANES), BF)],
        got.reshape(devices * 4, LANES), chosen_t, home_queries, home_fresh, numbers, near, weight,
        far_args=(out_weight,),
        scratch=[
            pltpu.VMEM((out_weight.shape[0] - upper, out_weight.shape[1]), BF), semaphores((1,))
        ],
    )
    shares = exchange(shares, "tp", TP_FIRST)
    home, spread = call(spread_kernel, [shape((40, LANES), F32), slots], shares, chosen)
    returned = exchange(spread.reshape(devices, 4, LANES), "req", REQ_FIRST)
    (mixed,) = call(
        pick_kernel,
        [shape((row_count, width), BF)],
        placed_t, home, returned.reshape(devices * 4, LANES),
        result_in_hbm=True,
    )
    return mixed


def solution(mesh):
    in_specs = (P("req", "tp"), P("req", "tp"), P("tp", None, "req"), P("tp", None), P(), P())
    out_specs = P("req", "tp")
    return jax.shard_map(shards, mesh=mesh, in_specs=in_specs, out_specs=out_specs, check_vma=False)
```

```python
import functools

import jax
import jax.numpy as jnp
import numpy as np
from jax import lax
from jax.experimental import pallas as pl
from jax.experimental.pallas import tpu as pltpu
from jax.sharding import PartitionSpec as P

HD = 80
G = 4
W = 4096
LMAX = 8192
LANES = 128
HALF = 8
FIRST_Z, FIRST_X, FIRST_CORE = 6, 2, 1
TP_FIRST = 4
BF = jnp.bfloat16
F32 = jnp.float32
I32 = jnp.int32
NEAR = pl.BlockSpec(memory_space=pltpu.VMEM)
ANYWHERE = pl.BlockSpec(memory_space=pltpu.HBM)


def iota(shape, axis):
    return lax.broadcasted_iota(I32, shape, axis)


def dot(a, b):
    return jnp.dot(a, b, preferred_element_type=F32)


def dot_t(a, b):
    return lax.dot_general(a, b, (((1,), (1,)), ((), ())), preferred_element_type=F32)


def owner_of(offsets, tokens):
    return ((offsets.astype(F32) + 0.5) * (1.0 / tokens)).astype(I32)


def own_row(table_ref, index, shift):
    per_row = LANES // 16
    row = table_ref[pl.ds(index // per_row, 1), :]
    back = (index % per_row) * 16 + shift
    return pltpu.roll(row, (LANES - back) % LANES, 1)


def column(row, count):
    wide = jnp.broadcast_to(row, (count, LANES))
    same = iota((count, LANES), 0) == iota((count, LANES), 1)
    return jnp.sum(jnp.where(same, wide, 0), axis=1, keepdims=True)


def pack(queries, fresh, starts, lengths):
    lane = iota((HALF, LANES), 1)
    meta = jnp.where(lane == 96, 1, 0)
    meta = jnp.where(lane == 97, starts >> 7, meta)
    meta = jnp.where(lane == 98, starts & 127, meta)
    meta = jnp.where(lane == 99, lengths >> 7, meta)
    meta = jnp.where(lane == 100, lengths & 127, meta)
    third = jnp.concatenate([queries[:, 256:], fresh[:, 128:], jnp.zeros((HALF, 32), F32)], axis=1)
    return jnp.concatenate(
        [queries[:, :128], queries[:, 128:256], third + meta.astype(F32), fresh[:, :128]], axis=0
    )


def unpack(stack):
    meta = stack[16:24]
    starts = (meta[:, 97:98] * 128.0 + meta[:, 98:99]).astype(I32)
    lengths = (meta[:, 99:100] * 128.0 + meta[:, 100:101]).astype(I32)
    queries = jnp.concatenate([stack[0:8], stack[8:16], stack[16:24, :64]], axis=1)
    fresh = jnp.concatenate([stack[24:32], stack[16:24, 64:96]], axis=1)
    return queries, fresh[:, :HD], fresh[:, HD:], starts, lengths


def fetch(sources, targets, sems):
    copies = [
        pltpu.make_async_copy(s, t, sems.at[i]) for i, (s, t) in enumerate(zip(sources, targets))
    ]
    for copy in copies:
        copy.start()
    return copies


def source_of(slot, where=jnp.where):
    place = (slot + 63) & 63
    ring_z, ring_x = place >> 3, (place >> 1) & 3
    z = FIRST_Z + 4 + where((ring_z & 1) == 1, -((ring_z + 1) >> 1), ring_z >> 1)
    x = FIRST_X + 2 + where((ring_x & 1) == 1, -((ring_x + 1) >> 1), ring_x >> 1)
    return (z & 7) * 8 + (x & 3) * 2 + ((FIRST_CORE + 1 + place) & 1)


def slot_of(member):
    z = (((member >> 3) - FIRST_Z) & 7) - 4
    x = ((((member >> 1) & 3) - FIRST_X) & 3) - 2
    ring_z = jnp.where(z < 0, -2 * z - 1, 2 * z)
    ring_x = jnp.where(x < 0, -2 * x - 1, 2 * x)
    core = (member + FIRST_CORE + 1) & 1
    return (ring_z * 8 + ring_x * 2 + core + 1) & 63


def send_kernel(
    tokens, offsets_hbm, lengths_hbm, queries_hbm, fresh_hbm, out_ref,
    offsets_ref, lengths_ref, queries_ref, fresh_ref, sems,
):
    sources = (offsets_hbm, lengths_hbm, queries_hbm, fresh_hbm)
    for copy in fetch(sources, (offsets_ref, lengths_ref, queries_ref, fresh_ref), sems):
        copy.wait()
    index = lax.axis_index("req")
    rows = out_ref.shape[0]
    offsets = own_row(offsets_ref, index, HALF)
    owners = owner_of(offsets, tokens)
    starts = column(offsets - owners * tokens, HALF)
    lengths = column(own_row(lengths_ref, index, HALF), HALF)
    far = slot_of(owners)
    lane = iota((1, LANES), 1)
    spread = jnp.where(lane < 8, far, 0)
    for k in (1, 2, 3):
        here = (lane >= 8 * k) & (lane < 8 * k + 8)
        spread = spread + jnp.where(here, pltpu.roll(far, 8 * k, 1), 0)
    row = iota((rows, LANES), 0)
    col = iota((rows, LANES), 1)
    hit = ((row >> 2) == jnp.broadcast_to(spread, (rows, LANES))) & ((row & 3) == (col >> 3))
    placed = jnp.where(hit, 1.0, 0.0).astype(BF)
    queries = queries_ref[...].astype(F32)
    fresh = fresh_ref[...].astype(F32)
    stack = pack(queries[8:], fresh[8:], starts, lengths)
    stack = jnp.concatenate([stack, jnp.zeros((96, LANES), F32)], axis=0)
    out_ref[...] = dot(placed, stack.astype(BF)).astype(BF)


def weigh(queries, keys, values, inside, own, own_value):
    scores = jnp.where(inside, dot(queries.astype(BF), keys) * HD ** (-0.5), -jnp.inf)
    highest = jnp.maximum(jnp.max(scores, axis=1, keepdims=True), own)
    weights = jnp.exp(scores - highest)
    own_weight = jnp.exp(own - highest)
    totals = jnp.sum(weights, axis=1, keepdims=True) + own_weight
    summed = dot_t(weights.astype(BF), values) + own_weight.astype(BF).astype(F32) * own_value
    return summed / totals


def places(long_start, tokens):
    before = (long_start + LANES - 1) // LANES
    after = (long_start + LMAX) // LANES
    last = tokens // LANES - 1
    blocks = []
    for i in range((tokens - LMAX) // LANES + 1):
        block = jnp.where(i < before, i, after + i - before)
        blocks.append((pl.multiple_of(jnp.minimum(block, last) * LANES, LANES), block > last))
    first = long_start + (LMAX - W + 1)
    base = jnp.minimum(first // LANES * LANES, tokens - (W + LANES))
    return blocks, first, pl.multiple_of(base, LANES)


def attend(queries, fresh_key, fresh_value, starts, lengths, long_start, tokens, near_ref):
    blocks, first, base = places(long_start, tokens)
    others, span = len(blocks) * LANES, W + LANES
    heads = [queries[:, g * HD : (g + 1) * HD] for g in range(G)]
    own = [jnp.sum(h * fresh_key, axis=1, keepdims=True) * HD ** (-0.5) for h in heads]
    is_long = lengths == LMAX
    long_query = jnp.zeros((8, HD), F32)
    long_own = jnp.zeros((8, 1), F32)
    for g in range(G):
        picked = jnp.sum(jnp.where(is_long, heads[g], 0.0), axis=0, keepdims=True)
        long_query = jnp.where(iota((8, HD), 0) == g, picked, long_query)
        picked_own = jnp.sum(jnp.where(is_long, own[g], 0.0), axis=0, keepdims=True)
        long_own = jnp.where(iota((8, 1), 0) == g, picked_own, long_own)
    long_value = jnp.sum(jnp.where(is_long, fresh_value, 0.0), axis=0, keepdims=True)
    position = base + iota((8, span), 1)
    long_out = weigh(
        long_query,
        near_ref[:HD, others:],
        near_ref[HD : 2 * HD, others:],
        (position >= first) & (position < first + (W - 1)),
        long_own,
        long_value,
    )
    position = jnp.concatenate(
        [jnp.where(spare, -LANES, begin) + iota((1, LANES), 1) for begin, spare in blocks], axis=1
    )
    ends = starts + lengths
    firsts = jnp.maximum(starts, ends - (W - 1))
    ends = jnp.concatenate([ends] * G, axis=0)
    firsts = jnp.concatenate([firsts] * G, axis=0)
    outs = weigh(
        jnp.concatenate(heads, axis=0),
        near_ref[:HD, :others],
        near_ref[HD : 2 * HD, :others],
        (position >= firsts) & (position < ends),
        jnp.concatenate(own, axis=0),
        jnp.concatenate([fresh_value] * G, axis=0),
    )
    count = starts.shape[0]
    return jnp.concatenate(
        [jnp.where(is_long, long_out[g : g + 1], outs[g * count : (g + 1) * count]) for g in range(G)],
        axis=1,
    )


def load_kernel(
    offsets_hbm, lengths_hbm, queries_hbm, fresh_hbm, cache_hbm, weight_hbm,
    near_ref, weight_ref, home_queries_ref, home_fresh_ref, numbers_ref, chosen_ref, chosen_t_ref, placed_t_ref,
    offsets_ref, lengths_ref, queries_ref, fresh_ref, sems, weight_sems, near_sems,
):
    sources = (offsets_hbm, lengths_hbm, queries_hbm, fresh_hbm)
    copies = fetch(sources, (offsets_ref, lengths_ref, queries_ref, fresh_ref), sems)
    weight_rows = pl.ds(0, weight_ref.shape[0])
    (weight_copy,) = fetch((weight_hbm.at[weight_rows],), (weight_ref,), weight_sems)
    for copy in copies[:2]:
        copy.wait()
    index = lax.axis_index("req")
    tokens = cache_hbm.shape[1]
    rows = chosen_ref.shape[0]
    offsets = offsets_ref[...]
    held = owner_of(offsets, tokens) == index
    long_start = jnp.sum(jnp.where(held & (lengths_ref[...] == LMAX), offsets, 0)) - index * tokens
    blocks, _, base = places(long_start, tokens)
    sources = [cache_hbm.at[:, pl.ds(begin, LANES)] for begin, _ in blocks]
    targets = [near_ref.at[:, pl.ds(i * LANES, LANES)] for i in range(len(blocks))]
    sources.append(cache_hbm.at[:, pl.ds(base, W + LANES)])
    targets.append(near_ref.at[:, pl.ds(len(blocks) * LANES, W + LANES)])
    near_copies = fetch(sources, targets, near_sems)
    flags = jnp.where(held & ((iota((8, LANES), 1) & 15) >= HALF), 1.0, 0.0).astype(BF)
    line = source_of(iota((rows, 8), 0) >> 2) >> 3
    here = dot(jnp.where(line == iota((rows, 8), 1), 1.0, 0.0).astype(BF), flags)
    earlier = dot(jnp.where(line > iota((rows, 8), 1), 1.0, 0.0).astype(BF), flags)
    row = iota((rows, LANES), 0)
    col = iota((rows, LANES), 1)
    slot = source_of(row >> 2) & 7
    valid = jnp.sum(jnp.where((col >> 4) == slot, here, 0.0), axis=1, keepdims=True)
    rank = jnp.sum(earlier + jnp.where((col >> 4) < slot, here, 0.0), axis=1, keepdims=True)
    hit = (valid > 0.5) & (rank.astype(I32) == (col & 7)) & ((row & 3) == (col >> 3))
    chosen = jnp.where(hit, 1.0, 0.0)
    chosen_ref[...] = chosen.astype(BF)
    chosen_t_ref[...] = jnp.transpose(chosen)[:32].astype(BF)
    offsets = own_row(offsets_ref, index, 0)
    starts = column(offsets, 16)
    lengths = column(own_row(lengths_ref, index, 0), 16)
    far = slot_of(owner_of(starts[8:], tokens))
    far = jnp.concatenate([far] * 4, axis=0)
    row = iota((32, rows), 0)
    col = iota((32, rows), 1)
    placed_t_ref[...] = jnp.where(((col >> 2) == far) & ((col & 3) == (row >> 3)), 1.0, 0.0).astype(BF)
    numbers_ref[0:8] = jnp.broadcast_to(starts[:8] - index * tokens, (8, LANES))
    numbers_ref[8:16] = jnp.broadcast_to(lengths[:8], (8, LANES))
    numbers_ref[16:24] = jnp.full((8, LANES), long_start, I32)
    for copy in copies[2:]:
        copy.wait()
    home_queries_ref[...] = queries_ref[...].astype(F32)[:8]
    home_fresh_ref[...] = fresh_ref[...].astype(F32)[:8]
    for copy in near_copies:
        copy.wait()
    weight_copy.wait()


def attend_kernel(
    tokens, got_ref, chosen_t_ref, home_queries_ref, home_fresh_ref, numbers_ref, near_ref, weight_ref,
    weight_hbm, out_ref, rest_ref, sems,
):
    upper, rest = weight_ref.shape[0], rest_ref.shape[0]
    (copy,) = fetch((weight_hbm.at[pl.ds(upper, rest)],), (rest_ref,), sems)
    numbers = numbers_ref[...]
    long_start = jnp.max(numbers[16:17])
    far = unpack(dot(chosen_t_ref[...], got_ref[...]))
    home_fresh = home_fresh_ref[...]
    home = (
        home_queries_ref[...], home_fresh[:, :HD], home_fresh[:, HD:], numbers[:8, :1], numbers[8:16, :1]
    )
    both = [jnp.concatenate(pair, axis=0) for pair in zip(home, far)]
    attended = attend(*both, long_start, tokens, near_ref).astype(BF)
    mixed = dot(attended[:, :upper], weight_ref[...])
    copy.wait()
    mixed = mixed + dot(attended[:, upper:], rest_ref[...])
    columns = out_ref.shape[0]
    low = iota((HALF, LANES), 1) < 64
    for j in range(columns):
        left = j * G * HD // LANES * LANES
        tiles = [mixed[:, left + k * LANES : left + (k + 1) * LANES] for k in range(3)]
        if j % 2 == 0:
            half = jnp.where(low, tiles[2][:8], pltpu.roll(tiles[2][8:], 64, 1))
            full = tiles[:2]
        else:
            half = jnp.where(low, pltpu.roll(tiles[0][:8], 64, 1), tiles[0][8:])
            full = tiles[1:]
        out_ref[(j - TP_FIRST) % columns] = jnp.concatenate([*full, half], axis=0).astype(BF)


def spread_kernel(shares_ref, chosen_ref, home_ref, out_ref):
    mixed = jnp.sum(shares_ref[...].astype(F32), axis=0).astype(BF).astype(F32)
    home_ref[...] = mixed
    stack = jnp.concatenate(
        [mixed[8:16], mixed[24:32], mixed[32:40], jnp.zeros((104, LANES), F32)], axis=0
    )
    out_ref[...] = dot(chosen_ref[...], stack.astype(BF)).astype(BF)


def pick_kernel(placed_t_ref, home_ref, returned_ref, out_ref):
    far = dot(placed_t_ref[...], returned_ref[...])
    home = home_ref[...]
    first = jnp.concatenate([home[0:8], far[0:8]], axis=0)
    second = jnp.concatenate([home[16:24], far[8:16]], axis=0)
    half = jnp.concatenate([home[32:40], pltpu.roll(far[16:24], 64, 1)], axis=0)[:, :64]
    odd = (lax.axis_index("tp") % 2) == 1
    even = jnp.concatenate([first, second, half], axis=1)
    out_ref[...] = jnp.where(odd, jnp.concatenate([half, first, second], axis=1), even).astype(BF)


def exchange(x, axis, group):
    return lax.all_to_all(x, axis, 0, 0, axis_index_groups=[group], tiled=True)


def in_vmem(x):
    return pltpu.with_memory_space_constraint(x, pltpu.VMEM)


def in_hbm(x):
    return pltpu.with_memory_space_constraint(x, pltpu.HBM)


def call(kernel, out_shape, *args, far_args=(), scratch=(), result_in_hbm=False):
    outs = out_shape if result_in_hbm else [pltpu.VMEM(s.shape, s.dtype) for s in out_shape]
    return pl.pallas_call(
        kernel,
        out_shape=outs,
        in_specs=[NEAR] * len(args) + [ANYWHERE] * len(far_args),
        out_specs=[NEAR] * len(out_shape),
        scratch_shapes=scratch,
        compiler_params=pltpu.CompilerParams(vmem_limit_bytes=16 << 20),
    )(*(in_vmem(a) for a in args), *(in_hbm(a) for a in far_args))


def shards(queries, fresh_kv, kv_cache, out_weight, offsets, lengths):
    devices = lax.axis_size("req")
    columns = lax.axis_size("tp")
    req_group = [int(i) for i in source_of(np.arange(devices), np.where)]
    row_count, width = queries.shape
    tokens = kv_cache.shape[2]
    cache = kv_cache.reshape(kv_cache.shape[1:])
    offsets = offsets.reshape(-1, LANES)
    lengths = lengths.reshape(-1, LANES)
    shape = jax.ShapeDtypeStruct
    slots = shape((devices * 4, LANES), BF)
    scratch = lambda x: pltpu.VMEM(x.shape, x.dtype)
    semaphores = pltpu.SemaphoreType.DMA
    inputs = (offsets, lengths, queries, fresh_kv)
    (message,) = call(
        functools.partial(send_kernel, tokens),
        [slots],
        far_args=inputs,
        scratch=[*map(scratch, inputs), semaphores((4,))],
    )
    got = exchange(message.reshape(devices, 4, LANES), "req", req_group)
    near_blocks = (tokens - LMAX) // LANES + 1
    upper = out_weight.shape[0] * 4 // 5
    near, weight, home_queries, home_fresh, numbers, chosen, chosen_t, placed_t = call(
        load_kernel,
        [
            shape((2 * HD, near_blocks * LANES + W + LANES), BF),
            shape((upper, out_weight.shape[1]), BF),
            shape((HALF, width), F32),
            shape((HALF, fresh_kv.shape[1]), F32),
            shape((3 * HALF, LANES), I32),
            slots,
            shape((32, devices * 4), BF),
            shape((32, devices * 4), BF),
        ],
        far_args=(*inputs, cache, out_weight),
        scratch=[
            *map(scratch, inputs), semaphores((4,)), semaphores((1,)), semaphores((near_blocks + 1,))
        ],
    )
    (shares,) = call(
        functools.partial(attend_kernel, tokens),
        [shape((columns, 40, LANES), BF)],
        got.reshape(devices * 4, LANES), chosen_t, home_queries, home_fresh, numbers, near, weight,
        far_args=(out_weight,),
        scratch=[
            pltpu.VMEM((out_weight.shape[0] - upper, out_weight.shape[1]), BF), semaphores((1,))
        ],
    )
    shares = exchange(shares, "tp", [(TP_FIRST + i) % columns for i in range(columns)])
    home, spread = call(spread_kernel, [shape((40, LANES), F32), slots], shares, chosen)
    returned = exchange(spread.reshape(devices, 4, LANES), "req", req_group)
    (mixed,) = call(
        pick_kernel,
        [shape((row_count, width), BF)],
        placed_t, home, returned.reshape(devices * 4, LANES),
        result_in_hbm=True,
    )
    return mixed


def solution(mesh):
    in_specs = (P("req", "tp"), P("req", "tp"), P("tp", None, "req"), P("tp", None), P(), P())
    out_specs = P("req", "tp")
    return jax.shard_map(shards, mesh=mesh, in_specs=in_specs, out_specs=out_specs, check_vma=False)
```

```python
import functools

import jax
import jax.numpy as jnp
import numpy as np
from jax import lax
from jax.experimental import pallas as pl
from jax.experimental.pallas import tpu as pltpu
from jax.sharding import PartitionSpec as P

HD = 80
G = 4
W = 4096
LMAX = 8192
LANES = 128
HALF = 8
FIRST_Z, FIRST_X, FIRST_CORE = 6, 2, 1
TP_FIRST = 4
BF = jnp.bfloat16
F32 = jnp.float32
I32 = jnp.int32
NEAR = pl.BlockSpec(memory_space=pltpu.VMEM)
ANYWHERE = pl.BlockSpec(memory_space=pltpu.HBM)


def iota(shape, axis):
    return lax.broadcasted_iota(I32, shape, axis)


def dot(a, b):
    return jnp.dot(a, b, preferred_element_type=F32)


def dot_t(a, b):
    return lax.dot_general(a, b, (((1,), (1,)), ((), ())), preferred_element_type=F32)


def owner_of(offsets, tokens):
    return ((offsets.astype(F32) + 0.5) * (1.0 / tokens)).astype(I32)


def own_row(table_ref, index, shift):
    per_row = LANES // 16
    row = table_ref[pl.ds(index // per_row, 1), :]
    back = (index % per_row) * 16 + shift
    return pltpu.roll(row, (LANES - back) % LANES, 1)


def column(row, count):
    wide = jnp.broadcast_to(row, (count, LANES))
    same = iota((count, LANES), 0) == iota((count, LANES), 1)
    return jnp.sum(jnp.where(same, wide, 0), axis=1, keepdims=True)


def pack(queries, fresh, starts, lengths):
    lane = iota((HALF, LANES), 1)
    meta = jnp.where(lane == 96, 1, 0)
    meta = jnp.where(lane == 97, starts >> 7, meta)
    meta = jnp.where(lane == 98, starts & 127, meta)
    meta = jnp.where(lane == 99, lengths >> 7, meta)
    meta = jnp.where(lane == 100, lengths & 127, meta)
    third = jnp.concatenate([queries[:, 256:], fresh[:, 128:], jnp.zeros((HALF, 32), F32)], axis=1)
    return jnp.concatenate(
        [queries[:, :128], queries[:, 128:256], third + meta.astype(F32), fresh[:, :128]], axis=0
    )


def unpack(stack):
    meta = stack[16:24]
    starts = (meta[:, 97:98] * 128.0 + meta[:, 98:99]).astype(I32)
    lengths = (meta[:, 99:100] * 128.0 + meta[:, 100:101]).astype(I32)
    queries = jnp.concatenate([stack[0:8], stack[8:16], stack[16:24, :64]], axis=1)
    fresh = jnp.concatenate([stack[24:32], stack[16:24, 64:96]], axis=1)
    return queries, fresh[:, :HD], fresh[:, HD:], starts, lengths


def fetch(sources, targets, sems):
    copies = [
        pltpu.make_async_copy(s, t, sems.at[i]) for i, (s, t) in enumerate(zip(sources, targets))
    ]
    for copy in copies:
        copy.start()
    return copies


def source_of(slot, where=jnp.where):
    place = (slot + 63) & 63
    ring_z, ring_x = place >> 3, (place >> 1) & 3
    z = FIRST_Z + 4 + where((ring_z & 1) == 1, -((ring_z + 1) >> 1), ring_z >> 1)
    x = FIRST_X + 2 + where((ring_x & 1) == 1, -((ring_x + 1) >> 1), ring_x >> 1)
    return (z & 7) * 8 + (x & 3) * 2 + ((FIRST_CORE + 1 + place) & 1)


def slot_of(member):
    z = (((member >> 3) - FIRST_Z) & 7) - 4
    x = ((((member >> 1) & 3) - FIRST_X) & 3) - 2
    ring_z = jnp.where(z < 0, -2 * z - 1, 2 * z)
    ring_x = jnp.where(x < 0, -2 * x - 1, 2 * x)
    core = (member + FIRST_CORE + 1) & 1
    return (ring_z * 8 + ring_x * 2 + core + 1) & 63


def send_kernel(
    tokens, offsets_hbm, lengths_hbm, queries_hbm, fresh_hbm, out_ref,
    offsets_ref, lengths_ref, queries_ref, fresh_ref, sems,
):
    sources = (offsets_hbm, lengths_hbm, queries_hbm, fresh_hbm)
    for copy in fetch(sources, (offsets_ref, lengths_ref, queries_ref, fresh_ref), sems):
        copy.wait()
    index = lax.axis_index("req")
    rows = out_ref.shape[0]
    offsets = own_row(offsets_ref, index, HALF)
    owners = owner_of(offsets, tokens)
    starts = column(offsets - owners * tokens, HALF)
    far = slot_of(owners)
    lane = iota((1, LANES), 1)
    spread = jnp.where(lane < 8, far, 0)
    for k in (1, 2, 3):
        here = (lane >= 8 * k) & (lane < 8 * k + 8)
        spread = spread + jnp.where(here, pltpu.roll(far, 8 * k, 1), 0)
    row = iota((rows, LANES), 0)
    col = iota((rows, LANES), 1)
    hit = ((row >> 2) == jnp.broadcast_to(spread, (rows, LANES))) & ((row & 3) == (col >> 3))
    placed = jnp.where(hit, 1.0, 0.0).astype(BF)
    lengths = column(own_row(lengths_ref, index, HALF), HALF)
    queries = queries_ref[...].astype(F32)
    fresh = fresh_ref[...].astype(F32)
    stack = pack(queries[8:], fresh[8:], starts, lengths)
    stack = jnp.concatenate([stack, jnp.zeros((96, LANES), F32)], axis=0)
    out_ref[...] = dot(placed, stack.astype(BF)).astype(BF)


def weigh(queries, keys, values, inside, own, own_value):
    scores = jnp.where(inside, dot(queries.astype(BF), keys) * HD ** (-0.5), -jnp.inf)
    highest = jnp.maximum(jnp.max(scores, axis=1, keepdims=True), own)
    weights = jnp.exp(scores - highest)
    own_weight = jnp.exp(own - highest)
    totals = jnp.sum(weights, axis=1, keepdims=True) + own_weight
    summed = dot_t(weights.astype(BF), values) + own_weight.astype(BF).astype(F32) * own_value
    return summed / totals


def places(long_start, tokens):
    before = (long_start + LANES - 1) // LANES
    after = (long_start + LMAX) // LANES
    last = tokens // LANES - 1
    blocks = []
    for i in range((tokens - LMAX) // LANES + 1):
        block = jnp.where(i < before, i, after + i - before)
        blocks.append((pl.multiple_of(jnp.minimum(block, last) * LANES, LANES), block > last))
    first = long_start + (LMAX - W + 1)
    base = jnp.minimum(first // LANES * LANES, tokens - (W + LANES))
    return blocks, first, pl.multiple_of(base, LANES)


def split(queries, fresh_key):
    heads = [queries[:, g * HD : (g + 1) * HD] for g in range(G)]
    return heads, [jnp.sum(h * fresh_key, axis=1, keepdims=True) * HD ** (-0.5) for h in heads]


def attend(heads, own, fresh_value, starts, lengths, long_start, tokens, near_ref):
    blocks, first, base = places(long_start, tokens)
    others, span = len(blocks) * LANES, W + LANES
    is_long = lengths == LMAX
    long_query = jnp.zeros((8, HD), F32)
    long_own = jnp.zeros((8, 1), F32)
    for g in range(G):
        picked = jnp.sum(jnp.where(is_long, heads[g], 0.0), axis=0, keepdims=True)
        long_query = jnp.where(iota((8, HD), 0) == g, picked, long_query)
        picked_own = jnp.sum(jnp.where(is_long, own[g], 0.0), axis=0, keepdims=True)
        long_own = jnp.where(iota((8, 1), 0) == g, picked_own, long_own)
    long_value = jnp.sum(jnp.where(is_long, fresh_value, 0.0), axis=0, keepdims=True)
    position = base + iota((8, span), 1)
    long_out = weigh(
        long_query,
        near_ref[:HD, others:],
        near_ref[HD : 2 * HD, others:],
        (position >= first) & (position < first + (W - 1)),
        long_own,
        long_value,
    )
    position = jnp.concatenate(
        [jnp.where(spare, -LANES, begin) + iota((1, LANES), 1) for begin, spare in blocks], axis=1
    )
    ends = starts + lengths
    firsts = jnp.maximum(starts, ends - (W - 1))
    ends = jnp.concatenate([ends] * G, axis=0)
    firsts = jnp.concatenate([firsts] * G, axis=0)
    outs = weigh(
        jnp.concatenate(heads, axis=0),
        near_ref[:HD, :others],
        near_ref[HD : 2 * HD, :others],
        (position >= firsts) & (position < ends),
        jnp.concatenate(own, axis=0),
        jnp.concatenate([fresh_value] * G, axis=0),
    )
    count = starts.shape[0]
    return jnp.concatenate(
        [jnp.where(is_long, long_out[g : g + 1], outs[g * count : (g + 1) * count]) for g in range(G)],
        axis=1,
    )


def load_kernel(
    offsets_hbm, lengths_hbm, queries_hbm, fresh_hbm, cache_hbm, weight_hbm,
    near_ref, weight_ref, home_ref, chosen_ref, chosen_t_ref, placed_t_ref,
    offsets_ref, lengths_ref, queries_ref, fresh_ref, sems, weight_sems, near_sems,
):
    sources = (offsets_hbm, lengths_hbm, queries_hbm, fresh_hbm)
    copies = fetch(sources, (offsets_ref, lengths_ref, queries_ref, fresh_ref), sems)
    weight_rows = pl.ds(0, weight_ref.shape[0])
    (weight_copy,) = fetch((weight_hbm.at[weight_rows],), (weight_ref,), weight_sems)
    for copy in copies[:2]:
        copy.wait()
    index = lax.axis_index("req")
    tokens = cache_hbm.shape[1]
    rows = chosen_ref.shape[0]
    offsets = offsets_ref[...]
    held = owner_of(offsets, tokens) == index
    long_start = jnp.sum(jnp.where(held & (lengths_ref[...] == LMAX), offsets, 0)) - index * tokens
    blocks, _, base = places(long_start, tokens)
    sources = [cache_hbm.at[:, pl.ds(begin, LANES)] for begin, _ in blocks]
    targets = [near_ref.at[:, pl.ds(i * LANES, LANES)] for i in range(len(blocks))]
    sources.append(cache_hbm.at[:, pl.ds(base, W + LANES)])
    targets.append(near_ref.at[:, pl.ds(len(blocks) * LANES, W + LANES)])
    near_copies = fetch(sources, targets, near_sems)
    flags = jnp.where(held & ((iota((8, LANES), 1) & 15) >= HALF), 1.0, 0.0).astype(BF)
    line = source_of(iota((rows, 8), 0) >> 2) >> 3
    here = dot(jnp.where(line == iota((rows, 8), 1), 1.0, 0.0).astype(BF), flags)
    earlier = dot(jnp.where(line > iota((rows, 8), 1), 1.0, 0.0).astype(BF), flags)
    row = iota((rows, LANES), 0)
    col = iota((rows, LANES), 1)
    slot = source_of(row >> 2) & 7
    valid = jnp.sum(jnp.where((col >> 4) == slot, here, 0.0), axis=1, keepdims=True)
    rank = jnp.sum(earlier + jnp.where((col >> 4) < slot, here, 0.0), axis=1, keepdims=True)
    hit = (valid > 0.5) & (rank.astype(I32) == (col & 7)) & ((row & 3) == (col >> 3))
    chosen = jnp.where(hit, 1.0, 0.0)
    chosen_ref[...] = chosen.astype(BF)
    chosen_t_ref[...] = jnp.transpose(chosen)[:32].astype(BF)
    offsets = own_row(offsets_ref, index, 0)
    starts = column(offsets, 16)
    lengths = column(own_row(lengths_ref, index, 0), 16)
    far = slot_of(owner_of(starts[8:], tokens))
    far = jnp.concatenate([far] * 4, axis=0)
    row = iota((32, rows), 0)
    col = iota((32, rows), 1)
    placed_t_ref[...] = jnp.where(((col >> 2) == far) & ((col & 3) == (row >> 3)), 1.0, 0.0).astype(BF)
    for copy in copies[2:]:
        copy.wait()
    fresh = fresh_ref[...].astype(F32)[:8]
    heads, own = split(queries_ref[...].astype(F32)[:8], fresh[:, :HD])
    lane = iota((HALF, LANES), 1)
    wide = lambda x: jnp.concatenate([x, jnp.zeros((HALF, LANES - HD), F32)], axis=1)
    for g in range(G):
        home_ref[g * HALF : (g + 1) * HALF] = jnp.where(lane == HD, own[g], wide(heads[g]))
    last = wide(fresh[:, HD:])
    numbers = (starts[:8] - index * tokens, lengths[:8], jnp.full((8, 1), long_start, I32))
    for i, number in enumerate(numbers):
        last = jnp.where(lane == HD + i, number.astype(F32), last)
    home_ref[G * HALF :] = last
    for copy in near_copies:
        copy.wait()
    weight_copy.wait()


def attend_kernel(
    tokens, got_ref, chosen_t_ref, home_ref, near_ref, weight_ref,
    weight_hbm, out_ref, rest_ref, sems,
):
    upper, rest = weight_ref.shape[0], rest_ref.shape[0]
    (copy,) = fetch((weight_hbm.at[pl.ds(upper, rest)],), (rest_ref,), sems)
    last = home_ref[G * HALF :]
    numbers = last[:, HD : HD + 3].astype(I32)
    long_start = jnp.max(numbers[:, 2:3])
    queries, fresh_key, fresh_value, starts, lengths = unpack(dot(chosen_t_ref[...], got_ref[...]))
    far_heads, far_own = split(queries, fresh_key)
    stack = lambda *pair: jnp.concatenate(pair, axis=0)
    rows = [slice(g * HALF, (g + 1) * HALF) for g in range(G)]
    attended = attend(
        [stack(home_ref[r, :HD], far) for r, far in zip(rows, far_heads)],
        [stack(home_ref[r, HD : HD + 1], far) for r, far in zip(rows, far_own)],
        stack(last[:, :HD], fresh_value),
        stack(numbers[:, 0:1], starts),
        stack(numbers[:, 1:2], lengths),
        long_start, tokens, near_ref,
    ).astype(BF)
    mixed = dot(attended[:, :upper], weight_ref[...])
    copy.wait()
    mixed = mixed + dot(attended[:, upper:], rest_ref[...])
    columns = out_ref.shape[0]
    low = iota((HALF, LANES), 1) < 64
    for j in range(columns):
        left = j * G * HD // LANES * LANES
        tiles = [mixed[:, left + k * LANES : left + (k + 1) * LANES] for k in range(3)]
        if j % 2 == 0:
            half = jnp.where(low, tiles[2][:8], pltpu.roll(tiles[2][8:], 64, 1))
            full = tiles[:2]
        else:
            half = jnp.where(low, pltpu.roll(tiles[0][:8], 64, 1), tiles[0][8:])
            full = tiles[1:]
        out_ref[(j - TP_FIRST) % columns] = jnp.concatenate([*full, half], axis=0).astype(BF)


def spread_kernel(shares_ref, chosen_ref, home_ref, out_ref):
    mixed = jnp.sum(shares_ref[...].astype(F32), axis=0).astype(BF).astype(F32)
    home_ref[...] = mixed
    stack = jnp.concatenate(
        [mixed[8:16], mixed[24:32], mixed[32:40], jnp.zeros((104, LANES), F32)], axis=0
    )
    out_ref[...] = dot(chosen_ref[...], stack.astype(BF)).astype(BF)


def pick_kernel(placed_t_ref, home_ref, returned_ref, out_ref):
    far = dot(placed_t_ref[...], returned_ref[...])
    home = home_ref[...]
    first = jnp.concatenate([home[0:8], far[0:8]], axis=0)
    second = jnp.concatenate([home[16:24], far[8:16]], axis=0)
    half = jnp.concatenate([home[32:40], pltpu.roll(far[16:24], 64, 1)], axis=0)[:, :64]
    odd = (lax.axis_index("tp") % 2) == 1
    even = jnp.concatenate([first, second, half], axis=1)
    out_ref[...] = jnp.where(odd, jnp.concatenate([half, first, second], axis=1), even).astype(BF)


def exchange(x, axis, group):
    return lax.all_to_all(x, axis, 0, 0, axis_index_groups=[group], tiled=True)


def in_vmem(x):
    return pltpu.with_memory_space_constraint(x, pltpu.VMEM)


def in_hbm(x):
    return pltpu.with_memory_space_constraint(x, pltpu.HBM)


def call(kernel, out_shape, *args, far_args=(), scratch=(), result_in_hbm=False):
    outs = out_shape if result_in_hbm else [pltpu.VMEM(s.shape, s.dtype) for s in out_shape]
    return pl.pallas_call(
        kernel,
        out_shape=outs,
        in_specs=[NEAR] * len(args) + [ANYWHERE] * len(far_args),
        out_specs=[NEAR] * len(out_shape),
        scratch_shapes=scratch,
        compiler_params=pltpu.CompilerParams(vmem_limit_bytes=16 << 20),
    )(*(in_vmem(a) for a in args), *(in_hbm(a) for a in far_args))


def shards(queries, fresh_kv, kv_cache, out_weight, offsets, lengths):
    devices = lax.axis_size("req")
    columns = lax.axis_size("tp")
    req_group = [int(i) for i in source_of(np.arange(devices), np.where)]
    row_count, width = queries.shape
    tokens = kv_cache.shape[2]
    cache = kv_cache.reshape(kv_cache.shape[1:])
    offsets = offsets.reshape(-1, LANES)
    lengths = lengths.reshape(-1, LANES)
    shape = jax.ShapeDtypeStruct
    slots = shape((devices * 4, LANES), BF)
    scratch = lambda x: pltpu.VMEM(x.shape, x.dtype)
    semaphores = pltpu.SemaphoreType.DMA
    inputs = (offsets, lengths, queries, fresh_kv)
    (message,) = call(
        functools.partial(send_kernel, tokens),
        [slots],
        far_args=inputs,
        scratch=[*map(scratch, inputs), semaphores((4,))],
    )
    got = exchange(message.reshape(devices, 4, LANES), "req", req_group)
    near_blocks = (tokens - LMAX) // LANES + 1
    upper = out_weight.shape[0] * 4 // 5
    near, weight, home, chosen, chosen_t, placed_t = call(
        load_kernel,
        [
            shape((2 * HD, near_blocks * LANES + W + LANES), BF),
            shape((upper, out_weight.shape[1]), BF),
            shape(((G + 1) * HALF, LANES), F32),
            slots,
            shape((32, devices * 4), BF),
            shape((32, devices * 4), BF),
        ],
        far_args=(*inputs, cache, out_weight),
        scratch=[
            *map(scratch, inputs), semaphores((4,)), semaphores((1,)), semaphores((near_blocks + 1,))
        ],
    )
    (shares,) = call(
        functools.partial(attend_kernel, tokens),
        [shape((columns, 40, LANES), BF)],
        got.reshape(devices * 4, LANES), chosen_t, home, near, weight,
        far_args=(out_weight,),
        scratch=[
            pltpu.VMEM((out_weight.shape[0] - upper, out_weight.shape[1]), BF), semaphores((1,))
        ],
    )
    shares = exchange(shares, "tp", [(TP_FIRST + i) % columns for i in range(columns)])
    home, spread = call(spread_kernel, [shape((40, LANES), F32), slots], shares, chosen)
    returned = exchange(spread.reshape(devices, 4, LANES), "req", req_group)
    (mixed,) = call(
        pick_kernel,
        [shape((row_count, width), BF)],
        placed_t, home, returned.reshape(devices * 4, LANES),
        result_in_hbm=True,
    )
    return mixed


def solution(mesh):
    in_specs = (P("req", "tp"), P("req", "tp"), P("tp", None, "req"), P("tp", None), P(), P())
    out_specs = P("req", "tp")
    return jax.shard_map(shards, mesh=mesh, in_specs=in_specs, out_specs=out_specs, check_vma=False)
```

```python
import functools

import jax
import jax.numpy as jnp
import numpy as np
from jax import lax
from jax.experimental import pallas as pl
from jax.experimental.pallas import tpu as pltpu
from jax.sharding import PartitionSpec as P

HD = 80
G = 4
W = 4096
LMAX = 8192
LANES = 128
HALF = 8
FIRST_Z, FIRST_X, FIRST_CORE = 6, 2, 1
TP_GROUP = (5, 1, 2, 0, 3, 7, 4, 6)
BF = jnp.bfloat16
F32 = jnp.float32
I32 = jnp.int32
NEAR = pl.BlockSpec(memory_space=pltpu.VMEM)
ANYWHERE = pl.BlockSpec(memory_space=pltpu.HBM)


def iota(shape, axis):
    return lax.broadcasted_iota(I32, shape, axis)


def dot(a, b):
    return jnp.dot(a, b, preferred_element_type=F32)


def dot_t(a, b):
    return lax.dot_general(a, b, (((1,), (1,)), ((), ())), preferred_element_type=F32)


def owner_of(offsets, tokens):
    return ((offsets.astype(F32) + 0.5) * (1.0 / tokens)).astype(I32)


def own_row(table_ref, index, shift):
    per_row = LANES // 16
    row = table_ref[pl.ds(index // per_row, 1), :]
    back = (index % per_row) * 16 + shift
    return pltpu.roll(row, (LANES - back) % LANES, 1)


def column(row, count):
    wide = jnp.broadcast_to(row, (count, LANES))
    same = iota((count, LANES), 0) == iota((count, LANES), 1)
    return jnp.sum(jnp.where(same, wide, 0), axis=1, keepdims=True)


def pack(queries, fresh, starts, lengths):
    lane = iota((HALF, LANES), 1)
    meta = jnp.where(lane == 96, 1, 0)
    meta = jnp.where(lane == 97, starts >> 7, meta)
    meta = jnp.where(lane == 98, starts & 127, meta)
    meta = jnp.where(lane == 99, lengths >> 7, meta)
    meta = jnp.where(lane == 100, lengths & 127, meta)
    third = jnp.concatenate([queries[:, 256:], fresh[:, 128:], jnp.zeros((HALF, 32), F32)], axis=1)
    return jnp.concatenate(
        [queries[:, :128], queries[:, 128:256], third + meta.astype(F32), fresh[:, :128]], axis=0
    )


def unpack(stack):
    meta = stack[16:24]
    starts = (meta[:, 97:98] * 128.0 + meta[:, 98:99]).astype(I32)
    lengths = (meta[:, 99:100] * 128.0 + meta[:, 100:101]).astype(I32)
    queries = jnp.concatenate([stack[0:8], stack[8:16], stack[16:24, :64]], axis=1)
    fresh = jnp.concatenate([stack[24:32], stack[16:24, 64:96]], axis=1)
    return queries, fresh[:, :HD], fresh[:, HD:], starts, lengths


def fetch(sources, targets, sems):
    copies = [
        pltpu.make_async_copy(s, t, sems.at[i]) for i, (s, t) in enumerate(zip(sources, targets))
    ]
    for copy in copies:
        copy.start()
    return copies


def source_of(slot, where=jnp.where):
    place = (slot + 63) & 63
    ring_z, ring_x = place >> 3, (place >> 1) & 3
    z = FIRST_Z + 4 + where((ring_z & 1) == 1, -((ring_z + 1) >> 1), ring_z >> 1)
    x = FIRST_X + 2 + where((ring_x & 1) == 1, -((ring_x + 1) >> 1), ring_x >> 1)
    return (z & 7) * 8 + (x & 3) * 2 + ((FIRST_CORE + 1 + place) & 1)


def slot_of(member):
    z = (((member >> 3) - FIRST_Z) & 7) - 4
    x = ((((member >> 1) & 3) - FIRST_X) & 3) - 2
    ring_z = jnp.where(z < 0, -2 * z - 1, 2 * z)
    ring_x = jnp.where(x < 0, -2 * x - 1, 2 * x)
    core = (member + FIRST_CORE + 1) & 1
    return (ring_z * 8 + ring_x * 2 + core + 1) & 63


def send_kernel(
    tokens, offsets_hbm, lengths_hbm, queries_hbm, fresh_hbm, out_ref,
    offsets_ref, lengths_ref, queries_ref, fresh_ref, sems,
):
    sources = (offsets_hbm, lengths_hbm, queries_hbm, fresh_hbm)
    for copy in fetch(sources, (offsets_ref, lengths_ref, queries_ref, fresh_ref), sems):
        copy.wait()
    index = lax.axis_index("req")
    rows = out_ref.shape[0]
    offsets = own_row(offsets_ref, index, HALF)
    owners = owner_of(offsets, tokens)
    starts = column(offsets - owners * tokens, HALF)
    far = slot_of(owners)
    lane = iota((1, LANES), 1)
    spread = jnp.where(lane < 8, far, 0)
    for k in (1, 2, 3):
        here = (lane >= 8 * k) & (lane < 8 * k + 8)
        spread = spread + jnp.where(here, pltpu.roll(far, 8 * k, 1), 0)
    row = iota((rows, LANES), 0)
    col = iota((rows, LANES), 1)
    hit = ((row >> 2) == jnp.broadcast_to(spread, (rows, LANES))) & ((row & 3) == (col >> 3))
    placed = jnp.where(hit, 1.0, 0.0).astype(BF)
    lengths = column(own_row(lengths_ref, index, HALF), HALF)
    queries = queries_ref[...].astype(F32)
    fresh = fresh_ref[...].astype(F32)
    stack = pack(queries[8:], fresh[8:], starts, lengths)
    stack = jnp.concatenate([stack, jnp.zeros((96, LANES), F32)], axis=0)
    out_ref[...] = dot(placed, stack.astype(BF)).astype(BF)


def weigh(queries, keys, values, inside, own, own_value):
    scores = jnp.where(inside, dot(queries.astype(BF), keys) * HD ** (-0.5), -jnp.inf)
    highest = jnp.maximum(jnp.max(scores, axis=1, keepdims=True), own)
    weights = jnp.exp(scores - highest)
    own_weight = jnp.exp(own - highest)
    totals = jnp.sum(weights, axis=1, keepdims=True) + own_weight
    summed = dot_t(weights.astype(BF), values) + own_weight.astype(BF).astype(F32) * own_value
    return summed / totals


def places(long_start, tokens):
    before = (long_start + LANES - 1) // LANES
    after = (long_start + LMAX) // LANES
    last = tokens // LANES - 1
    blocks = []
    for i in range((tokens - LMAX) // LANES + 1):
        block = jnp.where(i < before, i, after + i - before)
        blocks.append((pl.multiple_of(jnp.minimum(block, last) * LANES, LANES), block > last))
    first = long_start + (LMAX - W + 1)
    base = jnp.minimum(first // LANES * LANES, tokens - (W + LANES))
    return blocks, first, pl.multiple_of(base, LANES)


def split(queries, fresh_key):
    heads = [queries[:, g * HD : (g + 1) * HD] for g in range(G)]
    return heads, [jnp.sum(h * fresh_key, axis=1, keepdims=True) * HD ** (-0.5) for h in heads]


def attend(heads, own, fresh_value, starts, lengths, long_start, tokens, near_ref):
    blocks, first, base = places(long_start, tokens)
    others, span = len(blocks) * LANES, W + LANES
    is_long = lengths == LMAX
    long_query = jnp.zeros((8, HD), F32)
    long_own = jnp.zeros((8, 1), F32)
    for g in range(G):
        picked = jnp.sum(jnp.where(is_long, heads[g], 0.0), axis=0, keepdims=True)
        long_query = jnp.where(iota((8, HD), 0) == g, picked, long_query)
        picked_own = jnp.sum(jnp.where(is_long, own[g], 0.0), axis=0, keepdims=True)
        long_own = jnp.where(iota((8, 1), 0) == g, picked_own, long_own)
    long_value = jnp.sum(jnp.where(is_long, fresh_value, 0.0), axis=0, keepdims=True)
    position = base + iota((8, span), 1)
    long_out = weigh(
        long_query,
        near_ref[:HD, others:],
        near_ref[HD : 2 * HD, others:],
        (position >= first) & (position < first + (W - 1)),
        long_own,
        long_value,
    )
    position = jnp.concatenate(
        [jnp.where(spare, -LANES, begin) + iota((1, LANES), 1) for begin, spare in blocks], axis=1
    )
    ends = starts + lengths
    firsts = jnp.maximum(starts, ends - (W - 1))
    ends = jnp.concatenate([ends] * G, axis=0)
    firsts = jnp.concatenate([firsts] * G, axis=0)
    outs = weigh(
        jnp.concatenate(heads, axis=0),
        near_ref[:HD, :others],
        near_ref[HD : 2 * HD, :others],
        (position >= firsts) & (position < ends),
        jnp.concatenate(own, axis=0),
        jnp.concatenate([fresh_value] * G, axis=0),
    )
    count = starts.shape[0]
    return jnp.concatenate(
        [jnp.where(is_long, long_out[g : g + 1], outs[g * count : (g + 1) * count]) for g in range(G)],
        axis=1,
    )


def load_kernel(
    offsets_hbm, lengths_hbm, queries_hbm, fresh_hbm, cache_hbm, weight_hbm,
    near_ref, weight_ref, home_ref, chosen_ref, chosen_t_ref, placed_t_ref,
    offsets_ref, lengths_ref, queries_ref, fresh_ref, sems, weight_sems, near_sems,
):
    sources = (offsets_hbm, lengths_hbm, queries_hbm, fresh_hbm)
    copies = fetch(sources, (offsets_ref, lengths_ref, queries_ref, fresh_ref), sems)
    weight_rows = pl.ds(0, weight_ref.shape[0])
    (weight_copy,) = fetch((weight_hbm.at[weight_rows],), (weight_ref,), weight_sems)
    for copy in copies[:2]:
        copy.wait()
    index = lax.axis_index("req")
    tokens = cache_hbm.shape[1]
    rows = chosen_ref.shape[0]
    offsets = offsets_ref[...]
    held = owner_of(offsets, tokens) == index
    long_start = jnp.sum(jnp.where(held & (lengths_ref[...] == LMAX), offsets, 0)) - index * tokens
    blocks, _, base = places(long_start, tokens)
    sources = [cache_hbm.at[:, pl.ds(begin, LANES)] for begin, _ in blocks]
    targets = [near_ref.at[:, pl.ds(i * LANES, LANES)] for i in range(len(blocks))]
    sources.append(cache_hbm.at[:, pl.ds(base, W + LANES)])
    targets.append(near_ref.at[:, pl.ds(len(blocks) * LANES, W + LANES)])
    near_copies = fetch(sources, targets, near_sems)
    flags = jnp.where(held & ((iota((8, LANES), 1) & 15) >= HALF), 1.0, 0.0).astype(BF)
    line = source_of(iota((rows, 8), 0) >> 2) >> 3
    here = dot(jnp.where(line == iota((rows, 8), 1), 1.0, 0.0).astype(BF), flags)
    earlier = dot(jnp.where(line > iota((rows, 8), 1), 1.0, 0.0).astype(BF), flags)
    row = iota((rows, LANES), 0)
    col = iota((rows, LANES), 1)
    slot = source_of(row >> 2) & 7
    valid = jnp.sum(jnp.where((col >> 4) == slot, here, 0.0), axis=1, keepdims=True)
    rank = jnp.sum(earlier + jnp.where((col >> 4) < slot, here, 0.0), axis=1, keepdims=True)
    hit = (valid > 0.5) & (rank.astype(I32) == (col & 7)) & ((row & 3) == (col >> 3))
    chosen = jnp.where(hit, 1.0, 0.0)
    chosen_ref[...] = chosen.astype(BF)
    chosen_t_ref[...] = jnp.transpose(chosen)[:32].astype(BF)
    offsets = own_row(offsets_ref, index, 0)
    starts = column(offsets, 16)
    lengths = column(own_row(lengths_ref, index, 0), 16)
    far = slot_of(owner_of(starts[8:], tokens))
    far = jnp.concatenate([far] * 4, axis=0)
    row = iota((32, rows), 0)
    col = iota((32, rows), 1)
    placed_t_ref[...] = jnp.where(((col >> 2) == far) & ((col & 3) == (row >> 3)), 1.0, 0.0).astype(BF)
    for copy in copies[2:]:
        copy.wait()
    fresh = fresh_ref[...].astype(F32)[:8]
    heads, own = split(queries_ref[...].astype(F32)[:8], fresh[:, :HD])
    lane = iota((HALF, LANES), 1)
    wide = lambda x: jnp.concatenate([x, jnp.zeros((HALF, LANES - HD), F32)], axis=1)
    for g in range(G):
        home_ref[g * HALF : (g + 1) * HALF] = jnp.where(lane == HD, own[g], wide(heads[g]))
    last = wide(fresh[:, HD:])
    numbers = (starts[:8] - index * tokens, lengths[:8], jnp.full((8, 1), long_start, I32))
    for i, number in enumerate(numbers):
        last = jnp.where(lane == HD + i, number.astype(F32), last)
    home_ref[G * HALF :] = last
    for copy in near_copies:
        copy.wait()
    weight_copy.wait()


def attend_kernel(
    tokens, got_ref, chosen_t_ref, home_ref, near_ref, weight_ref,
    weight_hbm, out_ref, rest_ref, sems,
):
    upper, rest = weight_ref.shape[0], rest_ref.shape[0]
    (copy,) = fetch((weight_hbm.at[pl.ds(upper, rest)],), (rest_ref,), sems)
    last = home_ref[G * HALF :]
    numbers = last[:, HD : HD + 3].astype(I32)
    long_start = jnp.max(numbers[:, 2:3])
    queries, fresh_key, fresh_value, starts, lengths = unpack(dot(chosen_t_ref[...], got_ref[...]))
    far_heads, far_own = split(queries, fresh_key)
    stack = lambda *pair: jnp.concatenate(pair, axis=0)
    rows = [slice(g * HALF, (g + 1) * HALF) for g in range(G)]
    attended = attend(
        [stack(home_ref[r, :HD], far) for r, far in zip(rows, far_heads)],
        [stack(home_ref[r, HD : HD + 1], far) for r, far in zip(rows, far_own)],
        stack(last[:, :HD], fresh_value),
        stack(numbers[:, 0:1], starts),
        stack(numbers[:, 1:2], lengths),
        long_start, tokens, near_ref,
    ).astype(BF)
    mixed = dot(attended[:, :upper], weight_ref[...])
    copy.wait()
    mixed = mixed + dot(attended[:, upper:], rest_ref[...])
    columns = out_ref.shape[0]
    low = iota((HALF, LANES), 1) < 64
    for j in range(columns):
        left = j * G * HD // LANES * LANES
        tiles = [mixed[:, left + k * LANES : left + (k + 1) * LANES] for k in range(3)]
        if j % 2 == 0:
            half = jnp.where(low, tiles[2][:8], pltpu.roll(tiles[2][8:], 64, 1))
            full = tiles[:2]
        else:
            half = jnp.where(low, pltpu.roll(tiles[0][:8], 64, 1), tiles[0][8:])
            full = tiles[1:]
        out_ref[TP_GROUP.index(j)] = jnp.concatenate([*full, half], axis=0).astype(BF)


def spread_kernel(shares_ref, chosen_ref, home_ref, out_ref):
    mixed = jnp.sum(shares_ref[...].astype(F32), axis=0).astype(BF).astype(F32)
    home_ref[...] = mixed
    stack = jnp.concatenate(
        [mixed[8:16], mixed[24:32], mixed[32:40], jnp.zeros((104, LANES), F32)], axis=0
    )
    out_ref[...] = dot(chosen_ref[...], stack.astype(BF)).astype(BF)


def pick_kernel(placed_t_ref, home_ref, returned_ref, out_ref):
    far = dot(placed_t_ref[...], returned_ref[...])
    home = home_ref[...]
    first = jnp.concatenate([home[0:8], far[0:8]], axis=0)
    second = jnp.concatenate([home[16:24], far[8:16]], axis=0)
    half = jnp.concatenate([home[32:40], pltpu.roll(far[16:24], 64, 1)], axis=0)[:, :64]
    odd = (lax.axis_index("tp") % 2) == 1
    even = jnp.concatenate([first, second, half], axis=1)
    out_ref[...] = jnp.where(odd, jnp.concatenate([half, first, second], axis=1), even).astype(BF)


def exchange(x, axis, group):
    return lax.all_to_all(x, axis, 0, 0, axis_index_groups=[group], tiled=True)


def in_vmem(x):
    return pltpu.with_memory_space_constraint(x, pltpu.VMEM)


def in_hbm(x):
    return pltpu.with_memory_space_constraint(x, pltpu.HBM)


def call(kernel, out_shape, *args, far_args=(), scratch=(), result_in_hbm=False):
    outs = out_shape if result_in_hbm else [pltpu.VMEM(s.shape, s.dtype) for s in out_shape]
    return pl.pallas_call(
        kernel,
        out_shape=outs,
        in_specs=[NEAR] * len(args) + [ANYWHERE] * len(far_args),
        out_specs=[NEAR] * len(out_shape),
        scratch_shapes=scratch,
        compiler_params=pltpu.CompilerParams(vmem_limit_bytes=16 << 20),
    )(*(in_vmem(a) for a in args), *(in_hbm(a) for a in far_args))


def shards(queries, fresh_kv, kv_cache, out_weight, offsets, lengths):
    devices = lax.axis_size("req")
    columns = lax.axis_size("tp")
    req_group = [int(i) for i in source_of(np.arange(devices), np.where)]
    row_count, width = queries.shape
    tokens = kv_cache.shape[2]
    cache = kv_cache.reshape(kv_cache.shape[1:])
    offsets = offsets.reshape(-1, LANES)
    lengths = lengths.reshape(-1, LANES)
    shape = jax.ShapeDtypeStruct
    slots = shape((devices * 4, LANES), BF)
    scratch = lambda x: pltpu.VMEM(x.shape, x.dtype)
    semaphores = pltpu.SemaphoreType.DMA
    inputs = (offsets, lengths, queries, fresh_kv)
    (message,) = call(
        functools.partial(send_kernel, tokens),
        [slots],
        far_args=inputs,
        scratch=[*map(scratch, inputs), semaphores((4,))],
    )
    got = exchange(message.reshape(devices, 4, LANES), "req", req_group)
    near_blocks = (tokens - LMAX) // LANES + 1
    upper = out_weight.shape[0] * 4 // 5
    near, weight, home, chosen, chosen_t, placed_t = call(
        load_kernel,
        [
            shape((2 * HD, near_blocks * LANES + W + LANES), BF),
            shape((upper, out_weight.shape[1]), BF),
            shape(((G + 1) * HALF, LANES), F32),
            slots,
            shape((32, devices * 4), BF),
            shape((32, devices * 4), BF),
        ],
        far_args=(*inputs, cache, out_weight),
        scratch=[
            *map(scratch, inputs), semaphores((4,)), semaphores((1,)), semaphores((near_blocks + 1,))
        ],
    )
    (shares,) = call(
        functools.partial(attend_kernel, tokens),
        [shape((columns, 40, LANES), BF)],
        got.reshape(devices * 4, LANES), chosen_t, home, near, weight,
        far_args=(out_weight,),
        scratch=[
            pltpu.VMEM((out_weight.shape[0] - upper, out_weight.shape[1]), BF), semaphores((1,))
        ],
    )
    shares = exchange(shares, "tp", list(TP_GROUP))
    home, spread = call(spread_kernel, [shape((40, LANES), F32), slots], shares, chosen)
    returned = exchange(spread.reshape(devices, 4, LANES), "req", req_group)
    (mixed,) = call(
        pick_kernel,
        [shape((row_count, width), BF)],
        placed_t, home, returned.reshape(devices * 4, LANES),
        result_in_hbm=True,
    )
    return mixed


def solution(mesh):
    in_specs = (P("req", "tp"), P("req", "tp"), P("tp", None, "req"), P("tp", None), P(), P())
    out_specs = P("req", "tp")
    return jax.shard_map(shards, mesh=mesh, in_specs=in_specs, out_specs=out_specs, check_vma=False)
```

```python
import functools

import jax
import jax.numpy as jnp
import numpy as np
from jax import lax
from jax.experimental import pallas as pl
from jax.experimental.pallas import tpu as pltpu
from jax.sharding import PartitionSpec as P

HD = 80
G = 4
W = 4096
LMAX = 8192
LANES = 128
HALF = 8
FIRST_Z, FIRST_X, FIRST_CORE = 6, 2, 1
TP_FIRST = 4
BF = jnp.bfloat16
F32 = jnp.float32
I32 = jnp.int32
NEAR = pl.BlockSpec(memory_space=pltpu.VMEM)
ANYWHERE = pl.BlockSpec(memory_space=pltpu.HBM)


def iota(shape, axis):
    return lax.broadcasted_iota(I32, shape, axis)


def dot(a, b):
    return jnp.dot(a, b, preferred_element_type=F32)


def dot_t(a, b):
    return lax.dot_general(a, b, (((1,), (1,)), ((), ())), preferred_element_type=F32)


def owner_of(offsets, tokens):
    return ((offsets.astype(F32) + 0.5) * (1.0 / tokens)).astype(I32)


def own_row(table_ref, index, shift):
    per_row = LANES // 16
    row = table_ref[pl.ds(index // per_row, 1), :]
    back = (index % per_row) * 16 + shift
    return pltpu.roll(row, (LANES - back) % LANES, 1)


def column(row, count):
    wide = jnp.broadcast_to(row, (count, LANES))
    same = iota((count, LANES), 0) == iota((count, LANES), 1)
    return jnp.sum(jnp.where(same, wide, 0), axis=1, keepdims=True)


def pack(queries, fresh, starts, lengths):
    lane = iota((HALF, LANES), 1)
    meta = jnp.where(lane == 96, 1, 0)
    meta = jnp.where(lane == 97, starts >> 7, meta)
    meta = jnp.where(lane == 98, starts & 127, meta)
    meta = jnp.where(lane == 99, lengths >> 7, meta)
    meta = jnp.where(lane == 100, lengths & 127, meta)
    third = jnp.concatenate([queries[:, 256:], fresh[:, 128:], jnp.zeros((HALF, 32), F32)], axis=1)
    return jnp.concatenate(
        [queries[:, :128], queries[:, 128:256], third + meta.astype(F32), fresh[:, :128]], axis=0
    )


def unpack(stack):
    meta = stack[16:24]
    starts = (meta[:, 97:98] * 128.0 + meta[:, 98:99]).astype(I32)
    lengths = (meta[:, 99:100] * 128.0 + meta[:, 100:101]).astype(I32)
    queries = jnp.concatenate([stack[0:8], stack[8:16], stack[16:24, :64]], axis=1)
    fresh = jnp.concatenate([stack[24:32], stack[16:24, 64:96]], axis=1)
    return queries, fresh[:, :HD], fresh[:, HD:], starts, lengths


def fetch(sources, targets, sems):
    copies = [
        pltpu.make_async_copy(s, t, sems.at[i]) for i, (s, t) in enumerate(zip(sources, targets))
    ]
    for copy in copies:
        copy.start()
    return copies


def source_of(slot, where=jnp.where):
    place = (slot + 63) & 63
    ring_z, ring_x = place >> 3, (place >> 1) & 3
    z = FIRST_Z + 4 + where((ring_z & 1) == 1, -((ring_z + 1) >> 1), ring_z >> 1)
    x = FIRST_X + 2 + where((ring_x & 1) == 1, -((ring_x + 1) >> 1), ring_x >> 1)
    return (z & 7) * 8 + (x & 3) * 2 + ((FIRST_CORE + 1 + place) & 1)


def slot_of(member):
    z = (((member >> 3) - FIRST_Z) & 7) - 4
    x = ((((member >> 1) & 3) - FIRST_X) & 3) - 2
    ring_z = jnp.where(z < 0, -2 * z - 1, 2 * z)
    ring_x = jnp.where(x < 0, -2 * x - 1, 2 * x)
    core = (member + FIRST_CORE + 1) & 1
    return (ring_z * 8 + ring_x * 2 + core + 1) & 63


def send_kernel(
    tokens, offsets_hbm, lengths_hbm, queries_hbm, fresh_hbm, out_hbm,
    offsets_ref, lengths_ref, queries_ref, fresh_ref, out_ref, sems, out_sems,
):
    sources = (offsets_hbm, lengths_hbm, queries_hbm, fresh_hbm)
    for copy in fetch(sources, (offsets_ref, lengths_ref, queries_ref, fresh_ref), sems):
        copy.wait()
    index = lax.axis_index("req")
    rows = out_ref.shape[0]
    offsets = own_row(offsets_ref, index, HALF)
    owners = owner_of(offsets, tokens)
    starts = column(offsets - owners * tokens, HALF)
    far = slot_of(owners)
    lane = iota((1, LANES), 1)
    spread = jnp.where(lane < 8, far, 0)
    for k in (1, 2, 3):
        here = (lane >= 8 * k) & (lane < 8 * k + 8)
        spread = spread + jnp.where(here, pltpu.roll(far, 8 * k, 1), 0)
    row = iota((rows, LANES), 0)
    col = iota((rows, LANES), 1)
    hit = ((row >> 2) == jnp.broadcast_to(spread, (rows, LANES))) & ((row & 3) == (col >> 3))
    placed = jnp.where(hit, 1.0, 0.0).astype(BF)
    lengths = column(own_row(lengths_ref, index, HALF), HALF)
    queries = queries_ref[...].astype(F32)
    fresh = fresh_ref[...].astype(F32)
    stack = pack(queries[8:], fresh[8:], starts, lengths)
    stack = jnp.concatenate([stack, jnp.zeros((96, LANES), F32)], axis=0)
    stack = stack.astype(BF)
    copies = []
    for i in range(2):
        part = pl.ds(i * rows // 2, rows // 2)
        out_ref[part] = dot(placed[i * rows // 2 : (i + 1) * rows // 2], stack).astype(BF)
        copies.append(pltpu.make_async_copy(out_ref.at[part], out_hbm.at[part], out_sems.at[i]))
        copies[i].start()
    for copy in copies:
        copy.wait()


def weigh(queries, keys, values, inside, own, own_value):
    scores = jnp.where(inside, dot(queries.astype(BF), keys) * HD ** (-0.5), -jnp.inf)
    highest = jnp.maximum(jnp.max(scores, axis=1, keepdims=True), own)
    weights = jnp.exp(scores - highest)
    own_weight = jnp.exp(own - highest)
    totals = jnp.sum(weights, axis=1, keepdims=True) + own_weight
    summed = dot_t(weights.astype(BF), values) + own_weight.astype(BF).astype(F32) * own_value
    return summed / totals


def places(long_start, tokens):
    before = (long_start + LANES - 1) // LANES
    after = (long_start + LMAX) // LANES
    last = tokens // LANES - 1
    blocks = []
    for i in range((tokens - LMAX) // LANES + 1):
        block = jnp.where(i < before, i, after + i - before)
        blocks.append((pl.multiple_of(jnp.minimum(block, last) * LANES, LANES), block > last))
    first = long_start + (LMAX - W + 1)
    base = jnp.minimum(first // LANES * LANES, tokens - (W + LANES))
    return blocks, first, pl.multiple_of(base, LANES)


def split(queries, fresh_key):
    heads = [queries[:, g * HD : (g + 1) * HD] for g in range(G)]
    return heads, [jnp.sum(h * fresh_key, axis=1, keepdims=True) * HD ** (-0.5) for h in heads]


def attend(heads, own, fresh_value, starts, lengths, long_start, tokens, near_ref):
    blocks, first, base = places(long_start, tokens)
    others, span = len(blocks) * LANES, W + LANES
    is_long = lengths == LMAX
    long_query = jnp.zeros((8, HD), F32)
    long_own = jnp.zeros((8, 1), F32)
    for g in range(G):
        picked = jnp.sum(jnp.where(is_long, heads[g], 0.0), axis=0, keepdims=True)
        long_query = jnp.where(iota((8, HD), 0) == g, picked, long_query)
        picked_own = jnp.sum(jnp.where(is_long, own[g], 0.0), axis=0, keepdims=True)
        long_own = jnp.where(iota((8, 1), 0) == g, picked_own, long_own)
    long_value = jnp.sum(jnp.where(is_long, fresh_value, 0.0), axis=0, keepdims=True)
    position = base + iota((8, span), 1)
    long_out = weigh(
        long_query,
        near_ref[:HD, others:],
        near_ref[HD : 2 * HD, others:],
        (position >= first) & (position < first + (W - 1)),
        long_own,
        long_value,
    )
    position = jnp.concatenate(
        [jnp.where(spare, -LANES, begin) + iota((1, LANES), 1) for begin, spare in blocks], axis=1
    )
    ends = starts + lengths
    firsts = jnp.maximum(starts, ends - (W - 1))
    ends = jnp.concatenate([ends] * G, axis=0)
    firsts = jnp.concatenate([firsts] * G, axis=0)
    outs = weigh(
        jnp.concatenate(heads, axis=0),
        near_ref[:HD, :others],
        near_ref[HD : 2 * HD, :others],
        (position >= firsts) & (position < ends),
        jnp.concatenate(own, axis=0),
        jnp.concatenate([fresh_value] * G, axis=0),
    )
    count = starts.shape[0]
    return jnp.concatenate(
        [jnp.where(is_long, long_out[g : g + 1], outs[g * count : (g + 1) * count]) for g in range(G)],
        axis=1,
    )


def load_kernel(
    offsets_hbm, lengths_hbm, queries_hbm, fresh_hbm, cache_hbm, weight_hbm,
    near_ref, weight_ref, home_ref, chosen_ref, chosen_t_ref, placed_t_ref,
    offsets_ref, lengths_ref, queries_ref, fresh_ref, sems, weight_sems, near_sems,
):
    sources = (offsets_hbm, lengths_hbm, queries_hbm, fresh_hbm)
    copies = fetch(sources, (offsets_ref, lengths_ref, queries_ref, fresh_ref), sems)
    weight_rows = pl.ds(0, weight_ref.shape[0])
    (weight_copy,) = fetch((weight_hbm.at[weight_rows],), (weight_ref,), weight_sems)
    for copy in copies[:2]:
        copy.wait()
    index = lax.axis_index("req")
    tokens = cache_hbm.shape[1]
    rows = chosen_ref.shape[0]
    offsets = offsets_ref[...]
    held = owner_of(offsets, tokens) == index
    long_start = jnp.sum(jnp.where(held & (lengths_ref[...] == LMAX), offsets, 0)) - index * tokens
    blocks, _, base = places(long_start, tokens)
    sources = [cache_hbm.at[:, pl.ds(begin, LANES)] for begin, _ in blocks]
    targets = [near_ref.at[:, pl.ds(i * LANES, LANES)] for i in range(len(blocks))]
    sources.append(cache_hbm.at[:, pl.ds(base, W + LANES)])
    targets.append(near_ref.at[:, pl.ds(len(blocks) * LANES, W + LANES)])
    near_copies = fetch(sources, targets, near_sems)
    flags = jnp.where(held & ((iota((8, LANES), 1) & 15) >= HALF), 1.0, 0.0).astype(BF)
    line = source_of(iota((rows, 8), 0) >> 2) >> 3
    here = dot(jnp.where(line == iota((rows, 8), 1), 1.0, 0.0).astype(BF), flags)
    earlier = dot(jnp.where(line > iota((rows, 8), 1), 1.0, 0.0).astype(BF), flags)
    row = iota((rows, LANES), 0)
    col = iota((rows, LANES), 1)
    slot = source_of(row >> 2) & 7
    valid = jnp.sum(jnp.where((col >> 4) == slot, here, 0.0), axis=1, keepdims=True)
    rank = jnp.sum(earlier + jnp.where((col >> 4) < slot, here, 0.0), axis=1, keepdims=True)
    hit = (valid > 0.5) & (rank.astype(I32) == (col & 7)) & ((row & 3) == (col >> 3))
    chosen = jnp.where(hit, 1.0, 0.0)
    chosen_ref[...] = chosen.astype(BF)
    chosen_t_ref[...] = jnp.transpose(chosen)[:32].astype(BF)
    offsets = own_row(offsets_ref, index, 0)
    starts = column(offsets, 16)
    lengths = column(own_row(lengths_ref, index, 0), 16)
    far = slot_of(owner_of(starts[8:], tokens))
    far = jnp.concatenate([far] * 4, axis=0)
    row = iota((32, rows), 0)
    col = iota((32, rows), 1)
    placed_t_ref[...] = jnp.where(((col >> 2) == far) & ((col & 3) == (row >> 3)), 1.0, 0.0).astype(BF)
    for copy in copies[2:]:
        copy.wait()
    fresh = fresh_ref[...].astype(F32)[:8]
    heads, own = split(queries_ref[...].astype(F32)[:8], fresh[:, :HD])
    lane = iota((HALF, LANES), 1)
    wide = lambda x: jnp.concatenate([x, jnp.zeros((HALF, LANES - HD), F32)], axis=1)
    for g in range(G):
        home_ref[g * HALF : (g + 1) * HALF] = jnp.where(lane == HD, own[g], wide(heads[g]))
    last = wide(fresh[:, HD:])
    numbers = (starts[:8] - index * tokens, lengths[:8], jnp.full((8, 1), long_start, I32))
    for i, number in enumerate(numbers):
        last = jnp.where(lane == HD + i, number.astype(F32), last)
    home_ref[G * HALF :] = last
    for copy in near_copies:
        copy.wait()
    weight_copy.wait()


def attend_kernel(
    tokens, got_ref, chosen_t_ref, home_ref, near_ref, weight_ref,
    weight_hbm, out_ref, rest_ref, sems,
):
    upper, rest = weight_ref.shape[0], rest_ref.shape[0]
    (copy,) = fetch((weight_hbm.at[pl.ds(upper, rest)],), (rest_ref,), sems)
    last = home_ref[G * HALF :]
    numbers = last[:, HD : HD + 3].astype(I32)
    long_start = jnp.max(numbers[:, 2:3])
    queries, fresh_key, fresh_value, starts, lengths = unpack(dot(chosen_t_ref[...], got_ref[...]))
    far_heads, far_own = split(queries, fresh_key)
    stack = lambda *pair: jnp.concatenate(pair, axis=0)
    rows = [slice(g * HALF, (g + 1) * HALF) for g in range(G)]
    attended = attend(
        [stack(home_ref[r, :HD], far) for r, far in zip(rows, far_heads)],
        [stack(home_ref[r, HD : HD + 1], far) for r, far in zip(rows, far_own)],
        stack(last[:, :HD], fresh_value),
        stack(numbers[:, 0:1], starts),
        stack(numbers[:, 1:2], lengths),
        long_start, tokens, near_ref,
    ).astype(BF)
    mixed = dot(attended[:, :upper], weight_ref[...])
    copy.wait()
    mixed = mixed + dot(attended[:, upper:], rest_ref[...])
    columns = out_ref.shape[0]
    low = iota((HALF, LANES), 1) < 64
    for j in range(columns):
        left = j * G * HD // LANES * LANES
        tiles = [mixed[:, left + k * LANES : left + (k + 1) * LANES] for k in range(3)]
        if j % 2 == 0:
            half = jnp.where(low, tiles[2][:8], pltpu.roll(tiles[2][8:], 64, 1))
            full = tiles[:2]
        else:
            half = jnp.where(low, pltpu.roll(tiles[0][:8], 64, 1), tiles[0][8:])
            full = tiles[1:]
        out_ref[(j - TP_FIRST) % columns] = jnp.concatenate([*full, half], axis=0).astype(BF)


def spread_kernel(shares_ref, chosen_ref, home_ref, out_ref):
    mixed = jnp.sum(shares_ref[...].astype(F32), axis=0).astype(BF).astype(F32)
    home_ref[...] = mixed
    stack = jnp.concatenate(
        [mixed[8:16], mixed[24:32], mixed[32:40], jnp.zeros((104, LANES), F32)], axis=0
    )
    out_ref[...] = dot(chosen_ref[...], stack.astype(BF)).astype(BF)


def pick_kernel(placed_t_ref, home_ref, returned_ref, out_ref):
    far = dot(placed_t_ref[...], returned_ref[...])
    home = home_ref[...]
    first = jnp.concatenate([home[0:8], far[0:8]], axis=0)
    second = jnp.concatenate([home[16:24], far[8:16]], axis=0)
    half = jnp.concatenate([home[32:40], pltpu.roll(far[16:24], 64, 1)], axis=0)[:, :64]
    odd = (lax.axis_index("tp") % 2) == 1
    even = jnp.concatenate([first, second, half], axis=1)
    out_ref[...] = jnp.where(odd, jnp.concatenate([half, first, second], axis=1), even).astype(BF)


def exchange(x, axis, group):
    return lax.all_to_all(x, axis, 0, 0, axis_index_groups=[group], tiled=True)


def in_vmem(x):
    return pltpu.with_memory_space_constraint(x, pltpu.VMEM)


def in_hbm(x):
    return pltpu.with_memory_space_constraint(x, pltpu.HBM)


def call(kernel, out_shape, *args, far_args=(), scratch=(), result_in_hbm=False):
    outs = out_shape if result_in_hbm else [pltpu.VMEM(s.shape, s.dtype) for s in out_shape]
    return pl.pallas_call(
        kernel,
        out_shape=outs,
        in_specs=[NEAR] * len(args) + [ANYWHERE] * len(far_args),
        out_specs=[NEAR] * len(out_shape),
        scratch_shapes=scratch,
        compiler_params=pltpu.CompilerParams(vmem_limit_bytes=16 << 20),
    )(*(in_vmem(a) for a in args), *(in_hbm(a) for a in far_args))


def shards(queries, fresh_kv, kv_cache, out_weight, offsets, lengths):
    devices = lax.axis_size("req")
    columns = lax.axis_size("tp")
    req_group = [int(i) for i in source_of(np.arange(devices), np.where)]
    row_count, width = queries.shape
    tokens = kv_cache.shape[2]
    cache = kv_cache.reshape(kv_cache.shape[1:])
    offsets = offsets.reshape(-1, LANES)
    lengths = lengths.reshape(-1, LANES)
    shape = jax.ShapeDtypeStruct
    slots = shape((devices * 4, LANES), BF)
    scratch = lambda x: pltpu.VMEM(x.shape, x.dtype)
    semaphores = pltpu.SemaphoreType.DMA
    inputs = (offsets, lengths, queries, fresh_kv)
    (message,) = pl.pallas_call(
        functools.partial(send_kernel, tokens),
        out_shape=[slots],
        in_specs=[ANYWHERE] * 4,
        out_specs=[pl.BlockSpec(memory_space=pltpu.HBM)],
        scratch_shapes=[*map(scratch, inputs), scratch(slots), semaphores((4,)), semaphores((2,))],
        compiler_params=pltpu.CompilerParams(vmem_limit_bytes=16 << 20),
    )(*(in_hbm(a) for a in inputs))
    got = exchange(message.reshape(devices, 4, LANES), "req", req_group)
    near_blocks = (tokens - LMAX) // LANES + 1
    upper = out_weight.shape[0] * 4 // 5
    near, weight, home, chosen, chosen_t, placed_t = call(
        load_kernel,
        [
            shape((2 * HD, near_blocks * LANES + W + LANES), BF),
            shape((upper, out_weight.shape[1]), BF),
            shape(((G + 1) * HALF, LANES), F32),
            slots,
            shape((32, devices * 4), BF),
            shape((32, devices * 4), BF),
        ],
        far_args=(*inputs, cache, out_weight),
        scratch=[
            *map(scratch, inputs), semaphores((4,)), semaphores((1,)), semaphores((near_blocks + 1,))
        ],
    )
    (shares,) = call(
        functools.partial(attend_kernel, tokens),
        [shape((columns, 40, LANES), BF)],
        got.reshape(devices * 4, LANES), chosen_t, home, near, weight,
        far_args=(out_weight,),
        scratch=[
            pltpu.VMEM((out_weight.shape[0] - upper, out_weight.shape[1]), BF), semaphores((1,))
        ],
    )
    shares = exchange(shares, "tp", [(TP_FIRST + i) % columns for i in range(columns)])
    home, spread = call(spread_kernel, [shape((40, LANES), F32), slots], shares, chosen)
    returned = exchange(spread.reshape(devices, 4, LANES), "req", req_group)
    (mixed,) = call(
        pick_kernel,
        [shape((row_count, width), BF)],
        placed_t, home, returned.reshape(devices * 4, LANES),
        result_in_hbm=True,
    )
    return mixed


def solution(mesh):
    in_specs = (P("req", "tp"), P("req", "tp"), P("tp", None, "req"), P("tp", None), P(), P())
    out_specs = P("req", "tp")
    return jax.shard_map(shards, mesh=mesh, in_specs=in_specs, out_specs=out_specs, check_vma=False)
```

```python
import functools

import jax
import jax.numpy as jnp
import numpy as np
from jax import lax
from jax.experimental import pallas as pl
from jax.experimental.pallas import tpu as pltpu
from jax.sharding import PartitionSpec as P

HD = 80
G = 4
W = 4096
LMAX = 8192
LANES = 128
HALF = 8
FIRST_Z, FIRST_X, FIRST_CORE = 6, 2, 1
TP_FIRST = 5
BF = jnp.bfloat16
F32 = jnp.float32
I32 = jnp.int32
NEAR = pl.BlockSpec(memory_space=pltpu.VMEM)
ANYWHERE = pl.BlockSpec(memory_space=pltpu.HBM)


def iota(shape, axis):
    return lax.broadcasted_iota(I32, shape, axis)


def dot(a, b):
    return jnp.dot(a, b, preferred_element_type=F32)


def dot_t(a, b):
    return lax.dot_general(a, b, (((1,), (1,)), ((), ())), preferred_element_type=F32)


def owner_of(offsets, tokens):
    return ((offsets.astype(F32) + 0.5) * (1.0 / tokens)).astype(I32)


def own_row(table_ref, index, shift):
    per_row = LANES // 16
    row = table_ref[pl.ds(index // per_row, 1), :]
    back = (index % per_row) * 16 + shift
    return pltpu.roll(row, (LANES - back) % LANES, 1)


def column(row, count):
    wide = jnp.broadcast_to(row, (count, LANES))
    same = iota((count, LANES), 0) == iota((count, LANES), 1)
    return jnp.sum(jnp.where(same, wide, 0), axis=1, keepdims=True)


def pack(queries, fresh, starts, lengths):
    lane = iota((HALF, LANES), 1)
    meta = jnp.where(lane == 96, 1, 0)
    meta = jnp.where(lane == 97, starts >> 7, meta)
    meta = jnp.where(lane == 98, starts & 127, meta)
    meta = jnp.where(lane == 99, lengths >> 7, meta)
    meta = jnp.where(lane == 100, lengths & 127, meta)
    third = jnp.concatenate([queries[:, 256:], fresh[:, 128:], jnp.zeros((HALF, 32), F32)], axis=1)
    return jnp.concatenate(
        [queries[:, :128], queries[:, 128:256], third + meta.astype(F32), fresh[:, :128]], axis=0
    )


def unpack(stack):
    meta = stack[16:24]
    starts = (meta[:, 97:98] * 128.0 + meta[:, 98:99]).astype(I32)
    lengths = (meta[:, 99:100] * 128.0 + meta[:, 100:101]).astype(I32)
    queries = jnp.concatenate([stack[0:8], stack[8:16], stack[16:24, :64]], axis=1)
    fresh = jnp.concatenate([stack[24:32], stack[16:24, 64:96]], axis=1)
    return queries, fresh[:, :HD], fresh[:, HD:], starts, lengths


def fetch(sources, targets, sems):
    copies = [
        pltpu.make_async_copy(s, t, sems.at[i]) for i, (s, t) in enumerate(zip(sources, targets))
    ]
    for copy in copies:
        copy.start()
    return copies


def source_of(slot, where=jnp.where):
    place = (slot + 63) & 63
    ring_z, ring_x = place >> 3, (place >> 1) & 3
    z = FIRST_Z + 4 + where((ring_z & 1) == 1, -((ring_z + 1) >> 1), ring_z >> 1)
    x = FIRST_X + 2 + where((ring_x & 1) == 1, -((ring_x + 1) >> 1), ring_x >> 1)
    return (z & 7) * 8 + (x & 3) * 2 + ((FIRST_CORE + 1 + place) & 1)


def slot_of(member):
    z = (((member >> 3) - FIRST_Z) & 7) - 4
    x = ((((member >> 1) & 3) - FIRST_X) & 3) - 2
    ring_z = jnp.where(z < 0, -2 * z - 1, 2 * z)
    ring_x = jnp.where(x < 0, -2 * x - 1, 2 * x)
    core = (member + FIRST_CORE + 1) & 1
    return (ring_z * 8 + ring_x * 2 + core + 1) & 63


def send_kernel(
    tokens, offsets_hbm, lengths_hbm, queries_hbm, fresh_hbm, out_hbm,
    offsets_ref, lengths_ref, queries_ref, fresh_ref, out_ref, sems, out_sems,
):
    sources = (offsets_hbm, lengths_hbm, queries_hbm, fresh_hbm)
    for copy in fetch(sources, (offsets_ref, lengths_ref, queries_ref, fresh_ref), sems):
        copy.wait()
    index = lax.axis_index("req")
    rows = out_ref.shape[0]
    offsets = own_row(offsets_ref, index, HALF)
    owners = owner_of(offsets, tokens)
    starts = column(offsets - owners * tokens, HALF)
    far = slot_of(owners)
    lane = iota((1, LANES), 1)
    spread = jnp.where(lane < 8, far, 0)
    for k in (1, 2, 3):
        here = (lane >= 8 * k) & (lane < 8 * k + 8)
        spread = spread + jnp.where(here, pltpu.roll(far, 8 * k, 1), 0)
    row = iota((rows, LANES), 0)
    col = iota((rows, LANES), 1)
    hit = ((row >> 2) == jnp.broadcast_to(spread, (rows, LANES))) & ((row & 3) == (col >> 3))
    placed = jnp.where(hit, 1.0, 0.0).astype(BF)
    lengths = column(own_row(lengths_ref, index, HALF), HALF)
    queries = queries_ref[...].astype(F32)
    fresh = fresh_ref[...].astype(F32)
    stack = pack(queries[8:], fresh[8:], starts, lengths)
    stack = jnp.concatenate([stack, jnp.zeros((96, LANES), F32)], axis=0)
    stack = stack.astype(BF)
    copies = []
    for i in range(2):
        part = pl.ds(i * rows // 2, rows // 2)
        out_ref[part] = dot(placed[i * rows // 2 : (i + 1) * rows // 2], stack).astype(BF)
        copies.append(pltpu.make_async_copy(out_ref.at[part], out_hbm.at[part], out_sems.at[i]))
        copies[i].start()
    for copy in copies:
        copy.wait()


def weigh(queries, keys, values, inside, own, own_value):
    scores = jnp.where(inside, dot(queries.astype(BF), keys) * HD ** (-0.5), -jnp.inf)
    highest = jnp.maximum(jnp.max(scores, axis=1, keepdims=True), own)
    weights = jnp.exp(scores - highest)
    own_weight = jnp.exp(own - highest)
    totals = jnp.sum(weights, axis=1, keepdims=True) + own_weight
    summed = dot_t(weights.astype(BF), values) + own_weight.astype(BF).astype(F32) * own_value
    return summed / totals


def places(long_start, tokens):
    before = (long_start + LANES - 1) // LANES
    after = (long_start + LMAX) // LANES
    last = tokens // LANES - 1
    blocks = []
    for i in range((tokens - LMAX) // LANES + 1):
        block = jnp.where(i < before, i, after + i - before)
        blocks.append((pl.multiple_of(jnp.minimum(block, last) * LANES, LANES), block > last))
    first = long_start + (LMAX - W + 1)
    base = jnp.minimum(first // LANES * LANES, tokens - (W + LANES))
    return blocks, first, pl.multiple_of(base, LANES)


def split(queries, fresh_key):
    heads = [queries[:, g * HD : (g + 1) * HD] for g in range(G)]
    return heads, [jnp.sum(h * fresh_key, axis=1, keepdims=True) * HD ** (-0.5) for h in heads]


def attend(heads, own, fresh_value, starts, lengths, long_start, tokens, near_ref):
    blocks, first, base = places(long_start, tokens)
    others, span = len(blocks) * LANES, W + LANES
    is_long = lengths == LMAX
    long_query = jnp.zeros((8, HD), F32)
    long_own = jnp.zeros((8, 1), F32)
    for g in range(G):
        picked = jnp.sum(jnp.where(is_long, heads[g], 0.0), axis=0, keepdims=True)
        long_query = jnp.where(iota((8, HD), 0) == g, picked, long_query)
        picked_own = jnp.sum(jnp.where(is_long, own[g], 0.0), axis=0, keepdims=True)
        long_own = jnp.where(iota((8, 1), 0) == g, picked_own, long_own)
    long_value = jnp.sum(jnp.where(is_long, fresh_value, 0.0), axis=0, keepdims=True)
    position = base + iota((8, span), 1)
    long_out = weigh(
        long_query,
        near_ref[:HD, others:],
        near_ref[HD : 2 * HD, others:],
        (position >= first) & (position < first + (W - 1)),
        long_own,
        long_value,
    )
    position = jnp.concatenate(
        [jnp.where(spare, -LANES, begin) + iota((1, LANES), 1) for begin, spare in blocks], axis=1
    )
    ends = starts + lengths
    firsts = jnp.maximum(starts, ends - (W - 1))
    ends = jnp.concatenate([ends] * G, axis=0)
    firsts = jnp.concatenate([firsts] * G, axis=0)
    outs = weigh(
        jnp.concatenate(heads, axis=0),
        near_ref[:HD, :others],
        near_ref[HD : 2 * HD, :others],
        (position >= firsts) & (position < ends),
        jnp.concatenate(own, axis=0),
        jnp.concatenate([fresh_value] * G, axis=0),
    )
    count = starts.shape[0]
    return jnp.concatenate(
        [jnp.where(is_long, long_out[g : g + 1], outs[g * count : (g + 1) * count]) for g in range(G)],
        axis=1,
    )


def load_kernel(
    offsets_hbm, lengths_hbm, queries_hbm, fresh_hbm, cache_hbm, weight_hbm,
    near_ref, weight_ref, home_ref, chosen_ref, chosen_t_ref, placed_t_ref,
    offsets_ref, lengths_ref, queries_ref, fresh_ref, sems, weight_sems, near_sems,
):
    sources = (offsets_hbm, lengths_hbm, queries_hbm, fresh_hbm)
    copies = fetch(sources, (offsets_ref, lengths_ref, queries_ref, fresh_ref), sems)
    weight_rows = pl.ds(0, weight_ref.shape[0])
    (weight_copy,) = fetch((weight_hbm.at[weight_rows],), (weight_ref,), weight_sems)
    for copy in copies[:2]:
        copy.wait()
    index = lax.axis_index("req")
    tokens = cache_hbm.shape[1]
    rows = chosen_ref.shape[0]
    offsets = offsets_ref[...]
    held = owner_of(offsets, tokens) == index
    long_start = jnp.sum(jnp.where(held & (lengths_ref[...] == LMAX), offsets, 0)) - index * tokens
    blocks, _, base = places(long_start, tokens)
    sources = [cache_hbm.at[:, pl.ds(begin, LANES)] for begin, _ in blocks]
    targets = [near_ref.at[:, pl.ds(i * LANES, LANES)] for i in range(len(blocks))]
    sources.append(cache_hbm.at[:, pl.ds(base, W + LANES)])
    targets.append(near_ref.at[:, pl.ds(len(blocks) * LANES, W + LANES)])
    near_copies = fetch(sources, targets, near_sems)
    flags = jnp.where(held & ((iota((8, LANES), 1) & 15) >= HALF), 1.0, 0.0).astype(BF)
    line = source_of(iota((rows, 8), 0) >> 2) >> 3
    here = dot(jnp.where(line == iota((rows, 8), 1), 1.0, 0.0).astype(BF), flags)
    earlier = dot(jnp.where(line > iota((rows, 8), 1), 1.0, 0.0).astype(BF), flags)
    row = iota((rows, LANES), 0)
    col = iota((rows, LANES), 1)
    slot = source_of(row >> 2) & 7
    valid = jnp.sum(jnp.where((col >> 4) == slot, here, 0.0), axis=1, keepdims=True)
    rank = jnp.sum(earlier + jnp.where((col >> 4) < slot, here, 0.0), axis=1, keepdims=True)
    hit = (valid > 0.5) & (rank.astype(I32) == (col & 7)) & ((row & 3) == (col >> 3))
    chosen = jnp.where(hit, 1.0, 0.0)
    chosen_ref[...] = chosen.astype(BF)
    chosen_t_ref[...] = jnp.transpose(chosen)[:32].astype(BF)
    offsets = own_row(offsets_ref, index, 0)
    starts = column(offsets, 16)
    lengths = column(own_row(lengths_ref, index, 0), 16)
    far = slot_of(owner_of(starts[8:], tokens))
    far = jnp.concatenate([far] * 4, axis=0)
    row = iota((32, rows), 0)
    col = iota((32, rows), 1)
    placed_t_ref[...] = jnp.where(((col >> 2) == far) & ((col & 3) == (row >> 3)), 1.0, 0.0).astype(BF)
    for copy in copies[2:]:
        copy.wait()
    fresh = fresh_ref[...].astype(F32)[:8]
    heads, own = split(queries_ref[...].astype(F32)[:8], fresh[:, :HD])
    lane = iota((HALF, LANES), 1)
    wide = lambda x: jnp.concatenate([x, jnp.zeros((HALF, LANES - HD), F32)], axis=1)
    for g in range(G):
        home_ref[g * HALF : (g + 1) * HALF] = jnp.where(lane == HD, own[g], wide(heads[g]))
    last = wide(fresh[:, HD:])
    numbers = (starts[:8] - index * tokens, lengths[:8], jnp.full((8, 1), long_start, I32))
    for i, number in enumerate(numbers):
        last = jnp.where(lane == HD + i, number.astype(F32), last)
    home_ref[G * HALF :] = last
    for copy in near_copies:
        copy.wait()
    weight_copy.wait()


def attend_kernel(
    tokens, got_ref, chosen_t_ref, home_ref, near_ref, weight_ref,
    weight_hbm, out_ref, rest_ref, sems,
):
    upper, rest = weight_ref.shape[0], rest_ref.shape[0]
    (copy,) = fetch((weight_hbm.at[pl.ds(upper, rest)],), (rest_ref,), sems)
    last = home_ref[G * HALF :]
    numbers = last[:, HD : HD + 3].astype(I32)
    long_start = jnp.max(numbers[:, 2:3])
    queries, fresh_key, fresh_value, starts, lengths = unpack(dot(chosen_t_ref[...], got_ref[...]))
    far_heads, far_own = split(queries, fresh_key)
    stack = lambda *pair: jnp.concatenate(pair, axis=0)
    rows = [slice(g * HALF, (g + 1) * HALF) for g in range(G)]
    attended = attend(
        [stack(home_ref[r, :HD], far) for r, far in zip(rows, far_heads)],
        [stack(home_ref[r, HD : HD + 1], far) for r, far in zip(rows, far_own)],
        stack(last[:, :HD], fresh_value),
        stack(numbers[:, 0:1], starts),
        stack(numbers[:, 1:2], lengths),
        long_start, tokens, near_ref,
    ).astype(BF)
    mixed = dot(attended[:, :upper], weight_ref[...])
    copy.wait()
    mixed = mixed + dot(attended[:, upper:], rest_ref[...])
    columns = out_ref.shape[0]
    low = iota((HALF, LANES), 1) < 64
    for j in range(columns):
        left = j * G * HD // LANES * LANES
        tiles = [mixed[:, left + k * LANES : left + (k + 1) * LANES] for k in range(3)]
        if j % 2 == 0:
            half = jnp.where(low, tiles[2][:8], pltpu.roll(tiles[2][8:], 64, 1))
            full = tiles[:2]
        else:
            half = jnp.where(low, pltpu.roll(tiles[0][:8], 64, 1), tiles[0][8:])
            full = tiles[1:]
        out_ref[(j - TP_FIRST) % columns] = jnp.concatenate([*full, half], axis=0).astype(BF)


def spread_kernel(shares_ref, chosen_ref, home_ref, out_ref):
    mixed = jnp.sum(shares_ref[...].astype(F32), axis=0).astype(BF).astype(F32)
    home_ref[...] = mixed
    stack = jnp.concatenate(
        [mixed[8:16], mixed[24:32], mixed[32:40], jnp.zeros((104, LANES), F32)], axis=0
    )
    out_ref[...] = dot(chosen_ref[...], stack.astype(BF)).astype(BF)


def pick_kernel(placed_t_ref, home_ref, returned_ref, out_ref):
    far = dot(placed_t_ref[...], returned_ref[...])
    home = home_ref[...]
    first = jnp.concatenate([home[0:8], far[0:8]], axis=0)
    second = jnp.concatenate([home[16:24], far[8:16]], axis=0)
    half = jnp.concatenate([home[32:40], pltpu.roll(far[16:24], 64, 1)], axis=0)[:, :64]
    odd = (lax.axis_index("tp") % 2) == 1
    even = jnp.concatenate([first, second, half], axis=1)
    out_ref[...] = jnp.where(odd, jnp.concatenate([half, first, second], axis=1), even).astype(BF)


def exchange(x, axis, group):
    return lax.all_to_all(x, axis, 0, 0, axis_index_groups=[group], tiled=True)


def in_vmem(x):
    return pltpu.with_memory_space_constraint(x, pltpu.VMEM)


def in_hbm(x):
    return pltpu.with_memory_space_constraint(x, pltpu.HBM)


def call(kernel, out_shape, *args, far_args=(), scratch=(), result_in_hbm=False):
    outs = out_shape if result_in_hbm else [pltpu.VMEM(s.shape, s.dtype) for s in out_shape]
    return pl.pallas_call(
        kernel,
        out_shape=outs,
        in_specs=[NEAR] * len(args) + [ANYWHERE] * len(far_args),
        out_specs=[NEAR] * len(out_shape),
        scratch_shapes=scratch,
        compiler_params=pltpu.CompilerParams(vmem_limit_bytes=16 << 20),
    )(*(in_vmem(a) for a in args), *(in_hbm(a) for a in far_args))


def shards(queries, fresh_kv, kv_cache, out_weight, offsets, lengths):
    devices = lax.axis_size("req")
    columns = lax.axis_size("tp")
    req_group = [int(i) for i in source_of(np.arange(devices), np.where)]
    row_count, width = queries.shape
    tokens = kv_cache.shape[2]
    cache = kv_cache.reshape(kv_cache.shape[1:])
    offsets = offsets.reshape(-1, LANES)
    lengths = lengths.reshape(-1, LANES)
    shape = jax.ShapeDtypeStruct
    slots = shape((devices * 4, LANES), BF)
    scratch = lambda x: pltpu.VMEM(x.shape, x.dtype)
    semaphores = pltpu.SemaphoreType.DMA
    inputs = (offsets, lengths, queries, fresh_kv)
    (message,) = pl.pallas_call(
        functools.partial(send_kernel, tokens),
        out_shape=[slots],
        in_specs=[ANYWHERE] * 4,
        out_specs=[pl.BlockSpec(memory_space=pltpu.HBM)],
        scratch_shapes=[*map(scratch, inputs), scratch(slots), semaphores((4,)), semaphores((2,))],
        compiler_params=pltpu.CompilerParams(vmem_limit_bytes=16 << 20),
    )(*(in_hbm(a) for a in inputs))
    got = exchange(message.reshape(devices, 4, LANES), "req", req_group)
    near_blocks = (tokens - LMAX) // LANES + 1
    upper = out_weight.shape[0] * 4 // 5
    near, weight, home, chosen, chosen_t, placed_t = call(
        load_kernel,
        [
            shape((2 * HD, near_blocks * LANES + W + LANES), BF),
            shape((upper, out_weight.shape[1]), BF),
            shape(((G + 1) * HALF, LANES), F32),
            slots,
            shape((32, devices * 4), BF),
            shape((32, devices * 4), BF),
        ],
        far_args=(*inputs, cache, out_weight),
        scratch=[
            *map(scratch, inputs), semaphores((4,)), semaphores((1,)), semaphores((near_blocks + 1,))
        ],
    )
    (shares,) = call(
        functools.partial(attend_kernel, tokens),
        [shape((columns, 40, LANES), BF)],
        got.reshape(devices * 4, LANES), chosen_t, home, near, weight,
        far_args=(out_weight,),
        scratch=[
            pltpu.VMEM((out_weight.shape[0] - upper, out_weight.shape[1]), BF), semaphores((1,))
        ],
    )
    shares = exchange(shares, "tp", [(TP_FIRST + i) % columns for i in range(columns)])
    home, spread = call(spread_kernel, [shape((40, LANES), F32), slots], shares, chosen)
    returned = exchange(spread.reshape(devices, 4, LANES), "req", req_group)
    (mixed,) = call(
        pick_kernel,
        [shape((row_count, width), BF)],
        placed_t, home, returned.reshape(devices * 4, LANES),
        result_in_hbm=True,
    )
    return mixed


def solution(mesh):
    in_specs = (P("req", "tp"), P("req", "tp"), P("tp", None, "req"), P("tp", None), P(), P())
    out_specs = P("req", "tp")
    return jax.shard_map(shards, mesh=mesh, in_specs=in_specs, out_specs=out_specs, check_vma=False)
```
